128 devices in a mesh: ctx: 16 (over y_hi, x, core), wa: 8 (over y_lo, z).
Axes of the slice: x: 4, y: 4 (y_hi: 2, y_lo: 2; y = y_hi * 2 + y_lo), z: 4, core: 2. Of those that a mesh axis runs over, the one named last changes fastest.
Arguments:
- layer_input: bfloat16 [2048, 1024], P('ctx'), may hold values from -6 to 6
- block_order: int32 [32], replicated, may hold values from 0 to 31, each once
- seg_ids: int32 [2048], replicated, may hold values from 0 to 2, never falling along the last dimension, each value on 1 to 1024 neighbouring positions
- cotangent: bfloat16 [2048, 1024], P('ctx'), may hold values from -6 to 6
- ln1_gain: bfloat16 [1024], replicated, may hold values from 0.5 to 1.5
- ln1_bias: bfloat16 [1024], replicated, may hold values from -1.75 to 1.75
- w_qkv: bfloat16 [1024, 3, 1024], P(None, None, 'wa'), may hold values from -0.1875 to 0.1875
- b_qv: bfloat16 [2, 1024], P(None, 'wa'), may hold values from -1.75 to 1.75
- w_out: bfloat16 [1024, 1024], P('wa'), may hold values from -1.5 to 1.5
- b_out: bfloat16 [1024], replicated, may hold values from -1.75 to 1.75
- ln2_gain: bfloat16 [1024], replicated, may hold values from 0.5 to 1.5
- ln2_bias: bfloat16 [1024], replicated, may hold values from -1.75 to 1.75
- w_up: bfloat16 [1024, 4096], P(None, 'wa'), may hold values from -0.1875 to 0.1875
- b_up: bfloat16 [4096], P('wa'), may hold values from -1.75 to 1.75
- w_down: bfloat16 [4096, 1024], P('wa'), may hold values from -0.09375 to 0.09375
- b_down: bfloat16 [1024], replicated, may hold values from -1.75 to 1.75
Outputs:
- layer_output: bfloat16 [2048, 1024], P('ctx')
- grad_input: float32 [2048, 1024], P('ctx')
- grad_ln1_gain: float32 [1024], replicated
- grad_ln1_bias: float32 [1024], replicated
- grad_w_qkv: float32 [1024, 3, 1024], P(None, None, 'wa')
- grad_b_qv: float32 [2, 1024], P(None, 'wa')
- grad_w_out: float32 [1024, 1024], P('wa')
- grad_b_out: float32 [1024], replicated
- grad_ln2_gain: float32 [1024], replicated
- grad_ln2_bias: float32 [1024], replicated
- grad_w_up: float32 [1024, 4096], P(None, 'wa')
- grad_b_up: float32 [4096], P('wa')
- grad_w_down: float32 [4096, 1024], P('wa')
- grad_b_down: float32 [1024], replicated
The draws below stay inside these ranges and needn't reach their ends.
Inputs may be any that keep to these rules, and one draw needn't show every extreme that they name: Each of the 32 stream blocks appears once; row block b of layer_input holds stream block block_order[b]. `seg_ids`: non-decreasing along the stream; each of the 3 sequences has 1 to 1024 positions, one exactly 1024.
All inputs are finite; a program needn't handle non-finite values.
Results may differ from the reference program's by a relative error of at most 0.02.
Values may be sent and summed in bfloat16 or wider, within the bound.
A program may use at most 64 MiB of HBM per device.

```python
import math
import jax
import jax.numpy as jnp
import numpy as np
from jax import lax

D = 1024
H = 16
HD = 64
FF = 4096
NSEQ = 3
HHD = 1024
NBLK = 32
TOKENS = 2048


def steps_of(key, extent, shards, smallest, top_value):
    level, own = 1.0, jax.random.fold_in(key, 6)
    for axis_at, shards_of in shards:
        steps = jnp.exp(jax.random.uniform(jax.random.fold_in(own, axis_at), (shards_of,), jnp.float32, smallest / len(shards), top_value / len(shards)))
        level = level * jnp.repeat(steps, extent[axis_at] // shards_of).reshape([-1 if axis == axis_at else 1 for axis in range(len(extent))])
    return level


def length_profile(number_of, total, bound, skew):
    loads = [(1 << 20) // math.isqrt(grade ** skew) + 1 for grade in range(2, number_of + 1)]
    spare, given = total - bound - (number_of - 1), [1] * (number_of - 1)
    while spare > 0:
        free = [i for i in range(number_of - 1) if given[i] < bound]
        mass, remaining = sum([loads[i] for i in free]), spare
        for i in free:
            more = min(bound - given[i], max(1, remaining * loads[i] // mass), spare)
            given[i] = given[i] + more
            spare = spare - more
    return np.array([bound] + given)


def ragged(key, amount, total, most, skew):
    if amount == 2:
        one = jax.random.randint(key, (), max(1, total - most), min(most, total - 1) + 1)
        return jnp.stack([one, total - one])
    lengths = jnp.asarray(length_profile(amount, total, most, skew), jnp.int32)
    twos = (amount - 1) // 2
    giver, sink = lengths[1:1 + 2 * twos:2], lengths[2:2 + 2 * twos:2]
    room = jnp.minimum(giver - 1, most - sink)
    moved = jax.random.randint(jax.random.fold_in(key, 1), (twos,), 0, 1 << 20) % (room + 1)
    lengths = lengths.at[1:1 + 2 * twos:2].set(giver - moved).at[2:2 + 2 * twos:2].set(sink + moved)
    return lengths[jax.random.permutation(jax.random.fold_in(key, 2), amount)]


def bell_draw(stream_key, dims, scale, limit, cuts=(), kind=jnp.bfloat16):
    gain = steps_of(stream_key, dims, cuts, -0.22, 0.18) if cuts else 1.0
    entries = jax.random.normal(stream_key, dims, jnp.float32) * scale * gain
    return jnp.minimum(jnp.maximum(entries, -limit), limit).astype(kind)


def setup_inputs(seed: int = 0) -> dict:
    arg_keys = jax.random.split(jax.random.key(seed), 17)
    layer_input = bell_draw(arg_keys[0], (TOKENS, D), 1.0, 6.0, ((0, 16),))
    block_order = jax.random.permutation(arg_keys[1], NBLK).astype(jnp.int32)
    seg_ids = jnp.searchsorted(jnp.cumsum(ragged(arg_keys[2], NSEQ, TOKENS, TOKENS // 2, 0)), jnp.arange(TOKENS), side="right").astype(jnp.int32)
    cotangent = bell_draw(arg_keys[3], (TOKENS, D), 1.0, 6.0, ((0, 16),))
    ln1_gain = jnp.clip(1.0 + 0.1 * jax.random.normal(arg_keys[4], (D,), jnp.float32), 0.5, 1.5).astype(jnp.bfloat16)
    ln1_bias = bell_draw(arg_keys[5], (D,), 0.3, 1.75)
    w_qkv = bell_draw(arg_keys[6], (D, 3, HHD), D ** -0.5, 0.1875, ((2, 8),))
    b_qv = bell_draw(arg_keys[7], (2, HHD), 0.3, 1.75, ((1, 8),))
    w_out = bell_draw(arg_keys[8], (HHD, D), 16 ** -0.5, 1.5, ((0, 8),))
    b_out = bell_draw(arg_keys[9], (D,), 0.3, 1.75)
    ln2_gain = jnp.clip(1.0 + 0.1 * jax.random.normal(arg_keys[10], (D,), jnp.float32), 0.5, 1.5).astype(jnp.bfloat16)
    ln2_bias = bell_draw(arg_keys[11], (D,), 0.3, 1.75)
    w_up = bell_draw(arg_keys[12], (D, FF), D ** -0.5, 0.1875, ((1, 8),))
    b_up = bell_draw(arg_keys[13], (FF,), 0.3, 1.75, ((0, 8),))
    w_down = bell_draw(arg_keys[14], (FF, D), FF ** -0.5, 0.09375, ((0, 8),))
    b_down = bell_draw(arg_keys[15], (D,), 0.3, 1.75)
    return {"layer_input": layer_input, "block_order": block_order, "seg_ids": seg_ids, "cotangent": cotangent, "ln1_gain": ln1_gain, "ln1_bias": ln1_bias, "w_qkv": w_qkv, "b_qv": b_qv, "w_out": w_out, "b_out": b_out, "ln2_gain": ln2_gain, "ln2_bias": ln2_bias, "w_up": w_up, "b_up": b_up, "w_down": w_down, "b_down": b_down}


@jax.custom_vjp
def low(v):
    return lax.optimization_barrier(v.astype(jnp.bfloat16)).astype(jnp.float32)

@jax.custom_vjp
def low_back(v):
    return v

def low_keep(v):
    return (low(v), None)

def low_pass(kept, grad):
    return (grad,)

def back_keep(v):
    return (v, None)

def back_low(kept, grad):
    return (low(grad),)
low.defvjp(low_keep, low_pass)
low_back.defvjp(back_keep, back_low)

def layer_norm(rows_in, gain_vec, offset):
    row_mean = lax.optimization_barrier(jnp.mean(rows_in, -1, keepdims=True))
    centered = rows_in - row_mean
    variance = lax.optimization_barrier(jnp.mean(centered * centered, -1, keepdims=True))
    return centered * lax.rsqrt(variance + 1e-05) * gain_vec + offset

def attention(queries, keys_all, values_all, key_pos, seg_rows):
    all_rows = queries.shape[0]
    block_rows = math.gcd(512, all_rows)
    block_count = all_rows // block_rows
    key_heads = keys_all.reshape(all_rows, H, HD)
    value_heads = values_all.reshape(all_rows, H, HD)

    def query_block(pieces):
        query_heads, query_pos, query_seg = pieces
        scores = jnp.einsum('qhd,khd->hqk', query_heads, key_heads, precision=lax.Precision.HIGHEST) * HD ** (-0.5)
        scores = low_back(scores)
        allowed = (seg_rows[None, :] == query_seg[:, None]) & (key_pos[None, :] <= query_pos[:, None])
        weights = jax.nn.softmax(jnp.where(allowed[None], scores, -1e+30), axis=-1)
        mixed = jnp.einsum('hqk,khd->qhd', weights, value_heads, precision=lax.Precision.HIGHEST)
        return mixed.reshape(block_rows, H * HD)
    result = lax.map(jax.checkpoint(query_block), (queries.reshape(block_count, block_rows, H, HD), key_pos.reshape(block_count, block_rows), seg_rows.reshape(block_count, block_rows)))
    return result.reshape(all_rows, H * HD)

def reference(layer_input, block_order, seg_ids, cotangent, ln1_gain, ln1_bias, w_qkv, b_qv, w_out, b_out, ln2_gain, ln2_bias, w_up, b_up, w_down, b_down):
    all_rows = layer_input.shape[0]
    block_rows = all_rows // block_order.shape[0]
    row_index = jnp.arange(all_rows, dtype=jnp.int32)
    key_pos = (block_order[row_index // block_rows] * block_rows + row_index % block_rows).astype(jnp.int32)
    seg_rows = seg_ids[key_pos]
    highest = lax.Precision.HIGHEST

    def forward(x_float, gain_one, bias_one, proj_qkv, bias_qv, proj_out, bias_out, gain_two, bias_two, proj_up, bias_up, proj_down, bias_down):
        normed = low(layer_norm(x_float, gain_one, bias_one))
        width = proj_qkv.shape[0]
        projected = jnp.dot(normed, proj_qkv.reshape(width, 3 * H * HD), precision=highest).reshape(all_rows, 3, H * HD)
        queries = low_back(low(projected[:, 0] + bias_qv[0]))
        keys_all = low_back(low(projected[:, 1]))
        values_all = low_back(low(projected[:, 2] + bias_qv[1]))
        mixed = low_back(low(attention(queries, keys_all, values_all, key_pos, seg_rows)))
        hidden_res = x_float + low_back(jnp.dot(mixed, proj_out, precision=highest)) + bias_out
        normed_two = low(layer_norm(hidden_res, gain_two, bias_two))
        up_proj = low_back(jnp.dot(normed_two, proj_up, precision=highest) + bias_up)
        activated = low(jax.nn.gelu(up_proj, approximate=True))
        return hidden_res + low_back(jnp.dot(activated, proj_down, precision=highest)) + bias_down
    floats = [tensor.astype(jnp.float32) for tensor in (layer_input, ln1_gain, ln1_bias, w_qkv, b_qv, w_out, b_out, ln2_gain, ln2_bias, w_up, b_up, w_down, b_down)]
    result, pullback = jax.vjp(forward, *floats)
    gradients = pullback(cotangent.astype(jnp.float32))
    return (result.astype(jnp.bfloat16), gradients[0], gradients[1], gradients[2], gradients[3], gradients[4], gradients[5], gradients[6], gradients[7], gradients[8], gradients[9], gradients[10], gradients[11], gradients[12])
```

```python
import jax
import jax.numpy as jnp
from jax import lax
from jax.experimental import pallas as pl
from jax.experimental.pallas import tpu as pltpu
from jax.sharding import PartitionSpec as P

F32 = jnp.float32
BF = jnp.bfloat16
MESH = pl.DeviceIdType.MESH
GELU_A = 0.7978845608028654
GELU_B = 0.044715

(
    KV,
    KVF,
    RS1,
    AGC,
    RS2,
    RS3,
    AGD,
    AGY,
    CMB,
    RKV,
    RA,
    AGA,
    FWA,
    RB,
    AGB,
    FWB,
    RC,
    AGCC,
    FWC,
    RS4,
    RS5,
    AGG,
    AGV,
    NSEM,
) = range(24)


def nn(a, b):
    return lax.dot_general(a, b, (((1,), (0,)), ((), ())), preferred_element_type=F32)


def nt(a, b):
    return lax.dot_general(a, b, (((1,), (1,)), ((), ())), preferred_element_type=F32)


def tn(a, b):
    return lax.dot_general(a, b, (((0,), (0,)), ((), ())), preferred_element_type=F32)


def normalize(rows):
    centered = rows - jnp.mean(rows, -1, keepdims=True)
    rstd = lax.rsqrt(jnp.mean(centered * centered, -1, keepdims=True) + 1e-05)
    return centered * rstd, rstd


def norm_back(grad, gain, xhat, rstd):
    gx = grad * gain
    return rstd * (
        gx - jnp.mean(gx, -1, keepdims=True) - xhat * jnp.mean(gx * xhat, -1, keepdims=True)
    )


def kernel(
    order_ref,
    seg_ref,
    x_ref,
    g_ref,
    vec_ref,
    wqkv_hbm,
    wout_hbm,
    wup_hbm,
    wdn_hbm,
    y_out,
    gin_out,
    gup_out,
    gdn_out,
    gwo_out,
    gqkv_out,
    vec_out,
    ctx_out,
    wqkv,
    wout,
    wup,
    wdn,
    load_sem,
    xhat_all,
    normed,
    kv,
    q2,
    scores,
    acc,
    attn_t,
    attn_low,
    rs1s,
    rs1r,
    c_all,
    dm,
    rs2s,
    rs2r,
    rs3s,
    rs3r,
    dh_all,
    y_all,
    dkv,
    pkv,
    rkv,
    ga,
    pa,
    ra,
    oa,
    gb,
    pb,
    rb,
    ob,
    gc,
    pc,
    rc,
    oc,
    rs4s,
    rs4r,
    g_all,
    vs,
    vr,
    vall,
    cvs,
    cvr,
    ss,
    rs,
    cs_s,
    cs_r,
):
    ctx = lax.axis_index("ctx")
    wa = lax.axis_index("wa")
    core = lax.rem(ctx, 2)
    chip = lax.div(ctx, 2)
    other = 1 - core
    slot = core * 8 + chip
    partner = chip * 2 + other

    def to_wa(src, dst, kind, d):
        return pltpu.make_async_remote_copy(
            src_ref=src,
            dst_ref=dst,
            send_sem=ss.at[kind, d],
            recv_sem=rs.at[kind, d],
            device_id={"wa": lax.rem(wa + d, 8)},
            device_id_type=MESH,
        )

    def to_chip(src, dst, kind, d):
        return pltpu.make_async_remote_copy(
            src_ref=src,
            dst_ref=dst,
            send_sem=ss.at[kind, d],
            recv_sem=rs.at[kind, d],
            device_id={"ctx": lax.rem(chip + d, 8) * 2 + core},
            device_id_type=MESH,
        )

    def to_partner(src, dst, kind, d):
        return pltpu.make_async_remote_copy(
            src_ref=src,
            dst_ref=dst,
            send_sem=ss.at[kind, d],
            recv_sem=rs.at[kind, d],
            device_id={"ctx": partner},
            device_id_type=MESH,
        )

    def each(low, high, step):
        @pl.loop(low, high)
        def _(d):
            step(d)

    barrier = pltpu.get_barrier_semaphore()
    each(
        1,
        16,
        lambda d: pl.semaphore_signal(
            barrier, inc=1, device_id={"ctx": lax.rem(ctx + d, 16)}, device_id_type=MESH
        ),
    )
    each(
        1,
        8,
        lambda d: pl.semaphore_signal(
            barrier, inc=1, device_id={"wa": lax.rem(wa + d, 8)}, device_id_type=MESH
        ),
    )

    loads = [
        pltpu.make_async_copy(
            wqkv_hbm.at[i], wqkv.at[:, pl.ds(128 * i, 128)], load_sem.at[i]
        )
        for i in range(3)
    ] + [
        pltpu.make_async_copy(wdn_hbm, wdn, load_sem.at[3]),
        pltpu.make_async_copy(wout_hbm, wout, load_sem.at[4]),
        pltpu.make_async_copy(wup_hbm, wup, load_sem.at[5]),
    ]
    for load in loads:
        load.start()

    ln1_gain = vec_ref[0:1, :]
    ln1_bias = vec_ref[1:2, :]
    b_out = vec_ref[2:3, :]
    ln2_gain = vec_ref[3:4, :]
    ln2_bias = vec_ref[4:5, :]
    b_down = vec_ref[5:6, :]
    b_up = vec_ref[6:7, 0:512]
    b_q = vec_ref[7:8, 0:128]
    b_v = vec_ref[7:8, 128:256]

    xhat, _ = normalize(x_ref[...].astype(F32))
    xhat_all[...] = xhat
    normed[...] = (xhat * ln1_gain + ln1_bias).astype(BF)
    for i in range(3):
        loads[i].wait()
    proj = nn(normed[...], wqkv[...])
    kv[slot, :, 0:128] = proj[:, 128:256].astype(BF)
    kv[slot, :, 128:256] = (proj[:, 256:384] + b_v).astype(BF)
    pl.semaphore_wait(barrier, 22)

    to_partner(kv.at[slot], kv.at[slot], KV, 0).start()
    each(1, 8, lambda d: to_chip(kv.at[slot], kv.at[slot], KV, d).start())

    q_low = (proj[:, 0:128] + b_q).astype(BF) * jnp.asarray(0.125, BF)
    lane = lax.broadcasted_iota(jnp.int32, (128, 128), 1)
    zero = jnp.zeros((128, 128), BF)
    q2[0:128, :] = jnp.where(lane < 64, q_low, zero)
    q2[128:256, :] = jnp.where(lane >= 64, q_low, zero)

    lanes = lax.broadcasted_iota(jnp.int32, (1, 256), 1)
    lanes = jnp.where(lanes >= 128, lanes - 128, lanes)
    q_pos = jnp.where(
        lanes < 64, lanes + 64 * order_ref[2 * ctx], lanes - 64 + 64 * order_ref[2 * ctx + 1]
    )
    seg = seg_ref[...]
    one = jnp.ones(seg.shape, F32)
    none = jnp.zeros(seg.shape, F32)

    def count(test):
        part = jnp.sum(jnp.where(test, one, none), axis=0, keepdims=True)
        return jnp.sum(part, axis=1, keepdims=True)

    first_end = count(seg < 1)
    second_end = count(seg < 2)
    q_float = q_pos.astype(F32)
    q_first = jnp.where(
        q_float >= second_end,
        second_end,
        jnp.where(q_float >= first_end, first_end, jnp.zeros_like(q_float)),
    ).astype(jnp.int32)
    row = lax.broadcasted_iota(jnp.int32, (128, 256), 0)

    def score(s, top):
        keys = kv[s, :, 0:128]
        owner = 2 * lax.rem(s, 8) + lax.div(s, 8)
        k_pos = jnp.where(
            row < 64, row + 64 * order_ref[2 * owner], row - 64 + 64 * order_ref[2 * owner + 1]
        )
        allowed = (k_pos <= q_pos) & (k_pos >= q_first)
        masked = jnp.where(allowed, nt(keys, q2[...]), -1e30)
        scores[s] = masked
        return jnp.maximum(top, jnp.max(masked.reshape(16, 8, 256), axis=0))

    loads[3].wait()
    dm[...] = nt(g_ref[...], wdn[...])

    top = score(slot, jnp.full((8, 256), -1e30, F32))
    to_partner(kv.at[slot], kv.at[slot], KV, 0).wait_recv()
    top = score(other * 8 + chip, top)

    def near(d, top):
        s = core * 8 + lax.rem(chip + 8 - d, 8)
        to_chip(kv.at[slot], kv.at[s], KV, d).wait_recv()
        to_partner(kv.at[s], kv.at[s], KVF, d).start()
        return score(s, top)

    top = lax.fori_loop(1, 8, near, top)

    def far(d, top):
        s = other * 8 + lax.rem(chip + 8 - d, 8)
        to_partner(kv.at[s], kv.at[s], KVF, d).wait_recv()
        return score(s, top)

    top = lax.fori_loop(1, 8, far, top)

    top = jnp.max(top, axis=0, keepdims=True)
    acc[...] = jnp.zeros_like(acc)

    def mix(s, total):
        p = jnp.exp(scores[s] - top)
        acc[...] += tn(kv[s, :, 128:256], p.astype(BF))
        return total + jnp.sum(p.reshape(16, 8, 256), axis=0)

    total = lax.fori_loop(0, 16, mix, jnp.zeros((8, 256), F32))
    total = jnp.sum(total, axis=0, keepdims=True)
    lse = top + jnp.log(total)
    half = lax.broadcasted_iota(jnp.int32, (128, 128), 0) < 64

    def diagonal(both):
        return jnp.where(half, both[:, 0:128], both[:, 128:256])

    raw_t = diagonal(acc[...] / total)
    attn_t[...] = raw_t
    attn_low[...] = raw_t.T.astype(BF)

    def reduce_start(part, send, recv, kind):
        send[...] = part.astype(BF).reshape(8, 16, 1024)
        each(1, 8, lambda d: to_wa(send.at[lax.rem(wa + d, 8)], recv.at[d], kind, d).start())

    def reduce_end(send, recv, kind):
        each(1, 8, lambda d: to_wa(send.at[lax.rem(wa + d, 8)], recv.at[d], kind, d).wait_recv())
        whole = send[wa].astype(F32)
        for d in range(1, 8):
            whole = whole + recv[d].astype(F32)
        return whole

    def gather_start(buf, kind):
        each(1, 8, lambda d: to_wa(buf.at[wa], buf.at[wa], kind, d).start())

    def gather_end(buf, kind):
        each(
            1,
            8,
            lambda d: to_wa(buf.at[wa], buf.at[lax.rem(wa + 8 - d, 8)], kind, d).wait_recv(),
        )

    loads[4].wait()
    reduce_start(nn(attn_low[...], wout[...]), rs1s, rs1r, RS1)
    mine = pl.ds(pl.multiple_of(wa * 16, 16), 16)
    x_mine = x_ref[mine, :].astype(F32)
    g_mine = g_ref[mine, :].astype(F32)
    hidden = x_mine + reduce_end(rs1s, rs1r, RS1) + b_out
    hat_two, rstd_two = normalize(hidden)
    c_all[wa] = (hat_two * ln2_gain + ln2_bias).astype(BF)
    gather_start(c_all, AGC)
    loads[5].wait()
    gather_end(c_all, AGC)

    c_low = c_all[...].reshape(128, 1024)
    up = nn(c_low, wup[...]) + b_up
    tanh = jnp.tanh(GELU_A * (up + GELU_B * up * up * up))
    slope = 0.5 * (1.0 + tanh) + 0.5 * up * (1.0 - tanh * tanh) * GELU_A * (
        1.0 + 3.0 * GELU_B * up * up
    )
    du = (dm[...] * slope).astype(BF)
    act = (0.5 * up * (1.0 + tanh)).astype(BF)
    reduce_start(nt(du, wup[...]), rs2s, rs2r, RS2)
    reduce_start(nn(act, wdn[...]), rs3s, rs3r, RS3)
    ga[:, 0:64, :] = tn(c_low, du).astype(BF).reshape(16, 64, 512)
    down = tn(act, g_ref[...]).astype(BF)
    ga[:, 64:96, :] = down[:, 0:512].reshape(16, 32, 512)
    ga[:, 96:128, :] = down[:, 512:1024].reshape(16, 32, 512)

    def combine(buf, kept, index):
        return pltpu.make_async_remote_copy(
            src_ref=buf.at[pl.ds(pl.multiple_of(other * 8, 8), 8)],
            dst_ref=kept,
            send_sem=cs_s.at[index],
            recv_sem=cs_r.at[index],
            device_id={"ctx": partner},
            device_id_type=MESH,
        )

    def combined(buf, kept, index):
        combine(buf, kept, index).wait_recv()

        @pl.loop(0, 8)
        def _(j):
            buf[core * 8 + j] = (buf[core * 8 + j].astype(F32) + kept[j].astype(F32)).astype(BF)

    def scatter_start(buf, recv, kind):
        each(
            1,
            8,
            lambda d: to_chip(
                buf.at[core * 8 + lax.rem(chip + d, 8)], recv.at[d], kind, d
            ).start(),
        )

    def scatter_end(buf, recv, kind):
        each(
            1,
            8,
            lambda d: to_chip(
                buf.at[core * 8 + lax.rem(chip + d, 8)], recv.at[d], kind, d
            ).wait_recv(),
        )
        whole = buf[slot].astype(F32)
        for d in range(1, 8):
            whole = whole + recv[d].astype(F32)
        return whole.astype(BF)

    def spread_start(buf, kind):
        to_partner(buf.at[slot], buf.at[slot], kind, 0).start()
        each(1, 8, lambda d: to_chip(buf.at[slot], buf.at[slot], kind, d).start())

    def spread_pass(buf, kind, forward):
        def step(d):
            s = core * 8 + lax.rem(chip + 8 - d, 8)
            to_chip(buf.at[slot], buf.at[s], kind, d).wait_recv()
            to_partner(buf.at[s], buf.at[s], forward, d).start()

        each(1, 8, step)

    def spread_end(buf, kind, forward):
        s = other * 8 + chip
        to_partner(buf.at[s], buf.at[s], kind, 0).wait_recv()

        def step(d):
            t = other * 8 + lax.rem(chip + 8 - d, 8)
            to_partner(buf.at[t], buf.at[t], forward, d).wait_recv()

        each(1, 8, step)

    combine(ga, pa, 0).start()

    def vec_row(r, value):
        for j in range(8):
            vs[j, r : r + 1, :] = value[:, 128 * j : 128 * j + 128]

    def rows_sum(value):
        return jnp.sum(value, axis=0, keepdims=True)

    sum_up = rows_sum(du.astype(F32))
    for j in range(4):
        cvs[8 + j : 9 + j, :] = sum_up[:, 128 * j : 128 * j + 128]

    dc = reduce_end(rs2s, rs2r, RS2)
    d_hidden = g_mine + norm_back(dc, ln2_gain, hat_two, rstd_two)
    dh_all[wa] = d_hidden.astype(BF)
    gather_start(dh_all, AGD)
    combined(ga, pa, 0)
    scatter_start(ga, ra, RA)
    vec_row(0, rows_sum(dc * hat_two))
    vec_row(1, rows_sum(dc))
    vec_row(2, rows_sum(d_hidden))
    vec_row(3, rows_sum(g_mine))
    y_all[wa] = (hidden + reduce_end(rs3s, rs3r, RS3) + b_down).astype(BF)
    gather_start(y_all, AGY)
    gather_end(dh_all, AGD)

    dh_low = dh_all[...].reshape(128, 1024)
    d_attn = nt(dh_low, wout[...]).astype(BF)
    dot_t = d_attn.astype(F32).T * attn_t[...]
    delta = jnp.concatenate(
        [
            jnp.sum(dot_t[0:64], axis=0, keepdims=True),
            jnp.sum(dot_t[64:128], axis=0, keepdims=True),
        ],
        axis=1,
    )
    do2 = jnp.concatenate(
        [jnp.where(lane < 64, d_attn, zero), jnp.where(lane >= 64, d_attn, zero)], axis=0
    )
    acc[...] = jnp.zeros_like(acc)

    def back(s):
        p = jnp.exp(scores[s] - lse)
        ds = (p * (nt(kv[s, :, 128:256], do2) - delta)).astype(BF)
        acc[...] += tn(kv[s, :, 0:128], ds)
        dkv[s, :, 0:128] = nn(ds, q2[...]).astype(BF)
        dkv[s, :, 128:256] = nn(p.astype(BF), do2).astype(BF)

    each(0, 8, lambda j: back(other * 8 + j))
    combine(dkv, pkv, 1).start()
    each(0, 8, lambda j: back(core * 8 + j))
    combined(dkv, pkv, 1)
    scatter_start(dkv, rkv, RKV)

    dq = (diagonal(acc[...]) * 0.125).T.astype(BF)
    gb[:, 64:128, :] = tn(normed[...], dq).astype(BF).reshape(16, 64, 128)
    d_out = tn(attn_low[...], dh_low).astype(BF)
    for s in range(16):
        gb[s, 0:64, :] = d_out[64 * (s % 2) : 64 * (s % 2) + 64, 128 * (s // 2) : 128 * (s // 2) + 128]
    combine(gb, pb, 2).start()

    oa[slot] = scatter_end(ga, ra, RA)
    spread_start(oa, AGA)
    combined(gb, pb, 2)
    scatter_start(gb, rb, RB)

    dkv_mine = scatter_end(dkv, rkv, RKV)
    d_qkv = jnp.concatenate([dq, dkv_mine], axis=1)
    da = nt(d_qkv, wqkv[...])
    reduce_start(da, rs4s, rs4r, RS4)
    both = tn(normed[...], dkv_mine).astype(BF)
    gc[:, 0:64, :] = both[:, 0:128].reshape(16, 64, 128)
    gc[:, 64:128, :] = both[:, 128:256].reshape(16, 64, 128)
    combine(gc, pc, 3).start()
    vec_row(4, rows_sum(da * xhat_all[...]))
    vec_row(5, rows_sum(da))
    for j in range(8):
        vs[j, 6:8, :] = jnp.zeros((2, 128), F32)
    each(1, 8, lambda d: to_wa(vs.at[lax.rem(wa + d, 8)], vr.at[d], RS5, d).start())
    cvs[12:13, :] = rows_sum(dq.astype(F32))
    cvs[13:14, :] = rows_sum(dkv_mine[:, 128:256].astype(F32))
    cvs[14:16, :] = jnp.zeros((2, 128), F32)
    spread_pass(oa, AGA, FWA)
    combined(gc, pc, 3)
    scatter_start(gc, rc, RC)

    hat_one, rstd_one = normalize(x_mine)
    d_first = reduce_end(rs4s, rs4r, RS4)
    g_all[wa] = (d_hidden + norm_back(d_first, ln1_gain, hat_one, rstd_one)).astype(BF)
    gather_start(g_all, AGG)

    each(1, 8, lambda d: to_wa(vs.at[lax.rem(wa + d, 8)], vr.at[d], RS5, d).wait_recv())
    vec_sum = vs[wa]
    for d in range(1, 8):
        vec_sum = vec_sum + vr[d]
    cvs[0:8, :] = vec_sum
    cvr[ctx] = cvs[...]

    def to_ctx(dst, d):
        return pltpu.make_async_remote_copy(
            src_ref=cvs,
            dst_ref=cvr.at[dst],
            send_sem=cs_s.at[4 + d],
            recv_sem=cs_r.at[4 + d],
            device_id={"ctx": lax.rem(ctx + d, 16)},
            device_id_type=MESH,
        )

    each(1, 16, lambda d: to_ctx(ctx, d).start())
    ob[slot] = scatter_end(gb, rb, RB)
    spread_start(ob, AGB)
    oc[slot] = scatter_end(gc, rc, RC)
    spread_start(oc, AGCC)
    each(1, 16, lambda d: to_ctx(lax.rem(ctx + 16 - d, 16), d).wait_recv())
    ctx_sum = cvr[0]
    for i in range(1, 16):
        ctx_sum = ctx_sum + cvr[i]
    ctx_out[...] = ctx_sum[8:16, :]
    vall[wa] = ctx_sum[0:8, :]
    gather_start(vall, AGV)
    spread_pass(ob, AGB, FWB)
    spread_pass(oc, AGCC, FWC)

    spread_end(oa, AGA, FWA)
    gup_out[...] = oa[:, 0:64, :].reshape(1024, 512)
    gdn_out[:, 0:512] = oa[:, 64:96, :].reshape(512, 512)
    gdn_out[:, 512:1024] = oa[:, 96:128, :].reshape(512, 512)
    gather_end(y_all, AGY)
    y_out[...] = y_all[...].reshape(128, 1024)
    gather_end(g_all, AGG)
    gin_out[...] = g_all[...].reshape(128, 1024)
    spread_end(ob, AGB, FWB)
    for s in range(16):
        gwo_out[64 * (s % 2) : 64 * (s % 2) + 64, 128 * (s // 2) : 128 * (s // 2) + 128] = ob[
            s, 0:64, :
        ]
    gqkv_out[0] = ob[:, 64:128, :].reshape(1024, 128)
    spread_end(oc, AGCC, FWC)
    gqkv_out[1] = oc[:, 0:64, :].reshape(1024, 128)
    gqkv_out[2] = oc[:, 64:128, :].reshape(1024, 128)
    gather_end(vall, AGV)
    vec_out[...] = vall[...]

    for buf, kind, forward in ((kv, KV, KVF), (oa, AGA, FWA), (ob, AGB, FWB), (oc, AGCC, FWC)):
        to_partner(buf.at[slot], buf.at[slot], kind, 0).wait_send()

        def sent(d, buf=buf, kind=kind, forward=forward):
            to_chip(buf.at[slot], buf.at[slot], kind, d).wait_send()
            to_partner(buf.at[slot], buf.at[slot], forward, d).wait_send()

        each(1, 8, sent)
    for buf, kind in (
        (rs1s, RS1),
        (rs2s, RS2),
        (rs3s, RS3),
        (rs4s, RS4),
        (c_all, AGC),
        (dh_all, AGD),
        (y_all, AGY),
        (g_all, AGG),
        (vs, RS5),
        (vall, AGV),
    ):
        each(
            1,
            8,
            lambda d, buf=buf, kind=kind: to_wa(buf.at[wa], buf.at[wa], kind, d).wait_send(),
        )
    for buf, kind in ((ga, RA), (dkv, RKV), (gb, RB), (gc, RC)):
        each(
            1,
            8,
            lambda d, buf=buf, kind=kind: to_chip(
                buf.at[slot], buf.at[slot], kind, d
            ).wait_send(),
        )
    for index, (buf, kept) in enumerate(((ga, pa), (dkv, pkv), (gb, pb), (gc, pc))):
        combine(buf, kept, index).wait_send()
    each(1, 16, lambda d: to_ctx(ctx, d).wait_send())


def body(
    layer_input,
    block_order,
    seg_ids,
    cotangent,
    ln1_gain,
    ln1_bias,
    w_qkv,
    b_qv,
    w_out,
    b_out,
    ln2_gain,
    ln2_bias,
    w_up,
    b_up,
    w_down,
    b_down,
):
    vectors = jnp.stack(
        [
            ln1_gain,
            ln1_bias,
            b_out,
            ln2_gain,
            ln2_bias,
            b_down,
            jnp.pad(b_up, (0, 512)),
            jnp.pad(b_qv.reshape(256), (0, 768)),
        ]
    ).astype(F32)
    vmem = pl.BlockSpec(memory_space=pltpu.VMEM)
    smem = pl.BlockSpec(memory_space=pltpu.SMEM)
    hbm = pl.BlockSpec(memory_space=pl.ANY)

    def bf(*shape):
        return pltpu.VMEM(shape, BF)

    def f32(*shape):
        return pltpu.VMEM(shape, F32)

    outs = pl.pallas_call(
        kernel,
        out_shape=(
            jax.ShapeDtypeStruct((128, 1024), BF),
            jax.ShapeDtypeStruct((128, 1024), BF),
            jax.ShapeDtypeStruct((1024, 512), BF),
            jax.ShapeDtypeStruct((512, 1024), BF),
            jax.ShapeDtypeStruct((128, 1024), BF),
            jax.ShapeDtypeStruct((3, 1024, 128), BF),
            jax.ShapeDtypeStruct((8, 8, 128), F32),
            jax.ShapeDtypeStruct((8, 128), F32),
        ),
        in_specs=[smem, vmem, vmem, vmem, vmem, hbm, hbm, hbm, hbm],
        out_specs=(vmem,) * 8,
        scratch_shapes=[
            bf(1024, 384),
            bf(128, 1024),
            bf(1024, 512),
            bf(512, 1024),
            pltpu.SemaphoreType.DMA((6,)),
            f32(128, 1024),
            bf(128, 1024),
            bf(16, 128, 256),
            bf(256, 128),
            f32(16, 128, 256),
            f32(128, 256),
            f32(128, 128),
            bf(128, 128),
            bf(8, 16, 1024),
            bf(8, 16, 1024),
            bf(8, 16, 1024),
            f32(128, 512),
            bf(8, 16, 1024),
            bf(8, 16, 1024),
            bf(8, 16, 1024),
            bf(8, 16, 1024),
            bf(8, 16, 1024),
            bf(8, 16, 1024),
            bf(16, 128, 256),
            bf(8, 128, 256),
            bf(8, 128, 256),
            bf(16, 128, 512),
            bf(8, 128, 512),
            bf(8, 128, 512),
            bf(16, 128, 512),
            bf(16, 128, 128),
            bf(8, 128, 128),
            bf(8, 128, 128),
            bf(16, 128, 128),
            bf(16, 128, 128),
            bf(8, 128, 128),
            bf(8, 128, 128),
            bf(16, 128, 128),
            bf(8, 16, 1024),
            bf(8, 16, 1024),
            bf(8, 16, 1024),
            f32(8, 8, 128),
            f32(8, 8, 128),
            f32(8, 8, 128),
            f32(16, 128),
            f32(16, 16, 128),
            pltpu.SemaphoreType.DMA((NSEM, 8)),
            pltpu.SemaphoreType.DMA((NSEM, 8)),
            pltpu.SemaphoreType.DMA((20,)),
            pltpu.SemaphoreType.DMA((20,)),
        ],
        compiler_params=pltpu.CompilerParams(
            collective_id=0, has_side_effects=True, vmem_limit_bytes=56 << 20
        ),
        name="layer",
    )(
        block_order,
        seg_ids.reshape(16, 128),
        layer_input,
        cotangent,
        vectors,
        w_qkv.transpose(1, 0, 2),
        w_out,
        w_up,
        w_down,
    )
    y, gin, gup, gdn, gwo, gqkv, vec, ctx_vec = outs

    def whole(r):
        return vec[:, r, :].reshape(1024)

    return (
        y,
        gin.astype(F32),
        whole(4),
        whole(5),
        gqkv.astype(F32).transpose(1, 0, 2),
        ctx_vec[4:6, :],
        gwo.astype(F32),
        whole(2),
        whole(0),
        whole(1),
        gup.astype(F32),
        ctx_vec[0:4, :].reshape(512),
        gdn.astype(F32),
        whole(3),
    )


def solution(mesh):
    placed = (
        P("ctx", None),
        P(),
        P(),
        P("ctx", None),
        P(),
        P(),
        P(None, None, "wa"),
        P(None, "wa"),
        P("wa", None),
        P(),
        P(),
        P(),
        P(None, "wa"),
        P("wa"),
        P("wa", None),
        P(),
    )
    return jax.shard_map(
        body,
        mesh=mesh,
        in_specs=placed,
        out_specs=(
            P("ctx", None),
            P("ctx", None),
            P(),
            P(),
            P(None, None, "wa"),
            P(None, "wa"),
            P("wa", None),
            P(),
            P(),
            P(),
            P(None, "wa"),
            P("wa"),
            P("wa", None),
            P(),
        ),
        check_vma=False,
    )
```

```python
import jax
import jax.numpy as jnp
from jax import lax
from jax.experimental import pallas as pl
from jax.experimental.pallas import tpu as pltpu
from jax.sharding import PartitionSpec as P

F32 = jnp.float32
BF = jnp.bfloat16
MESH = pl.DeviceIdType.MESH
GELU_A = 0.7978845608028654
GELU_B = 0.044715

(
    KV,
    KVF,
    RS1,
    AGC,
    RS2,
    RS3,
    AGD,
    AGY,
    CMB,
    RKV,
    RA,
    AGA,
    FWA,
    RB,
    AGB,
    FWB,
    RC,
    AGCC,
    FWC,
    RS4,
    RS5,
    AGG,
    AGV,
    NSEM,
) = range(24)


def nn(a, b):
    return lax.dot_general(a, b, (((1,), (0,)), ((), ())), preferred_element_type=F32)


def nt(a, b):
    return lax.dot_general(a, b, (((1,), (1,)), ((), ())), preferred_element_type=F32)


def tn(a, b):
    return lax.dot_general(a, b, (((0,), (0,)), ((), ())), preferred_element_type=F32)


def normalize(rows):
    centered = rows - jnp.mean(rows, -1, keepdims=True)
    rstd = lax.rsqrt(jnp.mean(centered * centered, -1, keepdims=True) + 1e-05)
    return centered * rstd, rstd


def norm_back(grad, gain, xhat, rstd):
    gx = grad * gain
    return rstd * (
        gx - jnp.mean(gx, -1, keepdims=True) - xhat * jnp.mean(gx * xhat, -1, keepdims=True)
    )


def layer(
    order_ref,
    seg_ref,
    x_hbm,
    g_hbm,
    ln1g_ref,
    ln1b_ref,
    bout_ref,
    ln2g_ref,
    ln2b_ref,
    bdown_ref,
    bup_ref,
    bqv_ref,
    wqkv_hbm,
    wout_hbm,
    wup_hbm,
    wdn_hbm,
    y_out,
    gin_out,
    oa_out,
    ob_out,
    oc_out,
    vec_out,
    ctx_out,
    x_ref,
    g_ref,
    wqkv,
    wout,
    wup,
    wdn,
    load_sem,
    xhat_all,
    normed,
    kv,
    q2,
    scores,
    acc,
    attn_t,
    attn_low,
    rs1s,
    rs1r,
    c_all,
    dm,
    rs2s,
    rs2r,
    rs3s,
    rs3r,
    dh_all,
    y_all,
    dkv,
    pkv,
    rkv,
    ga,
    pa,
    ra,
    oa,
    gb,
    pb,
    rb,
    ob,
    gc,
    pc,
    rc,
    oc,
    rs4s,
    rs4r,
    g_all,
    vs,
    vr,
    vall,
    cvs,
    cvr,
    ss,
    rs,
    cs_s,
    cs_r,
):
    ctx = lax.axis_index("ctx")
    wa = lax.axis_index("wa")
    core = lax.rem(ctx, 2)
    chip = lax.div(ctx, 2)
    other = 1 - core
    slot = core * 8 + chip
    partner = chip * 2 + other

    def to_wa(src, dst, kind, d):
        return pltpu.make_async_remote_copy(
            src_ref=src,
            dst_ref=dst,
            send_sem=ss.at[kind, d],
            recv_sem=rs.at[kind, d],
            device_id={"wa": lax.rem(wa + d, 8)},
            device_id_type=MESH,
        )

    def to_chip(src, dst, kind, d):
        return pltpu.make_async_remote_copy(
            src_ref=src,
            dst_ref=dst,
            send_sem=ss.at[kind, d],
            recv_sem=rs.at[kind, d],
            device_id={"ctx": lax.rem(chip + d, 8) * 2 + core},
            device_id_type=MESH,
        )

    def to_partner(src, dst, kind, d):
        return pltpu.make_async_remote_copy(
            src_ref=src,
            dst_ref=dst,
            send_sem=ss.at[kind, d],
            recv_sem=rs.at[kind, d],
            device_id={"ctx": partner},
            device_id_type=MESH,
        )

    sends = []
    arrivals = {}

    def each(low, high, step):
        @pl.loop(low, high)
        def _(d):
            step(d)

    loads = [
        pltpu.make_async_copy(
            wqkv_hbm.at[i], wqkv.at[:, pl.ds(128 * i, 128)], load_sem.at[i]
        )
        for i in range(3)
    ] + [
        pltpu.make_async_copy(wdn_hbm, wdn, load_sem.at[3]),
        pltpu.make_async_copy(wout_hbm, wout, load_sem.at[4]),
        pltpu.make_async_copy(wup_hbm, wup, load_sem.at[5]),
        pltpu.make_async_copy(x_hbm, x_ref, load_sem.at[6]),
        pltpu.make_async_copy(g_hbm, g_ref, load_sem.at[7]),
    ]
    for i in (6, 0, 1, 2, 7, 3, 4, 5):
        loads[i].start()

    def combine(buf, kept, index):
        return pltpu.make_async_remote_copy(
            src_ref=buf.at[pl.ds(pl.multiple_of(other * 8, 8), 8)],
            dst_ref=kept,
            send_sem=cs_s.at[index],
            recv_sem=cs_r.at[index],
            device_id={"ctx": partner},
            device_id_type=MESH,
        )

    def combine_start(buf, kept, index):
        combine(buf, kept, index).start()
        sends.append(lambda: combine(buf, kept, index).wait_send())
        arrivals[100 + index] = lambda: combined(buf, kept, index)

    def combined(buf, kept, index):
        arrivals.pop(100 + index)
        combine(buf, kept, index).wait_recv()

        @pl.loop(0, 8)
        def _(j):
            buf[core * 8 + j] = (buf[core * 8 + j].astype(F32) + kept[j].astype(F32)).astype(BF)

    def scatter_start(buf, recv, kind):
        sends.append(
            lambda: each(
                1, 8, lambda d: to_chip(buf.at[slot], buf.at[slot], kind, d).wait_send()
            )
        )
        arrivals[kind] = lambda: scatter_end(buf, recv, kind)
        each(
            1,
            8,
            lambda d: to_chip(
                buf.at[core * 8 + lax.rem(chip + d, 8)], recv.at[d], kind, d
            ).start(),
        )

    def scatter_end(buf, recv, kind):
        arrivals.pop(kind)
        each(
            1,
            8,
            lambda d: to_chip(
                buf.at[core * 8 + lax.rem(chip + d, 8)], recv.at[d], kind, d
            ).wait_recv(),
        )
        whole = buf[slot].astype(F32)
        for d in range(1, 8):
            whole = whole + recv[d].astype(F32)
        return whole.astype(BF)

    def spread_start(buf, kind, forward):
        sends.append(lambda: spread_sent(buf, kind, forward))
        arrivals[kind] = lambda: (
            spread_pass(buf, kind, forward),
            spread_end(buf, kind, forward),
        )
        to_partner(buf.at[slot], buf.at[slot], kind, 0).start()
        each(1, 8, lambda d: to_chip(buf.at[slot], buf.at[slot], kind, d).start())

    def spread_sent(buf, kind, forward):
        to_partner(buf.at[slot], buf.at[slot], kind, 0).wait_send()

        def sent(d):
            to_chip(buf.at[slot], buf.at[slot], kind, d).wait_send()
            to_partner(buf.at[slot], buf.at[slot], forward, d).wait_send()

        each(1, 8, sent)

    def spread_pass(buf, kind, forward):
        arrivals[kind] = lambda: spread_end(buf, kind, forward)

        def step(d):
            s = core * 8 + lax.rem(chip + 8 - d, 8)
            to_chip(buf.at[slot], buf.at[s], kind, d).wait_recv()
            to_partner(buf.at[s], buf.at[s], forward, d).start()

        each(1, 8, step)

    def spread_end(buf, kind, forward):
        arrivals.pop(kind)
        s = other * 8 + chip
        to_partner(buf.at[s], buf.at[s], kind, 0).wait_recv()

        def step(d):
            t = other * 8 + lax.rem(chip + 8 - d, 8)
            to_partner(buf.at[t], buf.at[t], forward, d).wait_recv()

        each(1, 8, step)

    def reduce_start(part, send, recv, kind):
        send[...] = part.astype(BF).reshape(8, 16, 1024)
        each(1, 8, lambda d: to_wa(send.at[lax.rem(wa + d, 8)], recv.at[d], kind, d).start())
        sends.append(lambda: wa_sent(send, kind))
        arrivals[kind] = lambda: reduce_end(send, recv, kind)

    def reduce_end(send, recv, kind):
        arrivals.pop(kind)
        each(1, 8, lambda d: to_wa(send.at[lax.rem(wa + d, 8)], recv.at[d], kind, d).wait_recv())
        whole = send[wa].astype(F32)
        for d in range(1, 8):
            whole = whole + recv[d].astype(F32)
        return whole

    def gather_start(buf, kind):
        each(1, 8, lambda d: to_wa(buf.at[wa], buf.at[wa], kind, d).start())
        sends.append(lambda: wa_sent(buf, kind))
        arrivals[kind] = lambda: gather_end(buf, kind)

    def wa_sent(buf, kind):
        each(1, 8, lambda d: to_wa(buf.at[wa], buf.at[wa], kind, d).wait_send())

    def gather_end(buf, kind):
        arrivals.pop(kind)
        each(
            1,
            8,
            lambda d: to_wa(buf.at[wa], buf.at[lax.rem(wa + 8 - d, 8)], kind, d).wait_recv(),
        )

    barrier = pltpu.get_barrier_semaphore()
    each(
        1,
        16,
        lambda d: pl.semaphore_signal(
            barrier, inc=1, device_id={"ctx": lax.rem(ctx + d, 16)}, device_id_type=MESH
        ),
    )
    each(
        1,
        8,
        lambda d: pl.semaphore_signal(
            barrier, inc=1, device_id={"wa": lax.rem(wa + d, 8)}, device_id_type=MESH
        ),
    )

    def vector(ref):
        rows = ref[...].astype(F32)
        return jnp.concatenate([rows[j : j + 1, :] for j in range(rows.shape[0])], axis=1)

    ln1_gain = vector(ln1g_ref)
    ln1_bias = vector(ln1b_ref)
    b_out = vector(bout_ref)
    ln2_gain = vector(ln2g_ref)
    ln2_bias = vector(ln2b_ref)
    b_down = vector(bdown_ref)
    b_up = vector(bup_ref)
    b_qv = bqv_ref[...].astype(F32)
    b_q = b_qv[0:1, :]
    b_v = b_qv[1:2, :]

    loads[6].wait()
    xhat, _ = normalize(x_ref[...].astype(F32))
    xhat_all[...] = xhat
    normed[...] = (xhat * ln1_gain + ln1_bias).astype(BF)
    for i in range(3):
        loads[i].wait()
    proj = nn(normed[...], wqkv[...])
    kv[slot, :, 0:128] = proj[:, 128:256].astype(BF)
    kv[slot, :, 128:256] = (proj[:, 256:384] + b_v).astype(BF)
    pl.semaphore_wait(barrier, 22)

    to_partner(kv.at[slot], kv.at[slot], KV, 0).start()
    each(1, 8, lambda d: to_chip(kv.at[slot], kv.at[slot], KV, d).start())
    sends.append(lambda: spread_sent(kv, KV, KVF))
    arrivals[KV] = lambda: (spread_pass(kv, KV, KVF), spread_end(kv, KV, KVF))

    q_low = (proj[:, 0:128] + b_q).astype(BF) * jnp.asarray(0.125, BF)
    lane = lax.broadcasted_iota(jnp.int32, (128, 128), 1)
    zero = jnp.zeros((128, 128), BF)
    q2[0:128, :] = jnp.where(lane < 64, q_low, zero)
    q2[128:256, :] = jnp.where(lane >= 64, q_low, zero)

    lanes = lax.broadcasted_iota(jnp.int32, (1, 256), 1)
    lanes = jnp.where(lanes >= 128, lanes - 128, lanes)
    q_pos = jnp.where(
        lanes < 64, lanes + 64 * order_ref[2 * ctx], lanes - 64 + 64 * order_ref[2 * ctx + 1]
    )
    seg = seg_ref[...]
    one = jnp.ones(seg.shape, F32)
    none = jnp.zeros(seg.shape, F32)

    def count(test):
        part = jnp.sum(jnp.where(test, one, none), axis=0, keepdims=True)
        return jnp.sum(part, axis=1, keepdims=True)

    first_end = count(seg < 1)
    second_end = count(seg < 2)
    q_float = q_pos.astype(F32)
    q_first = jnp.where(
        q_float >= second_end,
        second_end,
        jnp.where(q_float >= first_end, first_end, jnp.zeros_like(q_float)),
    ).astype(jnp.int32)
    row = lax.broadcasted_iota(jnp.int32, (128, 256), 0)

    def score(s, top):
        keys = kv[s, :, 0:128]
        owner = 2 * lax.rem(s, 8) + lax.div(s, 8)
        k_pos = jnp.where(
            row < 64, row + 64 * order_ref[2 * owner], row - 64 + 64 * order_ref[2 * owner + 1]
        )
        allowed = (k_pos <= q_pos) & (k_pos >= q_first)
        masked = jnp.where(allowed, nt(keys, q2[...]), -1e30)
        scores[s] = masked
        return jnp.maximum(top, jnp.max(masked.reshape(16, 8, 256), axis=0))

    loads[7].wait()
    loads[3].wait()
    dm[...] = nt(g_ref[...], wdn[...])

    top = score(slot, jnp.full((8, 256), -1e30, F32))
    to_partner(kv.at[slot], kv.at[slot], KV, 0).wait_recv()
    top = score(other * 8 + chip, top)

    def near(d, top):
        s = core * 8 + lax.rem(chip + 8 - d, 8)
        to_chip(kv.at[slot], kv.at[s], KV, d).wait_recv()
        to_partner(kv.at[s], kv.at[s], KVF, d).start()
        return score(s, top)

    top = lax.fori_loop(1, 8, near, top)

    def far(d, top):
        s = other * 8 + lax.rem(chip + 8 - d, 8)
        to_partner(kv.at[s], kv.at[s], KVF, d).wait_recv()
        return score(s, top)

    top = lax.fori_loop(1, 8, far, top)
    arrivals.pop(KV)

    top = jnp.max(top, axis=0, keepdims=True)
    acc[...] = jnp.zeros_like(acc)

    def mix(s, total):
        p = jnp.exp(scores[s] - top)
        acc[...] += tn(kv[s, :, 128:256], p.astype(BF))
        return total + jnp.sum(p.reshape(16, 8, 256), axis=0)

    total = lax.fori_loop(0, 16, mix, jnp.zeros((8, 256), F32))
    total = jnp.sum(total, axis=0, keepdims=True)
    lse = top + jnp.log(total)
    half = lax.broadcasted_iota(jnp.int32, (128, 128), 0) < 64

    def diagonal(both):
        return jnp.where(half, both[:, 0:128], both[:, 128:256])

    raw_t = diagonal(acc[...] / total)
    attn_t[...] = raw_t
    attn_low[...] = raw_t.T.astype(BF)

    loads[4].wait()
    reduce_start(nn(attn_low[...], wout[...]), rs1s, rs1r, RS1)
    mine = pl.ds(pl.multiple_of(wa * 16, 16), 16)
    x_mine = x_ref[mine, :].astype(F32)
    g_mine = g_ref[mine, :].astype(F32)
    hidden = x_mine + reduce_end(rs1s, rs1r, RS1) + b_out
    hat_two, rstd_two = normalize(hidden)
    c_all[wa] = (hat_two * ln2_gain + ln2_bias).astype(BF)
    gather_start(c_all, AGC)
    loads[5].wait()
    gather_end(c_all, AGC)

    c_low = c_all[...].reshape(128, 1024)
    up = nn(c_low, wup[...]) + b_up
    tanh = jnp.tanh(GELU_A * (up + GELU_B * up * up * up))
    slope = 0.5 * (1.0 + tanh) + 0.5 * up * (1.0 - tanh * tanh) * GELU_A * (
        1.0 + 3.0 * GELU_B * up * up
    )
    du = (dm[...] * slope).astype(BF)
    act = (0.5 * up * (1.0 + tanh)).astype(BF)
    reduce_start(nt(du, wup[...]), rs2s, rs2r, RS2)
    reduce_start(nn(act, wdn[...]), rs3s, rs3r, RS3)
    ga[:, 0:64, :] = tn(c_low, du).astype(BF).reshape(16, 64, 512)
    down = tn(act, g_ref[...]).astype(BF)
    ga[:, 64:96, :] = down[:, 0:512].reshape(16, 32, 512)
    ga[:, 96:128, :] = down[:, 512:1024].reshape(16, 32, 512)

    combine_start(ga, pa, 0)

    def vec_row(r, value):
        for j in range(8):
            vs[j, r : r + 1, :] = value[:, 128 * j : 128 * j + 128]

    def rows_sum(value):
        return jnp.sum(value, axis=0, keepdims=True)

    sum_up = rows_sum(du.astype(F32))
    for j in range(4):
        cvs[8 + j : 9 + j, :] = sum_up[:, 128 * j : 128 * j + 128]

    dc = reduce_end(rs2s, rs2r, RS2)
    d_hidden = g_mine + norm_back(dc, ln2_gain, hat_two, rstd_two)
    dh_all[wa] = d_hidden.astype(BF)
    gather_start(dh_all, AGD)
    combined(ga, pa, 0)
    scatter_start(ga, ra, RA)
    vec_row(0, rows_sum(dc * hat_two))
    vec_row(1, rows_sum(dc))
    vec_row(2, rows_sum(d_hidden))
    vec_row(3, rows_sum(g_mine))
    y_all[wa] = (hidden + reduce_end(rs3s, rs3r, RS3) + b_down).astype(BF)
    gather_start(y_all, AGY)
    gather_end(dh_all, AGD)

    dh_low = dh_all[...].reshape(128, 1024)
    d_attn = nt(dh_low, wout[...]).astype(BF)
    dot_t = d_attn.astype(F32).T * attn_t[...]
    delta = jnp.concatenate(
        [
            jnp.sum(dot_t[0:64], axis=0, keepdims=True),
            jnp.sum(dot_t[64:128], axis=0, keepdims=True),
        ],
        axis=1,
    )
    do2 = jnp.concatenate(
        [jnp.where(lane < 64, d_attn, zero), jnp.where(lane >= 64, d_attn, zero)], axis=0
    )
    acc[...] = jnp.zeros_like(acc)

    def back(s):
        p = jnp.exp(scores[s] - lse)
        ds = (p * (nt(kv[s, :, 128:256], do2) - delta)).astype(BF)
        acc[...] += tn(kv[s, :, 0:128], ds)
        dkv[s, :, 0:128] = nn(ds, q2[...]).astype(BF)
        dkv[s, :, 128:256] = nn(p.astype(BF), do2).astype(BF)

    each(0, 8, lambda j: back(other * 8 + j))
    combine_start(dkv, pkv, 1)
    each(0, 8, lambda j: back(core * 8 + j))
    combined(dkv, pkv, 1)
    scatter_start(dkv, rkv, RKV)

    dq = (diagonal(acc[...]) * 0.125).T.astype(BF)
    gb[:, 64:128, :] = tn(normed[...], dq).astype(BF).reshape(16, 64, 128)
    d_out = tn(attn_low[...], dh_low).astype(BF)
    for s in range(16):
        gb[s, 0:64, :] = d_out[64 * (s % 2) : 64 * (s % 2) + 64, 128 * (s // 2) : 128 * (s // 2) + 128]
    combine_start(gb, pb, 2)

    oa[slot] = scatter_end(ga, ra, RA)
    spread_start(oa, AGA, FWA)
    combined(gb, pb, 2)
    scatter_start(gb, rb, RB)

    dkv_mine = scatter_end(dkv, rkv, RKV)
    d_qkv = jnp.concatenate([dq, dkv_mine], axis=1)
    da = nt(d_qkv, wqkv[...])
    reduce_start(da, rs4s, rs4r, RS4)
    both = tn(normed[...], dkv_mine).astype(BF)
    gc[:, 0:64, :] = both[:, 0:128].reshape(16, 64, 128)
    gc[:, 64:128, :] = both[:, 128:256].reshape(16, 64, 128)
    combine_start(gc, pc, 3)
    vec_row(4, rows_sum(da * xhat_all[...]))
    vec_row(5, rows_sum(da))
    for j in range(8):
        vs[j, 6:8, :] = jnp.zeros((2, 128), F32)
    each(1, 8, lambda d: to_wa(vs.at[lax.rem(wa + d, 8)], vr.at[d], RS5, d).start())
    sends.append(lambda: wa_sent(vs, RS5))
    cvs[12:13, :] = rows_sum(dq.astype(F32))
    cvs[13:14, :] = rows_sum(dkv_mine[:, 128:256].astype(F32))
    cvs[14:16, :] = jnp.zeros((2, 128), F32)
    spread_pass(oa, AGA, FWA)
    combined(gc, pc, 3)
    scatter_start(gc, rc, RC)

    hat_one, rstd_one = normalize(x_mine)
    d_first = reduce_end(rs4s, rs4r, RS4)
    g_all[wa] = (d_hidden + norm_back(d_first, ln1_gain, hat_one, rstd_one)).astype(BF)
    gather_start(g_all, AGG)

    each(1, 8, lambda d: to_wa(vs.at[lax.rem(wa + d, 8)], vr.at[d], RS5, d).wait_recv())
    vec_sum = vs[wa]
    for d in range(1, 8):
        vec_sum = vec_sum + vr[d]
    cvs[0:8, :] = vec_sum
    cvr[ctx] = cvs[...]

    def to_ctx(dst, d):
        return pltpu.make_async_remote_copy(
            src_ref=cvs,
            dst_ref=cvr.at[dst],
            send_sem=cs_s.at[4 + d],
            recv_sem=cs_r.at[4 + d],
            device_id={"ctx": lax.rem(ctx + d, 16)},
            device_id_type=MESH,
        )

    each(1, 16, lambda d: to_ctx(ctx, d).start())
    sends.append(lambda: each(1, 16, lambda d: to_ctx(ctx, d).wait_send()))
    ob[slot] = scatter_end(gb, rb, RB)
    spread_start(ob, AGB, FWB)
    oc[slot] = scatter_end(gc, rc, RC)
    spread_start(oc, AGCC, FWC)
    each(1, 16, lambda d: to_ctx(lax.rem(ctx + 16 - d, 16), d).wait_recv())
    ctx_sum = cvr[0]
    for i in range(1, 16):
        ctx_sum = ctx_sum + cvr[i]
    ctx_out[...] = ctx_sum[8:16, :]
    vall[wa] = ctx_sum[0:8, :]
    gather_start(vall, AGV)
    spread_pass(ob, AGB, FWB)
    spread_pass(oc, AGCC, FWC)

    spread_end(oa, AGA, FWA)
    oa_out[...] = oa[...]
    gather_end(y_all, AGY)
    y_out[...] = y_all[...].reshape(128, 1024)
    gather_end(g_all, AGG)
    gin_out[...] = g_all[...].reshape(128, 1024)
    spread_end(ob, AGB, FWB)
    ob_out[...] = ob[...]
    spread_end(oc, AGCC, FWC)
    oc_out[...] = oc[...]
    gather_end(vall, AGV)
    vec_out[...] = vall[...]

    for sent in sends:
        sent()


def finish(
    y_ref,
    gin_ref,
    oa_ref,
    ob_ref,
    oc_ref,
    vec_ref,
    ctx_ref,
    y_out,
    gin_out,
    ln1g_out,
    ln1b_out,
    gqkv_out,
    bqv_out,
    gwo_out,
    bout_out,
    ln2g_out,
    ln2b_out,
    gup_out,
    bup_out,
    gdn_out,
    bdown_out,
    gin,
    gqkv,
    gwo,
    gup,
    gdn,
    sems,
):
    copies = []

    def leave(src, dst):
        copies.append(pltpu.make_async_copy(src, dst, sems.at[len(copies)]))
        copies[-1].start()

    leave(y_ref, y_out)
    for i in range(4):
        rows = pl.ds(256 * i, 256)
        gup[rows, :] = oa_ref[4 * i : 4 * i + 4, 0:64, :].astype(F32).reshape(256, 512)
        leave(gup.at[rows], gup_out.at[rows])
    for i in range(4):
        rows = pl.ds(128 * i, 128)
        part = oa_ref[4 * i : 4 * i + 4, 64:128, :].astype(F32)
        gdn[rows, 0:512] = part[:, 0:32].reshape(128, 512)
        gdn[rows, 512:1024] = part[:, 32:64].reshape(128, 512)
        leave(gdn.at[rows], gdn_out.at[rows])
    gin[...] = gin_ref[...].astype(F32)
    leave(gin, gin_out)
    for s in range(16):
        gwo[64 * (s % 2) : 64 * (s % 2) + 64, 128 * (s // 2) : 128 * (s // 2) + 128] = ob_ref[
            s, 0:64, :
        ].astype(F32)
    leave(gwo, gwo_out)
    gqkv[0] = ob_ref[:, 64:128, :].astype(F32).reshape(1024, 128)
    leave(gqkv.at[0], gqkv_out.at[0])
    gqkv[1] = oc_ref[:, 0:64, :].astype(F32).reshape(1024, 128)
    leave(gqkv.at[1], gqkv_out.at[1])
    gqkv[2] = oc_ref[:, 64:128, :].astype(F32).reshape(1024, 128)
    leave(gqkv.at[2], gqkv_out.at[2])
    for r, out in enumerate((ln2g_out, ln2b_out, bout_out, bdown_out, ln1g_out, ln1b_out)):
        out[...] = vec_ref[:, r, :]
    bup_out[...] = ctx_ref[0:4, :]
    bqv_out[...] = ctx_ref[4:6, :]
    for copy in copies:
        copy.wait()


def body(
    layer_input,
    block_order,
    seg_ids,
    cotangent,
    ln1_gain,
    ln1_bias,
    w_qkv,
    b_qv,
    w_out,
    b_out,
    ln2_gain,
    ln2_bias,
    w_up,
    b_up,
    w_down,
    b_down,
):
    vmem = pl.BlockSpec(memory_space=pltpu.VMEM)
    smem = pl.BlockSpec(memory_space=pltpu.SMEM)
    hbm = pl.BlockSpec(memory_space=pl.ANY)
    far = pl.BlockSpec(memory_space=pltpu.HBM)

    def stay(operand):
        return pltpu.with_memory_space_constraint(operand, pltpu.HBM)

    def bf(*shape):
        return pltpu.VMEM(shape, BF)

    def f32(*shape):
        return pltpu.VMEM(shape, F32)

    outs = pl.pallas_call(
        layer,
        out_shape=(
            jax.ShapeDtypeStruct((128, 1024), BF),
            jax.ShapeDtypeStruct((128, 1024), BF),
            jax.ShapeDtypeStruct((16, 128, 512), BF),
            jax.ShapeDtypeStruct((16, 128, 128), BF),
            jax.ShapeDtypeStruct((16, 128, 128), BF),
            jax.ShapeDtypeStruct((8, 8, 128), F32),
            jax.ShapeDtypeStruct((8, 128), F32),
        ),
        in_specs=[smem, vmem, far, far] + [vmem] * 8 + [far] * 4,
        out_specs=(vmem,) * 7,
        scratch_shapes=[
            bf(128, 1024),
            bf(128, 1024),
            bf(1024, 384),
            bf(128, 1024),
            bf(1024, 512),
            bf(512, 1024),
            pltpu.SemaphoreType.DMA((8,)),
            f32(128, 1024),
            bf(128, 1024),
            bf(16, 128, 256),
            bf(256, 128),
            f32(16, 128, 256),
            f32(128, 256),
            f32(128, 128),
            bf(128, 128),
            bf(8, 16, 1024),
            bf(8, 16, 1024),
            bf(8, 16, 1024),
            f32(128, 512),
            bf(8, 16, 1024),
            bf(8, 16, 1024),
            bf(8, 16, 1024),
            bf(8, 16, 1024),
            bf(8, 16, 1024),
            bf(8, 16, 1024),
            bf(16, 128, 256),
            bf(8, 128, 256),
            bf(8, 128, 256),
            bf(16, 128, 512),
            bf(8, 128, 512),
            bf(8, 128, 512),
            bf(16, 128, 512),
            bf(16, 128, 128),
            bf(8, 128, 128),
            bf(8, 128, 128),
            bf(16, 128, 128),
            bf(16, 128, 128),
            bf(8, 128, 128),
            bf(8, 128, 128),
            bf(16, 128, 128),
            bf(8, 16, 1024),
            bf(8, 16, 1024),
            bf(8, 16, 1024),
            f32(8, 8, 128),
            f32(8, 8, 128),
            f32(8, 8, 128),
            f32(16, 128),
            f32(16, 16, 128),
            pltpu.SemaphoreType.DMA((NSEM, 8)),
            pltpu.SemaphoreType.DMA((NSEM, 8)),
            pltpu.SemaphoreType.DMA((20,)),
            pltpu.SemaphoreType.DMA((20,)),
        ],
        compiler_params=pltpu.CompilerParams(
            collective_id=0, has_side_effects=True, vmem_limit_bytes=32 << 20
        ),
        name="decoder",
    )(
        block_order,
        seg_ids.reshape(16, 128),
        stay(layer_input),
        stay(cotangent),
        *(v.reshape(-1, 128) for v in (ln1_gain, ln1_bias, b_out, ln2_gain, ln2_bias, b_down, b_up)),
        b_qv,
        stay(w_qkv.transpose(1, 0, 2)),
        stay(w_out),
        stay(w_up),
        stay(w_down),
    )
    shapes = (
        ((128, 1024), BF),
        ((128, 1024), F32),
        ((8, 128), F32),
        ((8, 128), F32),
        ((3, 1024, 128), F32),
        ((2, 128), F32),
        ((128, 1024), F32),
        ((8, 128), F32),
        ((8, 128), F32),
        ((8, 128), F32),
        ((1024, 512), F32),
        ((4, 128), F32),
        ((512, 1024), F32),
        ((8, 128), F32),
    )
    large = (0, 1, 4, 6, 10, 12)
    done = list(
        pl.pallas_call(
            finish,
            out_shape=tuple(jax.ShapeDtypeStruct(*shape) for shape in shapes),
            in_specs=[vmem] * 7,
            out_specs=tuple(hbm if i in large else vmem for i in range(14)),
            scratch_shapes=[
                f32(128, 1024),
                f32(3, 1024, 128),
                f32(128, 1024),
                f32(1024, 512),
                f32(512, 1024),
                pltpu.SemaphoreType.DMA((14,)),
            ],
            compiler_params=pltpu.CompilerParams(vmem_limit_bytes=24 << 20),
            name="finish",
        )(*outs)
    )
    for i in (2, 3, 7, 8, 9, 11, 13):
        done[i] = done[i].reshape(-1)
    done[4] = done[4].transpose(1, 0, 2)
    return tuple(done)


def solution(mesh):
    placed = (
        P("ctx", None),
        P(),
        P(),
        P("ctx", None),
        P(),
        P(),
        P(None, None, "wa"),
        P(None, "wa"),
        P("wa", None),
        P(),
        P(),
        P(),
        P(None, "wa"),
        P("wa"),
        P("wa", None),
        P(),
    )
    return jax.shard_map(
        body,
        mesh=mesh,
        in_specs=placed,
        out_specs=(
            P("ctx", None),
            P("ctx", None),
            P(),
            P(),
            P(None, None, "wa"),
            P(None, "wa"),
            P("wa", None),
            P(),
            P(),
            P(),
            P(None, "wa"),
            P("wa"),
            P("wa", None),
            P(),
        ),
        check_vma=False,
    )
```

```python
import jax
import jax.numpy as jnp
from jax import lax
from jax.experimental import pallas as pl
from jax.experimental.pallas import tpu as pltpu
from jax.sharding import PartitionSpec as P

F32 = jnp.float32
BF = jnp.bfloat16
MESH = pl.DeviceIdType.MESH
GELU_A = 0.7978845608028654
GELU_B = 0.044715

(
    KK,
    KKF,
    VV,
    VVF,
    RS1,
    AGC,
    RS2,
    RS3,
    AGD,
    AGY,
    RKV,
    RU,
    AGU,
    FWU,
    RD,
    AGW,
    FWW,
    RB,
    AGB,
    FWB,
    RC,
    AGCC,
    FWC,
    RS4,
    RS5,
    AGG,
    AGV,
    NSEM,
) = range(28)


def nn(a, b):
    return lax.dot_general(a, b, (((1,), (0,)), ((), ())), preferred_element_type=F32)


def nt(a, b):
    return lax.dot_general(a, b, (((1,), (1,)), ((), ())), preferred_element_type=F32)


def tn(a, b):
    return lax.dot_general(a, b, (((0,), (0,)), ((), ())), preferred_element_type=F32)


def normalize(rows):
    centered = rows - jnp.mean(rows, -1, keepdims=True)
    rstd = lax.rsqrt(jnp.mean(centered * centered, -1, keepdims=True) + 1e-05)
    return centered * rstd, rstd


def norm_back(grad, gain, xhat, rstd):
    gx = grad * gain
    return rstd * (
        gx - jnp.mean(gx, -1, keepdims=True) - xhat * jnp.mean(gx * xhat, -1, keepdims=True)
    )


def layer(
    order_hbm,
    seg_hbm,
    x_hbm,
    g_hbm,
    ln1g_hbm,
    ln1b_hbm,
    bout_hbm,
    ln2g_hbm,
    ln2b_hbm,
    bdown_hbm,
    bup_hbm,
    bqv_hbm,
    wqkv_hbm,
    wout_hbm,
    wup_hbm,
    wdn_hbm,
    y_out,
    gin_out,
    ou_out,
    od_out,
    ob_out,
    oc_out,
    vec_out,
    ctx_out,
    order_ref,
    seg_ref,
    x_ref,
    g_ref,
    ln1g_ref,
    ln1b_ref,
    bout_ref,
    ln2g_ref,
    ln2b_ref,
    bdown_ref,
    bup_ref,
    bqv_ref,
    wqkv,
    wout,
    wup,
    wdn,
    load_sem,
    xhat_all,
    normed,
    k_all,
    v_all,
    q2,
    scores,
    acc,
    attn_t,
    attn_low,
    rs1s,
    rs1r,
    c_all,
    dm,
    rs2s,
    rs2r,
    rs3s,
    rs3r,
    dh_all,
    y_all,
    dkv,
    pkv,
    rkv,
    gu,
    pu,
    ru,
    ou,
    gd,
    pd,
    rd,
    od,
    gb,
    pb,
    rb,
    ob,
    gc,
    pc,
    rc,
    oc,
    rs4s,
    rs4r,
    g_all,
    vs,
    vr,
    vall,
    cvs,
    cvr,
    ss,
    rs,
    cs_s,
    cs_r,
):
    ctx = lax.axis_index("ctx")
    wa = lax.axis_index("wa")
    core = lax.rem(ctx, 2)
    chip = lax.div(ctx, 2)
    other = 1 - core
    slot = core * 8 + chip
    partner = chip * 2 + other

    def to_wa(src, dst, kind, d):
        return pltpu.make_async_remote_copy(
            src_ref=src,
            dst_ref=dst,
            send_sem=ss.at[kind, d],
            recv_sem=rs.at[kind, d],
            device_id={"wa": lax.rem(wa + d, 8)},
            device_id_type=MESH,
        )

    def to_chip(src, dst, kind, d):
        return pltpu.make_async_remote_copy(
            src_ref=src,
            dst_ref=dst,
            send_sem=ss.at[kind, d],
            recv_sem=rs.at[kind, d],
            device_id={"ctx": lax.rem(chip + d, 8) * 2 + core},
            device_id_type=MESH,
        )

    def to_partner(src, dst, kind, d):
        return pltpu.make_async_remote_copy(
            src_ref=src,
            dst_ref=dst,
            send_sem=ss.at[kind, d],
            recv_sem=rs.at[kind, d],
            device_id={"ctx": partner},
            device_id_type=MESH,
        )

    sends = []
    arrivals = {}

    def each(low, high, step):
        @pl.loop(low, high)
        def _(d):
            step(d)

    loads = [
        pltpu.make_async_copy(
            wqkv_hbm.at[i], wqkv.at[:, pl.ds(128 * i, 128)], load_sem.at[i]
        )
        for i in range(3)
    ] + [
        pltpu.make_async_copy(wdn_hbm, wdn, load_sem.at[3]),
        pltpu.make_async_copy(wout_hbm, wout, load_sem.at[4]),
        pltpu.make_async_copy(wup_hbm, wup, load_sem.at[5]),
        pltpu.make_async_copy(x_hbm, x_ref, load_sem.at[6]),
        pltpu.make_async_copy(g_hbm, g_ref, load_sem.at[7]),
    ]
    small = [
        pltpu.make_async_copy(src, dst, load_sem.at[8 + i])
        for i, (src, dst) in enumerate(
            (
                (ln1g_hbm, ln1g_ref),
                (ln1b_hbm, ln1b_ref),
                (bqv_hbm, bqv_ref),
                (order_hbm, order_ref),
                (seg_hbm, seg_ref),
                (bout_hbm, bout_ref),
                (ln2g_hbm, ln2g_ref),
                (ln2b_hbm, ln2b_ref),
                (bdown_hbm, bdown_ref),
                (bup_hbm, bup_ref),
            )
        )
    ]
    loads[6].start()
    for load in small:
        load.start()
    for i in (1, 2, 0, 7, 3, 4, 5):
        loads[i].start()

    def combine(buf, kept, index):
        return pltpu.make_async_remote_copy(
            src_ref=buf.at[pl.ds(pl.multiple_of(other * 8, 8), 8)],
            dst_ref=kept,
            send_sem=cs_s.at[index],
            recv_sem=cs_r.at[index],
            device_id={"ctx": partner},
            device_id_type=MESH,
        )

    def combine_start(buf, kept, index):
        combine(buf, kept, index).start()
        sends.append(lambda: combine(buf, kept, index).wait_send())
        arrivals[100 + index] = lambda: combined(buf, kept, index)

    def combined(buf, kept, index):
        arrivals.pop(100 + index)
        combine(buf, kept, index).wait_recv()

        @pl.loop(0, 8)
        def _(j):
            buf[core * 8 + j] = (buf[core * 8 + j].astype(F32) + kept[j].astype(F32)).astype(BF)

    def scatter_start(buf, recv, kind):
        sends.append(
            lambda: each(
                1, 8, lambda d: to_chip(buf.at[slot], buf.at[slot], kind, d).wait_send()
            )
        )
        arrivals[kind] = lambda: scatter_end(buf, recv, kind)
        each(
            1,
            8,
            lambda d: to_chip(
                buf.at[core * 8 + lax.rem(chip + d, 8)], recv.at[d], kind, d
            ).start(),
        )

    def scatter_end(buf, recv, kind):
        arrivals.pop(kind)
        each(
            1,
            8,
            lambda d: to_chip(
                buf.at[core * 8 + lax.rem(chip + d, 8)], recv.at[d], kind, d
            ).wait_recv(),
        )
        whole = buf[slot].astype(F32)
        for d in range(1, 8):
            whole = whole + recv[d].astype(F32)
        return whole.astype(BF)

    def spread_start(buf, kind, forward):
        sends.append(lambda: spread_sent(buf, kind, forward))
        arrivals[kind] = lambda: (
            spread_pass(buf, kind, forward),
            spread_end(buf, kind, forward),
        )
        to_partner(buf.at[slot], buf.at[slot], kind, 0).start()
        each(1, 8, lambda d: to_chip(buf.at[slot], buf.at[slot], kind, d).start())

    def spread_sent(buf, kind, forward):
        to_partner(buf.at[slot], buf.at[slot], kind, 0).wait_send()

        def sent(d):
            to_chip(buf.at[slot], buf.at[slot], kind, d).wait_send()
            to_partner(buf.at[slot], buf.at[slot], forward, d).wait_send()

        each(1, 8, sent)

    def spread_pass(buf, kind, forward):
        arrivals[kind] = lambda: spread_end(buf, kind, forward)

        def step(d):
            s = core * 8 + lax.rem(chip + 8 - d, 8)
            to_chip(buf.at[slot], buf.at[s], kind, d).wait_recv()
            to_partner(buf.at[s], buf.at[s], forward, d).start()

        each(1, 8, step)

    def spread_end(buf, kind, forward):
        arrivals.pop(kind)
        s = other * 8 + chip
        to_partner(buf.at[s], buf.at[s], kind, 0).wait_recv()

        def step(d):
            t = other * 8 + lax.rem(chip + 8 - d, 8)
            to_partner(buf.at[t], buf.at[t], forward, d).wait_recv()

        each(1, 8, step)

    def reduce_start(part, send, recv, kind):
        send[...] = part.astype(BF).reshape(8, 16, 1024)
        each(1, 8, lambda d: to_wa(send.at[lax.rem(wa + d, 8)], recv.at[d], kind, d).start())
        sends.append(lambda: wa_sent(send, kind))
        arrivals[kind] = lambda: reduce_end(send, recv, kind)

    def reduce_end(send, recv, kind):
        arrivals.pop(kind)
        each(1, 8, lambda d: to_wa(send.at[lax.rem(wa + d, 8)], recv.at[d], kind, d).wait_recv())
        whole = send[wa].astype(F32)
        for d in range(1, 8):
            whole = whole + recv[d].astype(F32)
        return whole

    def gather_start(buf, kind):
        each(1, 8, lambda d: to_wa(buf.at[wa], buf.at[wa], kind, d).start())
        sends.append(lambda: wa_sent(buf, kind))
        arrivals[kind] = lambda: gather_end(buf, kind)

    def wa_sent(buf, kind):
        each(1, 8, lambda d: to_wa(buf.at[wa], buf.at[wa], kind, d).wait_send())

    def gather_end(buf, kind):
        arrivals.pop(kind)
        each(
            1,
            8,
            lambda d: to_wa(buf.at[wa], buf.at[lax.rem(wa + 8 - d, 8)], kind, d).wait_recv(),
        )

    barrier = pltpu.get_barrier_semaphore()
    each(
        1,
        16,
        lambda d: pl.semaphore_signal(
            barrier, inc=1, device_id={"ctx": lax.rem(ctx + d, 16)}, device_id_type=MESH
        ),
    )
    each(
        1,
        8,
        lambda d: pl.semaphore_signal(
            barrier, inc=1, device_id={"wa": lax.rem(wa + d, 8)}, device_id_type=MESH
        ),
    )

    def vector(ref):
        rows = ref[...].astype(F32)
        return jnp.concatenate([rows[j : j + 1, :] for j in range(rows.shape[0])], axis=1)

    loads[6].wait()
    xhat, _ = normalize(x_ref[...].astype(F32))
    xhat_all[...] = xhat
    for load in small:
        load.wait()
    ln1_gain = vector(ln1g_ref)
    ln1_bias = vector(ln1b_ref)
    b_qv = bqv_ref[...].astype(F32)
    normed[...] = (xhat * ln1_gain + ln1_bias).astype(BF)
    for i in range(1, 3):
        loads[i].wait()
    proj = nn(normed[...], wqkv[:, 128:384])
    k_all[slot] = proj[:, 0:128].astype(BF)
    v_all[slot] = (proj[:, 128:256] + b_qv[1:2, :]).astype(BF)
    pl.semaphore_wait(barrier, 22)

    spread_start(k_all, KK, KKF)
    spread_start(v_all, VV, VVF)

    loads[0].wait()
    q_low = (nn(normed[...], wqkv[:, 0:128]) + b_qv[0:1, :]).astype(BF) * jnp.asarray(0.125, BF)
    lane = lax.broadcasted_iota(jnp.int32, (128, 128), 1)
    zero = jnp.zeros((128, 128), BF)
    q2[0:128, :] = jnp.where(lane < 64, q_low, zero)
    q2[128:256, :] = jnp.where(lane >= 64, q_low, zero)

    lanes = lax.broadcasted_iota(jnp.int32, (1, 256), 1)
    lanes = jnp.where(lanes >= 128, lanes - 128, lanes)
    q_pos = jnp.where(
        lanes < 64, lanes + 64 * order_ref[2 * ctx], lanes - 64 + 64 * order_ref[2 * ctx + 1]
    )
    seg = seg_ref[...]
    one = jnp.ones(seg.shape, F32)
    none = jnp.zeros(seg.shape, F32)

    def count(test):
        part = jnp.sum(jnp.where(test, one, none), axis=0, keepdims=True)
        return jnp.sum(part, axis=1, keepdims=True)

    first_end = count(seg < 1)
    second_end = count(seg < 2)
    q_float = q_pos.astype(F32)
    q_first = jnp.where(
        q_float >= second_end,
        second_end,
        jnp.where(q_float >= first_end, first_end, jnp.zeros_like(q_float)),
    ).astype(jnp.int32)
    row = lax.broadcasted_iota(jnp.int32, (128, 256), 0)

    def score(s, top):
        keys = k_all[s]
        owner = 2 * lax.rem(s, 8) + lax.div(s, 8)
        k_pos = jnp.where(
            row < 64, row + 64 * order_ref[2 * owner], row - 64 + 64 * order_ref[2 * owner + 1]
        )
        allowed = (k_pos <= q_pos) & (k_pos >= q_first)
        masked = jnp.where(allowed, nt(keys, q2[...]), -1e30)
        scores[s] = masked
        return jnp.maximum(top, jnp.max(masked.reshape(16, 8, 256), axis=0))

    top = score(slot, jnp.full((8, 256), -1e30, F32))
    loads[7].wait()
    loads[3].wait()
    dm[...] = nt(g_ref[...], wdn[...])
    b_out = vector(bout_ref)
    ln2_gain = vector(ln2g_ref)
    ln2_bias = vector(ln2b_ref)
    b_down = vector(bdown_ref)
    b_up = vector(bup_ref)

    def near(d, top):
        s = core * 8 + lax.rem(chip + 8 - d, 8)
        to_chip(k_all.at[slot], k_all.at[s], KK, d).wait_recv()
        to_partner(k_all.at[s], k_all.at[s], KKF, d).start()
        return score(s, top)

    top = lax.fori_loop(1, 8, near, top)
    to_partner(k_all.at[slot], k_all.at[other * 8 + chip], KK, 0).wait_recv()
    top = score(other * 8 + chip, top)
    spread_pass(v_all, VV, VVF)

    def far(d, top):
        s = other * 8 + lax.rem(chip + 8 - d, 8)
        to_partner(k_all.at[s], k_all.at[s], KKF, d).wait_recv()
        return score(s, top)

    top = lax.fori_loop(1, 8, far, top)
    arrivals.pop(KK)
    spread_end(v_all, VV, VVF)
    top = jnp.max(top, axis=0, keepdims=True)
    acc[...] = jnp.zeros_like(acc)

    def mix(s, total):
        p = jnp.exp(scores[s] - top)
        acc[...] += tn(v_all[s], p.astype(BF))
        return total + jnp.sum(p.reshape(16, 8, 256), axis=0)

    total = lax.fori_loop(0, 16, mix, jnp.zeros((8, 256), F32))
    total = jnp.sum(total, axis=0, keepdims=True)
    lse = top + jnp.log(total)
    half = lax.broadcasted_iota(jnp.int32, (128, 128), 0) < 64

    def diagonal(both):
        return jnp.where(half, both[:, 0:128], both[:, 128:256])

    raw_t = diagonal(acc[...] / total)
    attn_t[...] = raw_t
    attn_low[...] = raw_t.T.astype(BF)

    loads[4].wait()
    reduce_start(nn(attn_low[...], wout[...]), rs1s, rs1r, RS1)
    mine = pl.ds(pl.multiple_of(wa * 16, 16), 16)
    x_mine = x_ref[mine, :].astype(F32)
    g_mine = g_ref[mine, :].astype(F32)
    hidden = x_mine + reduce_end(rs1s, rs1r, RS1) + b_out
    hat_two, rstd_two = normalize(hidden)
    c_all[wa] = (hat_two * ln2_gain + ln2_bias).astype(BF)
    gather_start(c_all, AGC)
    loads[5].wait()
    gather_end(c_all, AGC)

    c_low = c_all[...].reshape(128, 1024)
    up = nn(c_low, wup[...]) + b_up
    tanh = jnp.tanh(GELU_A * (up + GELU_B * up * up * up))
    slope = 0.5 * (1.0 + tanh) + 0.5 * up * (1.0 - tanh * tanh) * GELU_A * (
        1.0 + 3.0 * GELU_B * up * up
    )
    du = (dm[...] * slope).astype(BF)
    act = (0.5 * up * (1.0 + tanh)).astype(BF)
    reduce_start(nt(du, wup[...]), rs2s, rs2r, RS2)
    gu[...] = tn(c_low, du).astype(BF).reshape(16, 64, 512)
    combine_start(gu, pu, 0)
    down = tn(act, g_ref[...]).astype(BF)
    gd[:, 0:32, :] = down[:, 0:512].reshape(16, 32, 512)
    gd[:, 32:64, :] = down[:, 512:1024].reshape(16, 32, 512)
    combine_start(gd, pd, 1)

    def vec_row(r, value):
        for j in range(8):
            vs[j, r : r + 1, :] = value[:, 128 * j : 128 * j + 128]

    def rows_sum(value):
        return jnp.sum(value, axis=0, keepdims=True)

    sum_up = rows_sum(du.astype(F32))
    for j in range(4):
        cvs[8 + j : 9 + j, :] = sum_up[:, 128 * j : 128 * j + 128]

    dc = reduce_end(rs2s, rs2r, RS2)
    d_hidden = g_mine + norm_back(dc, ln2_gain, hat_two, rstd_two)
    dh_all[wa] = d_hidden.astype(BF)
    gather_start(dh_all, AGD)
    combined(gu, pu, 0)
    scatter_start(gu, ru, RU)
    combined(gd, pd, 1)
    scatter_start(gd, rd, RD)
    vec_row(0, rows_sum(dc * hat_two))
    vec_row(1, rows_sum(dc))
    vec_row(2, rows_sum(d_hidden))
    vec_row(3, rows_sum(g_mine))
    gather_end(dh_all, AGD)

    dh_low = dh_all[...].reshape(128, 1024)
    d_attn = nt(dh_low, wout[...]).astype(BF)
    dot_t = d_attn.astype(F32).T * attn_t[...]
    delta = jnp.concatenate(
        [
            jnp.sum(dot_t[0:64], axis=0, keepdims=True),
            jnp.sum(dot_t[64:128], axis=0, keepdims=True),
        ],
        axis=1,
    )
    do2 = jnp.concatenate(
        [jnp.where(lane < 64, d_attn, zero), jnp.where(lane >= 64, d_attn, zero)], axis=0
    )
    acc[...] = jnp.zeros_like(acc)

    def back(s):
        p = jnp.exp(scores[s] - lse)
        ds = (p * (nt(v_all[s], do2) - delta)).astype(BF)
        acc[...] += tn(k_all[s], ds)
        dkv[s, :, 0:128] = nn(ds, q2[...]).astype(BF)
        dkv[s, :, 128:256] = nn(p.astype(BF), do2).astype(BF)

    each(0, 8, lambda j: back(other * 8 + j))
    combine_start(dkv, pkv, 2)
    each(0, 8, lambda j: back(core * 8 + j))
    combined(dkv, pkv, 2)
    scatter_start(dkv, rkv, RKV)

    dq = (diagonal(acc[...]) * 0.125).T.astype(BF)
    gb[:, 64:128, :] = tn(normed[...], dq).astype(BF).reshape(16, 64, 128)
    d_out = tn(attn_low[...], dh_low).astype(BF)
    for s in range(16):
        gb[s, 0:64, :] = d_out[64 * (s % 2) : 64 * (s % 2) + 64, 128 * (s // 2) : 128 * (s // 2) + 128]
    combine_start(gb, pb, 3)
    reduce_start(nn(act, wdn[...]), rs3s, rs3r, RS3)
    ou[slot] = scatter_end(gu, ru, RU)
    od[slot] = scatter_end(gd, rd, RD)

    dkv_mine = scatter_end(dkv, rkv, RKV)
    d_qkv = jnp.concatenate([dq, dkv_mine], axis=1)
    da = nt(d_qkv, wqkv[...])
    reduce_start(da, rs4s, rs4r, RS4)
    spread_start(ou, AGU, FWU)
    both = tn(normed[...], dkv_mine).astype(BF)
    gc[:, 0:64, :] = both[:, 0:128].reshape(16, 64, 128)
    gc[:, 64:128, :] = both[:, 128:256].reshape(16, 64, 128)
    combine_start(gc, pc, 4)
    combined(gb, pb, 3)
    scatter_start(gb, rb, RB)
    vec_row(4, rows_sum(da * xhat_all[...]))
    vec_row(5, rows_sum(da))
    for j in range(8):
        vs[j, 6:8, :] = jnp.zeros((2, 128), F32)
    each(1, 8, lambda d: to_wa(vs.at[lax.rem(wa + d, 8)], vr.at[d], RS5, d).start())
    sends.append(lambda: wa_sent(vs, RS5))
    cvs[12:13, :] = rows_sum(dq.astype(F32))
    cvs[13:14, :] = rows_sum(dkv_mine[:, 128:256].astype(F32))
    cvs[14:16, :] = jnp.zeros((2, 128), F32)
    combined(gc, pc, 4)
    scatter_start(gc, rc, RC)
    spread_start(od, AGW, FWW)

    hat_one, rstd_one = normalize(x_mine)
    d_first = reduce_end(rs4s, rs4r, RS4)
    g_all[wa] = (d_hidden + norm_back(d_first, ln1_gain, hat_one, rstd_one)).astype(BF)
    gather_start(g_all, AGG)

    each(1, 8, lambda d: to_wa(vs.at[lax.rem(wa + d, 8)], vr.at[d], RS5, d).wait_recv())
    vec_sum = vs[wa]
    for d in range(1, 8):
        vec_sum = vec_sum + vr[d]
    cvs[0:8, :] = vec_sum
    cvr[ctx] = cvs[...]

    def to_ctx(dst, d):
        return pltpu.make_async_remote_copy(
            src_ref=cvs,
            dst_ref=cvr.at[dst],
            send_sem=cs_s.at[5 + d],
            recv_sem=cs_r.at[5 + d],
            device_id={"ctx": lax.rem(ctx + d, 16)},
            device_id_type=MESH,
        )

    each(1, 16, lambda d: to_ctx(ctx, d).start())
    sends.append(lambda: each(1, 16, lambda d: to_ctx(ctx, d).wait_send()))
    spread_pass(ou, AGU, FWU)
    ob[slot] = scatter_end(gb, rb, RB)
    spread_start(ob, AGB, FWB)
    oc[slot] = scatter_end(gc, rc, RC)
    spread_start(oc, AGCC, FWC)
    each(1, 16, lambda d: to_ctx(lax.rem(ctx + 16 - d, 16), d).wait_recv())
    ctx_sum = cvr[0]
    for i in range(1, 16):
        ctx_sum = ctx_sum + cvr[i]
    ctx_out[...] = ctx_sum[8:16, :]
    vall[wa] = ctx_sum[0:8, :]
    gather_start(vall, AGV)
    spread_pass(od, AGW, FWW)
    y_all[wa] = (hidden + reduce_end(rs3s, rs3r, RS3) + b_down).astype(BF)
    gather_start(y_all, AGY)
    spread_pass(ob, AGB, FWB)
    spread_pass(oc, AGCC, FWC)

    spread_end(ou, AGU, FWU)
    ou_out[...] = ou[...]
    spread_end(od, AGW, FWW)
    od_out[...] = od[...]
    gather_end(y_all, AGY)
    y_out[...] = y_all[...].reshape(128, 1024)
    gather_end(g_all, AGG)
    gin_out[...] = g_all[...].reshape(128, 1024)
    spread_end(ob, AGB, FWB)
    ob_out[...] = ob[...]
    spread_end(oc, AGCC, FWC)
    oc_out[...] = oc[...]
    gather_end(vall, AGV)
    vec_out[...] = vall[...]

    for sent in sends:
        sent()


def finish(
    y_ref,
    gin_ref,
    ou_ref,
    od_ref,
    ob_ref,
    oc_ref,
    vec_ref,
    ctx_ref,
    y_out,
    gin_out,
    ln1g_out,
    ln1b_out,
    gqkv_out,
    bqv_out,
    gwo_out,
    bout_out,
    ln2g_out,
    ln2b_out,
    gup_out,
    bup_out,
    gdn_out,
    bdown_out,
    gin,
    gqkv,
    gwo,
    gup,
    gdn,
    sems,
):
    copies = []

    def leave(src, dst):
        copies.append(pltpu.make_async_copy(src, dst, sems.at[len(copies)]))
        copies[-1].start()

    leave(y_ref, y_out)
    for i in range(4):
        rows = pl.ds(256 * i, 256)
        gup[rows, :] = ou_ref[4 * i : 4 * i + 4].astype(F32).reshape(256, 512)
        leave(gup.at[rows], gup_out.at[rows])
    for i in range(4):
        rows = pl.ds(128 * i, 128)
        part = od_ref[4 * i : 4 * i + 4].astype(F32)
        gdn[rows, 0:512] = part[:, 0:32].reshape(128, 512)
        gdn[rows, 512:1024] = part[:, 32:64].reshape(128, 512)
        leave(gdn.at[rows], gdn_out.at[rows])
    gin[...] = gin_ref[...].astype(F32)
    leave(gin, gin_out)
    for s in range(16):
        gwo[64 * (s % 2) : 64 * (s % 2) + 64, 128 * (s // 2) : 128 * (s // 2) + 128] = ob_ref[
            s, 0:64, :
        ].astype(F32)
    leave(gwo, gwo_out)
    gqkv[0] = ob_ref[:, 64:128, :].astype(F32).reshape(1024, 128)
    leave(gqkv.at[0], gqkv_out.at[0])
    gqkv[1] = oc_ref[:, 0:64, :].astype(F32).reshape(1024, 128)
    leave(gqkv.at[1], gqkv_out.at[1])
    gqkv[2] = oc_ref[:, 64:128, :].astype(F32).reshape(1024, 128)
    leave(gqkv.at[2], gqkv_out.at[2])
    for r, out in enumerate((ln2g_out, ln2b_out, bout_out, bdown_out, ln1g_out, ln1b_out)):
        out[...] = vec_ref[:, r, :]
    bup_out[...] = ctx_ref[0:4, :]
    bqv_out[...] = ctx_ref[4:6, :]
    for copy in copies:
        copy.wait()


def body(
    layer_input,
    block_order,
    seg_ids,
    cotangent,
    ln1_gain,
    ln1_bias,
    w_qkv,
    b_qv,
    w_out,
    b_out,
    ln2_gain,
    ln2_bias,
    w_up,
    b_up,
    w_down,
    b_down,
):
    vmem = pl.BlockSpec(memory_space=pltpu.VMEM)
    hbm = pl.BlockSpec(memory_space=pl.ANY)
    far = pl.BlockSpec(memory_space=pltpu.HBM)

    def stay(operand):
        return pltpu.with_memory_space_constraint(operand, pltpu.HBM)

    def bf(*shape):
        return pltpu.VMEM(shape, BF)

    def f32(*shape):
        return pltpu.VMEM(shape, F32)

    outs = pl.pallas_call(
        layer,
        out_shape=(
            jax.ShapeDtypeStruct((128, 1024), BF),
            jax.ShapeDtypeStruct((128, 1024), BF),
            jax.ShapeDtypeStruct((16, 64, 512), BF),
            jax.ShapeDtypeStruct((16, 64, 512), BF),
            jax.ShapeDtypeStruct((16, 128, 128), BF),
            jax.ShapeDtypeStruct((16, 128, 128), BF),
            jax.ShapeDtypeStruct((8, 8, 128), F32),
            jax.ShapeDtypeStruct((8, 128), F32),
        ),
        in_specs=[far] * 16,
        out_specs=(vmem,) * 8,
        scratch_shapes=[
            pltpu.SMEM((32,), jnp.int32),
            pltpu.VMEM((16, 128), jnp.int32),
            bf(128, 1024),
            bf(128, 1024),
            bf(8, 128),
            bf(8, 128),
            bf(8, 128),
            bf(8, 128),
            bf(8, 128),
            bf(8, 128),
            bf(4, 128),
            bf(2, 128),
            bf(1024, 384),
            bf(128, 1024),
            bf(1024, 512),
            bf(512, 1024),
            pltpu.SemaphoreType.DMA((18,)),
            f32(128, 1024),
            bf(128, 1024),
            bf(16, 128, 128),
            bf(16, 128, 128),
            bf(256, 128),
            f32(16, 128, 256),
            f32(128, 256),
            f32(128, 128),
            bf(128, 128),
            bf(8, 16, 1024),
            bf(8, 16, 1024),
            bf(8, 16, 1024),
            f32(128, 512),
            bf(8, 16, 1024),
            bf(8, 16, 1024),
            bf(8, 16, 1024),
            bf(8, 16, 1024),
            bf(8, 16, 1024),
            bf(8, 16, 1024),
            bf(16, 128, 256),
            bf(8, 128, 256),
            bf(8, 128, 256),
            bf(16, 64, 512),
            bf(8, 64, 512),
            bf(8, 64, 512),
            bf(16, 64, 512),
            bf(16, 64, 512),
            bf(8, 64, 512),
            bf(8, 64, 512),
            bf(16, 64, 512),
            bf(16, 128, 128),
            bf(8, 128, 128),
            bf(8, 128, 128),
            bf(16, 128, 128),
            bf(16, 128, 128),
            bf(8, 128, 128),
            bf(8, 128, 128),
            bf(16, 128, 128),
            bf(8, 16, 1024),
            bf(8, 16, 1024),
            bf(8, 16, 1024),
            f32(8, 8, 128),
            f32(8, 8, 128),
            f32(8, 8, 128),
            f32(16, 128),
            f32(16, 16, 128),
            pltpu.SemaphoreType.DMA((NSEM, 8)),
            pltpu.SemaphoreType.DMA((NSEM, 8)),
            pltpu.SemaphoreType.DMA((21,)),
            pltpu.SemaphoreType.DMA((21,)),
        ],
        compiler_params=pltpu.CompilerParams(
            collective_id=0, has_side_effects=True, vmem_limit_bytes=32 << 20
        ),
        name="decoder",
    )(
        stay(block_order),
        stay(seg_ids.reshape(16, 128)),
        stay(layer_input),
        stay(cotangent),
        *(
            stay(v.reshape(-1, 128))
            for v in (ln1_gain, ln1_bias, b_out, ln2_gain, ln2_bias, b_down, b_up)
        ),
        stay(b_qv),
        stay(w_qkv.transpose(1, 0, 2)),
        stay(w_out),
        stay(w_up),
        stay(w_down),
    )
    shapes = (
        ((128, 1024), BF),
        ((128, 1024), F32),
        ((8, 128), F32),
        ((8, 128), F32),
        ((3, 1024, 128), F32),
        ((2, 128), F32),
        ((128, 1024), F32),
        ((8, 128), F32),
        ((8, 128), F32),
        ((8, 128), F32),
        ((1024, 512), F32),
        ((4, 128), F32),
        ((512, 1024), F32),
        ((8, 128), F32),
    )
    large = (0, 1, 4, 6, 10, 12)
    done = list(
        pl.pallas_call(
            finish,
            out_shape=tuple(jax.ShapeDtypeStruct(*shape) for shape in shapes),
            in_specs=[vmem] * 8,
            out_specs=tuple(hbm if i in large else vmem for i in range(14)),
            scratch_shapes=[
                f32(128, 1024),
                f32(3, 1024, 128),
                f32(128, 1024),
                f32(1024, 512),
                f32(512, 1024),
                pltpu.SemaphoreType.DMA((14,)),
            ],
            compiler_params=pltpu.CompilerParams(vmem_limit_bytes=24 << 20),
            name="finish",
        )(*outs)
    )
    for i in (2, 3, 7, 8, 9, 11, 13):
        done[i] = done[i].reshape(-1)
    done[4] = done[4].transpose(1, 0, 2)
    return tuple(done)


def solution(mesh):
    placed = (
        P("ctx", None),
        P(),
        P(),
        P("ctx", None),
        P(),
        P(),
        P(None, None, "wa"),
        P(None, "wa"),
        P("wa", None),
        P(),
        P(),
        P(),
        P(None, "wa"),
        P("wa"),
        P("wa", None),
        P(),
    )
    return jax.shard_map(
        body,
        mesh=mesh,
        in_specs=placed,
        out_specs=(
            P("ctx", None),
            P("ctx", None),
            P(),
            P(),
            P(None, None, "wa"),
            P(None, "wa"),
            P("wa", None),
            P(),
            P(),
            P(),
            P(None, "wa"),
            P("wa"),
            P("wa", None),
            P(),
        ),
        check_vma=False,
    )
```

```python
import jax
import jax.numpy as jnp
from jax import lax
from jax.experimental import pallas as pl
from jax.experimental.pallas import tpu as pltpu
from jax.sharding import PartitionSpec as P

F32 = jnp.float32
BF = jnp.bfloat16
MESH = pl.DeviceIdType.MESH
GELU_A = 0.7978845608028654
GELU_B = 0.044715

(
    KK,
    KKF,
    VV,
    VVF,
    RS1,
    AGC,
    RS2,
    RS3,
    AGD,
    AGY,
    RKV,
    RUX,
    RUY,
    AGU,
    FWU,
    RDY,
    RDX,
    AGW,
    FWW,
    RB,
    AGB,
    FWB,
    RC,
    AGCC,
    FWC,
    RS4,
    RS5,
    AGG,
    AGV,
    NSEM,
) = range(30)


def nn(a, b):
    return lax.dot_general(a, b, (((1,), (0,)), ((), ())), preferred_element_type=F32)


def nt(a, b):
    return lax.dot_general(a, b, (((1,), (1,)), ((), ())), preferred_element_type=F32)


def tn(a, b):
    return lax.dot_general(a, b, (((0,), (0,)), ((), ())), preferred_element_type=F32)


def normalize(rows):
    centered = rows - jnp.mean(rows, -1, keepdims=True)
    rstd = lax.rsqrt(jnp.mean(centered * centered, -1, keepdims=True) + 1e-05)
    return centered * rstd, rstd


def norm_back(grad, gain, xhat, rstd):
    gx = grad * gain
    return rstd * (
        gx - jnp.mean(gx, -1, keepdims=True) - xhat * jnp.mean(gx * xhat, -1, keepdims=True)
    )


def layer(
    order_hbm,
    seg_hbm,
    x_hbm,
    g_hbm,
    ln1g_hbm,
    ln1b_hbm,
    bout_hbm,
    ln2g_hbm,
    ln2b_hbm,
    bdown_hbm,
    bup_hbm,
    bqv_hbm,
    wqkv_hbm,
    wout_hbm,
    wup_hbm,
    wdn_hbm,
    y_out,
    gin_out,
    ou_out,
    od_out,
    ob_out,
    oc_out,
    vec_out,
    ctx_out,
    order_ref,
    seg_ref,
    x_ref,
    g_ref,
    ln1g_ref,
    ln1b_ref,
    bout_ref,
    ln2g_ref,
    ln2b_ref,
    bdown_ref,
    bup_ref,
    bqv_ref,
    wqkv,
    wout,
    wup,
    wdn,
    load_sem,
    xhat_all,
    normed,
    k_all,
    v_all,
    q2,
    scores,
    acc,
    attn_t,
    attn_low,
    rs1s,
    rs1r,
    c_all,
    dm,
    rs2s,
    rs2r,
    rs3s,
    rs3r,
    dh_all,
    y_all,
    dkv,
    pkv,
    rkv,
    gu,
    pu,
    rux,
    tu,
    ruy,
    ou,
    gd,
    pd,
    rdy,
    td,
    rdx,
    od,
    gb,
    pb,
    rb,
    ob,
    gc,
    pc,
    rc,
    oc,
    rs4s,
    rs4r,
    g_all,
    vs,
    vr,
    vall,
    cvs,
    cvr,
    ss,
    rs,
    cs_s,
    cs_r,
):
    ctx = lax.axis_index("ctx")
    wa = lax.axis_index("wa")
    core = lax.rem(ctx, 2)
    chip = lax.div(ctx, 2)
    other = 1 - core
    row_at = lax.div(chip, 4)
    col_at = lax.rem(chip, 4)
    row_far = 1 - row_at
    slot = core * 8 + chip
    partner = chip * 2 + other

    def to_wa(src, dst, kind, d):
        return pltpu.make_async_remote_copy(
            src_ref=src,
            dst_ref=dst,
            send_sem=ss.at[kind, d],
            recv_sem=rs.at[kind, d],
            device_id={"wa": lax.rem(wa + d, 8)},
            device_id_type=MESH,
        )

    def to_chip(src, dst, kind, d):
        return pltpu.make_async_remote_copy(
            src_ref=src,
            dst_ref=dst,
            send_sem=ss.at[kind, d],
            recv_sem=rs.at[kind, d],
            device_id={"ctx": lax.rem(chip + d, 8) * 2 + core},
            device_id_type=MESH,
        )

    def to_partner(src, dst, kind, d):
        return pltpu.make_async_remote_copy(
            src_ref=src,
            dst_ref=dst,
            send_sem=ss.at[kind, d],
            recv_sem=rs.at[kind, d],
            device_id={"ctx": partner},
            device_id_type=MESH,
        )

    sends = []
    arrivals = {}

    def each(low, high, step):
        @pl.loop(low, high)
        def _(d):
            step(d)

    loads = [
        pltpu.make_async_copy(
            wqkv_hbm.at[i], wqkv.at[:, pl.ds(128 * i, 128)], load_sem.at[i]
        )
        for i in range(3)
    ] + [
        pltpu.make_async_copy(wdn_hbm, wdn, load_sem.at[3]),
        pltpu.make_async_copy(wout_hbm, wout, load_sem.at[4]),
        pltpu.make_async_copy(wup_hbm, wup, load_sem.at[5]),
        pltpu.make_async_copy(x_hbm, x_ref, load_sem.at[6]),
        pltpu.make_async_copy(g_hbm, g_ref, load_sem.at[7]),
    ]
    small = [
        pltpu.make_async_copy(src, dst, load_sem.at[8 + i])
        for i, (src, dst) in enumerate(
            (
                (ln1g_hbm, ln1g_ref),
                (ln1b_hbm, ln1b_ref),
                (bqv_hbm, bqv_ref),
                (order_hbm, order_ref),
                (seg_hbm, seg_ref),
                (bout_hbm, bout_ref),
                (ln2g_hbm, ln2g_ref),
                (ln2b_hbm, ln2b_ref),
                (bdown_hbm, bdown_ref),
                (bup_hbm, bup_ref),
            )
        )
    ]
    loads[6].start()
    for load in small:
        load.start()
    for i in (1, 2, 0, 7, 3, 4, 5):
        loads[i].start()

    def combine(buf, kept, index):
        return pltpu.make_async_remote_copy(
            src_ref=buf.at[pl.ds(pl.multiple_of(other * 8, 8), 8)],
            dst_ref=kept,
            send_sem=cs_s.at[index],
            recv_sem=cs_r.at[index],
            device_id={"ctx": partner},
            device_id_type=MESH,
        )

    def combine_start(buf, kept, index):
        combine(buf, kept, index).start()
        sends.append(lambda: combine(buf, kept, index).wait_send())
        arrivals[100 + index] = lambda: combined(buf, kept, index)

    def combined(buf, kept, index):
        arrivals.pop(100 + index)
        combine(buf, kept, index).wait_recv()

        @pl.loop(0, 8)
        def _(j):
            buf[core * 8 + j] = (buf[core * 8 + j].astype(F32) + kept[j].astype(F32)).astype(BF)

    def scatter_start(buf, recv, kind):
        sends.append(
            lambda: each(
                1, 8, lambda d: to_chip(buf.at[slot], buf.at[slot], kind, d).wait_send()
            )
        )
        arrivals[kind] = lambda: scatter_end(buf, recv, kind)
        each(
            1,
            8,
            lambda d: to_chip(
                buf.at[core * 8 + lax.rem(chip + d, 8)], recv.at[d], kind, d
            ).start(),
        )

    def scatter_end(buf, recv, kind):
        arrivals.pop(kind)
        each(
            1,
            8,
            lambda d: to_chip(
                buf.at[core * 8 + lax.rem(chip + d, 8)], recv.at[d], kind, d
            ).wait_recv(),
        )
        whole = buf[slot].astype(F32)
        for d in range(1, 8):
            whole = whole + recv[d].astype(F32)
        return whole.astype(BF)

    def spread_start(buf, kind, forward):
        sends.append(lambda: spread_sent(buf, kind, forward))
        arrivals[kind] = lambda: (
            spread_pass(buf, kind, forward),
            spread_end(buf, kind, forward),
        )
        to_partner(buf.at[slot], buf.at[slot], kind, 0).start()
        each(1, 8, lambda d: to_chip(buf.at[slot], buf.at[slot], kind, d).start())

    def spread_sent(buf, kind, forward):
        to_partner(buf.at[slot], buf.at[slot], kind, 0).wait_send()

        def sent(d):
            to_chip(buf.at[slot], buf.at[slot], kind, d).wait_send()
            to_partner(buf.at[slot], buf.at[slot], forward, d).wait_send()

        each(1, 8, sent)

    def spread_pass(buf, kind, forward):
        arrivals[kind] = lambda: spread_end(buf, kind, forward)

        def step(d):
            s = core * 8 + lax.rem(chip + 8 - d, 8)
            to_chip(buf.at[slot], buf.at[s], kind, d).wait_recv()
            to_partner(buf.at[s], buf.at[s], forward, d).start()

        each(1, 8, step)

    def spread_end(buf, kind, forward):
        arrivals.pop(kind)
        s = other * 8 + chip
        to_partner(buf.at[s], buf.at[s], kind, 0).wait_recv()

        def step(d):
            t = other * 8 + lax.rem(chip + 8 - d, 8)
            to_partner(buf.at[t], buf.at[t], forward, d).wait_recv()

        each(1, 8, step)

    def reduce_start(part, send, recv, kind):
        send[...] = part.astype(BF).reshape(8, 16, 1024)
        each(1, 8, lambda d: to_wa(send.at[lax.rem(wa + d, 8)], recv.at[d], kind, d).start())
        sends.append(lambda: wa_sent(send, kind))
        arrivals[kind] = lambda: reduce_end(send, recv, kind)

    def reduce_end(send, recv, kind):
        arrivals.pop(kind)
        each(1, 8, lambda d: to_wa(send.at[lax.rem(wa + d, 8)], recv.at[d], kind, d).wait_recv())
        whole = send[wa].astype(F32)
        for d in range(1, 8):
            whole = whole + recv[d].astype(F32)
        return whole

    def gather_start(buf, kind):
        each(1, 8, lambda d: to_wa(buf.at[wa], buf.at[wa], kind, d).start())
        sends.append(lambda: wa_sent(buf, kind))
        arrivals[kind] = lambda: gather_end(buf, kind)

    def wa_sent(buf, kind):
        each(1, 8, lambda d: to_wa(buf.at[wa], buf.at[wa], kind, d).wait_send())

    def gather_end(buf, kind):
        arrivals.pop(kind)
        each(
            1,
            8,
            lambda d: to_wa(buf.at[wa], buf.at[lax.rem(wa + 8 - d, 8)], kind, d).wait_recv(),
        )

    def to_x(src, dst, kind, at, d):
        return pltpu.make_async_remote_copy(
            src_ref=src,
            dst_ref=dst,
            send_sem=ss.at[kind, at],
            recv_sem=rs.at[kind, at],
            device_id={"ctx": (row_at * 4 + lax.rem(col_at + d, 4)) * 2 + core},
            device_id_type=MESH,
        )

    def to_y(src, dst, kind, at):
        return pltpu.make_async_remote_copy(
            src_ref=src,
            dst_ref=dst,
            send_sem=ss.at[kind, at],
            recv_sem=rs.at[kind, at],
            device_id={"ctx": lax.rem(chip + 4, 8) * 2 + core},
            device_id_type=MESH,
        )

    def pair(buf, kept, index):
        return pltpu.make_async_remote_copy(
            src_ref=buf.at[other],
            dst_ref=kept,
            send_sem=cs_s.at[index],
            recv_sem=cs_r.at[index],
            device_id={"ctx": partner},
            device_id_type=MESH,
        )

    def pair_start(buf, kept, index):
        pair(buf, kept, index).start()
        sends.append(lambda: pair(buf, kept, index).wait_send())
        arrivals[100 + index] = lambda: pair_end(buf, kept, index)

    def pair_end(buf, kept, index):
        arrivals.pop(100 + index)
        pair(buf, kept, index).wait_recv()

        @pl.loop(0, 8)
        def _(j):
            at = (lax.div(j, 4), lax.rem(j, 4))
            buf[(core, *at)] = (buf[(core, *at)].astype(F32) + kept[at].astype(F32)).astype(BF)

    def up_x(d):
        return to_x(gu.at[core, :, lax.rem(col_at + d, 4)], rux.at[d], RUX, d, d)

    def up_start():
        each(1, 4, lambda d: up_x(d).start())
        sends.append(lambda: each(1, 4, lambda d: up_x(d).wait_send()))
        arrivals[RUX] = up_mid

    def up_mid():
        arrivals.pop(RUX)
        each(1, 4, lambda d: up_x(d).wait_recv())
        for y in range(2):
            whole = gu[core, y, col_at].astype(F32)
            for d in range(1, 4):
                whole = whole + rux[d, y].astype(F32)
            tu[y] = whole.astype(BF)
        to_y(tu.at[row_far], ruy, RUY, 0).start()
        sends.append(lambda: to_y(tu.at[row_far], ruy, RUY, 0).wait_send())
        arrivals[RUY] = up_end

    def up_end():
        arrivals.pop(RUY)
        to_y(tu.at[row_far], ruy, RUY, 0).wait_recv()
        ou[slot] = (tu[row_at].astype(F32) + ruy[...].astype(F32)).astype(BF)

    def down_y():
        return to_y(gd.at[core, row_far], rdy, RDY, 0)

    def down_x(d):
        return to_x(td.at[lax.rem(col_at + d, 4)], rdx.at[d], RDX, d, d)

    def down_start():
        down_y().start()
        sends.append(lambda: down_y().wait_send())
        arrivals[RDY] = down_mid

    def down_mid():
        arrivals.pop(RDY)
        down_y().wait_recv()
        for x in range(4):
            td[x] = (gd[core, row_at, x].astype(F32) + rdy[x].astype(F32)).astype(BF)
        each(1, 4, lambda d: down_x(d).start())
        sends.append(lambda: each(1, 4, lambda d: down_x(d).wait_send()))
        arrivals[RDX] = down_end

    def down_end():
        arrivals.pop(RDX)
        each(1, 4, lambda d: down_x(d).wait_recv())
        whole = td[col_at].astype(F32)
        for d in range(1, 4):
            whole = whole + rdx[d].astype(F32)
        od[slot] = whole.astype(BF)

    def place(side, y, d):
        return side * 8 + y * 4 + lax.rem(col_at + 4 - d, 4)

    def tree_start(buf, kind, forward, middle):
        own = buf.at[slot]
        to_y(own, own, kind, 4).start()
        each(1, 4, lambda d: to_x(own, own, kind, d, d).start())
        to_partner(own, own, kind, 0).start()

        def sent():
            each(0, 8, lambda d: to_y(own, own, kind, d).wait_send())
            each(1, 8, lambda d: to_y(own, own, forward, d).wait_send())

        sends.append(sent)
        arrivals[kind] = lambda: (
            middle(buf, kind, forward),
            tree_pass(buf, kind, forward),
            tree_end(buf, kind, forward),
        )

    def take(buf, s, kind, forward, d):
        at = buf.at[s]
        to_y(at, at, kind, d).wait_recv()
        to_partner(at, at, forward, d).start()

    def up_tree_mid(buf, kind, forward):
        s = place(core, row_far, 0)
        take(buf, s, kind, forward, 4)
        each(1, 4, lambda d: to_x(buf.at[s], buf.at[s], kind, 4 + d, d).start())
        each(1, 4, lambda d: take(buf, place(core, row_at, d), kind, forward, d))
        arrivals[kind] = lambda: (tree_pass(buf, kind, forward), tree_end(buf, kind, forward))

    def down_tree_mid(buf, kind, forward):
        def step(d):
            s = place(core, row_at, d)
            take(buf, s, kind, forward, d)
            to_y(buf.at[s], buf.at[s], kind, 4 + d).start()

        each(1, 4, step)
        take(buf, place(core, row_far, 0), kind, forward, 4)
        arrivals[kind] = lambda: (tree_pass(buf, kind, forward), tree_end(buf, kind, forward))

    def tree_pass(buf, kind, forward):
        each(1, 4, lambda d: take(buf, place(core, row_far, d), kind, forward, 4 + d))
        arrivals[kind] = lambda: tree_end(buf, kind, forward)

    def tree_end(buf, kind, forward):
        arrivals.pop(kind)

        def landed(s, sem, d):
            to_partner(buf.at[s], buf.at[s], sem, d).wait_recv()

        landed(other * 8 + chip, kind, 0)
        landed(place(other, row_far, 0), forward, 4)

        def step(d):
            landed(place(other, row_at, d), forward, d)
            landed(place(other, row_far, d), forward, 4 + d)

        each(1, 4, step)

    barrier = pltpu.get_barrier_semaphore()
    each(
        1,
        16,
        lambda d: pl.semaphore_signal(
            barrier, inc=1, device_id={"ctx": lax.rem(ctx + d, 16)}, device_id_type=MESH
        ),
    )
    each(
        1,
        8,
        lambda d: pl.semaphore_signal(
            barrier, inc=1, device_id={"wa": lax.rem(wa + d, 8)}, device_id_type=MESH
        ),
    )

    def vector(ref):
        rows = ref[...].astype(F32)
        return jnp.concatenate([rows[j : j + 1, :] for j in range(rows.shape[0])], axis=1)

    loads[6].wait()
    xhat, _ = normalize(x_ref[...].astype(F32))
    xhat_all[...] = xhat
    for load in small:
        load.wait()
    ln1_gain = vector(ln1g_ref)
    ln1_bias = vector(ln1b_ref)
    b_qv = bqv_ref[...].astype(F32)
    normed[...] = (xhat * ln1_gain + ln1_bias).astype(BF)
    for i in range(1, 3):
        loads[i].wait()
    proj = nn(normed[...], wqkv[:, 128:384])
    k_all[slot] = proj[:, 0:128].astype(BF)
    v_all[slot] = (proj[:, 128:256] + b_qv[1:2, :]).astype(BF)
    pl.semaphore_wait(barrier, 22)

    spread_start(k_all, KK, KKF)
    spread_start(v_all, VV, VVF)

    loads[0].wait()
    q_low = (nn(normed[...], wqkv[:, 0:128]) + b_qv[0:1, :]).astype(BF) * jnp.asarray(0.125, BF)
    lane = lax.broadcasted_iota(jnp.int32, (128, 128), 1)
    zero = jnp.zeros((128, 128), BF)
    q2[0:128, :] = jnp.where(lane < 64, q_low, zero)
    q2[128:256, :] = jnp.where(lane >= 64, q_low, zero)

    lanes = lax.broadcasted_iota(jnp.int32, (1, 256), 1)
    lanes = jnp.where(lanes >= 128, lanes - 128, lanes)
    q_pos = jnp.where(
        lanes < 64, lanes + 64 * order_ref[2 * ctx], lanes - 64 + 64 * order_ref[2 * ctx + 1]
    )
    seg = seg_ref[...]
    one = jnp.ones(seg.shape, F32)
    none = jnp.zeros(seg.shape, F32)

    def count(test):
        part = jnp.sum(jnp.where(test, one, none), axis=0, keepdims=True)
        return jnp.sum(part, axis=1, keepdims=True)

    first_end = count(seg < 1)
    second_end = count(seg < 2)
    q_float = q_pos.astype(F32)
    q_first = jnp.where(
        q_float >= second_end,
        second_end,
        jnp.where(q_float >= first_end, first_end, jnp.zeros_like(q_float)),
    ).astype(jnp.int32)
    row = lax.broadcasted_iota(jnp.int32, (128, 256), 0)

    def score(s, top):
        keys = k_all[s]
        owner = 2 * lax.rem(s, 8) + lax.div(s, 8)
        k_pos = jnp.where(
            row < 64, row + 64 * order_ref[2 * owner], row - 64 + 64 * order_ref[2 * owner + 1]
        )
        allowed = (k_pos <= q_pos) & (k_pos >= q_first)
        masked = jnp.where(allowed, nt(keys, q2[...]), -1e30)
        scores[s] = masked
        return jnp.maximum(top, jnp.max(masked.reshape(16, 8, 256), axis=0))

    top = score(slot, jnp.full((8, 256), -1e30, F32))
    loads[7].wait()
    loads[3].wait()
    dm[...] = nt(g_ref[...], wdn[...])
    b_out = vector(bout_ref)
    ln2_gain = vector(ln2g_ref)
    ln2_bias = vector(ln2b_ref)
    b_down = vector(bdown_ref)
    b_up = vector(bup_ref)

    def near(d, top):
        s = core * 8 + lax.rem(chip + 8 - d, 8)
        to_chip(k_all.at[slot], k_all.at[s], KK, d).wait_recv()
        to_partner(k_all.at[s], k_all.at[s], KKF, d).start()
        return score(s, top)

    top = lax.fori_loop(1, 8, near, top)
    to_partner(k_all.at[slot], k_all.at[other * 8 + chip], KK, 0).wait_recv()
    top = score(other * 8 + chip, top)
    spread_pass(v_all, VV, VVF)

    def far(d, top):
        s = other * 8 + lax.rem(chip + 8 - d, 8)
        to_partner(k_all.at[s], k_all.at[s], KKF, d).wait_recv()
        return score(s, top)

    top = lax.fori_loop(1, 8, far, top)
    arrivals.pop(KK)
    spread_end(v_all, VV, VVF)
    top = jnp.max(top, axis=0, keepdims=True)
    acc[...] = jnp.zeros_like(acc)

    def mix(s, total):
        p = jnp.exp(scores[s] - top)
        acc[...] += tn(v_all[s], p.astype(BF))
        return total + jnp.sum(p.reshape(16, 8, 256), axis=0)

    total = lax.fori_loop(0, 16, mix, jnp.zeros((8, 256), F32))
    total = jnp.sum(total, axis=0, keepdims=True)
    lse = top + jnp.log(total)
    half = lax.broadcasted_iota(jnp.int32, (128, 128), 0) < 64

    def diagonal(both):
        return jnp.where(half, both[:, 0:128], both[:, 128:256])

    raw_t = diagonal(acc[...] / total)
    attn_t[...] = raw_t
    attn_low[...] = raw_t.T.astype(BF)

    loads[4].wait()
    reduce_start(nn(attn_low[...], wout[...]), rs1s, rs1r, RS1)
    mine = pl.ds(pl.multiple_of(wa * 16, 16), 16)
    x_mine = x_ref[mine, :].astype(F32)
    g_mine = g_ref[mine, :].astype(F32)
    hidden = x_mine + reduce_end(rs1s, rs1r, RS1) + b_out
    hat_two, rstd_two = normalize(hidden)
    c_all[wa] = (hat_two * ln2_gain + ln2_bias).astype(BF)
    gather_start(c_all, AGC)
    loads[5].wait()
    gather_end(c_all, AGC)

    c_low = c_all[...].reshape(128, 1024)
    up = nn(c_low, wup[...]) + b_up
    tanh = jnp.tanh(GELU_A * (up + GELU_B * up * up * up))
    slope = 0.5 * (1.0 + tanh) + 0.5 * up * (1.0 - tanh * tanh) * GELU_A * (
        1.0 + 3.0 * GELU_B * up * up
    )
    du = (dm[...] * slope).astype(BF)
    act = (0.5 * up * (1.0 + tanh)).astype(BF)
    reduce_start(nt(du, wup[...]), rs2s, rs2r, RS2)
    gu[...] = tn(c_low, du).astype(BF).reshape(2, 2, 4, 64, 512)
    pair_start(gu, pu, 0)
    down = tn(act, g_ref[...]).astype(BF)
    gd[:, :, :, 0:32, :] = down[:, 0:512].reshape(2, 2, 4, 32, 512)
    gd[:, :, :, 32:64, :] = down[:, 512:1024].reshape(2, 2, 4, 32, 512)
    pair_start(gd, pd, 1)
    pair_end(gu, pu, 0)
    up_start()

    def vec_row(r, value):
        for j in range(8):
            vs[j, r : r + 1, :] = value[:, 128 * j : 128 * j + 128]

    def rows_sum(value):
        return jnp.sum(value, axis=0, keepdims=True)

    sum_up = rows_sum(du.astype(F32))
    for j in range(4):
        cvs[8 + j : 9 + j, :] = sum_up[:, 128 * j : 128 * j + 128]

    dc = reduce_end(rs2s, rs2r, RS2)
    d_hidden = g_mine + norm_back(dc, ln2_gain, hat_two, rstd_two)
    dh_all[wa] = d_hidden.astype(BF)
    gather_start(dh_all, AGD)
    pair_end(gd, pd, 1)
    vec_row(0, rows_sum(dc * hat_two))
    vec_row(1, rows_sum(dc))
    vec_row(2, rows_sum(d_hidden))
    vec_row(3, rows_sum(g_mine))
    gather_end(dh_all, AGD)
    down_start()
    up_mid()

    dh_low = dh_all[...].reshape(128, 1024)
    d_attn = nt(dh_low, wout[...]).astype(BF)
    dot_t = d_attn.astype(F32).T * attn_t[...]
    delta = jnp.concatenate(
        [
            jnp.sum(dot_t[0:64], axis=0, keepdims=True),
            jnp.sum(dot_t[64:128], axis=0, keepdims=True),
        ],
        axis=1,
    )
    do2 = jnp.concatenate(
        [jnp.where(lane < 64, d_attn, zero), jnp.where(lane >= 64, d_attn, zero)], axis=0
    )
    acc[...] = jnp.zeros_like(acc)

    def back(s):
        p = jnp.exp(scores[s] - lse)
        ds = (p * (nt(v_all[s], do2) - delta)).astype(BF)
        acc[...] += tn(k_all[s], ds)
        dkv[s, :, 0:128] = nn(ds, q2[...]).astype(BF)
        dkv[s, :, 128:256] = nn(p.astype(BF), do2).astype(BF)

    each(0, 8, lambda j: back(other * 8 + j))
    combine_start(dkv, pkv, 2)
    each(0, 8, lambda j: back(core * 8 + j))
    combined(dkv, pkv, 2)
    scatter_start(dkv, rkv, RKV)

    dq = (diagonal(acc[...]) * 0.125).T.astype(BF)
    gb[:, 64:128, :] = tn(normed[...], dq).astype(BF).reshape(16, 64, 128)
    d_out = tn(attn_low[...], dh_low).astype(BF)
    for s in range(16):
        gb[s, 0:64, :] = d_out[64 * (s % 2) : 64 * (s % 2) + 64, 128 * (s // 2) : 128 * (s // 2) + 128]
    combine_start(gb, pb, 3)
    reduce_start(nn(act, wdn[...]), rs3s, rs3r, RS3)
    combined(gb, pb, 3)
    scatter_start(gb, rb, RB)
    up_end()
    tree_start(ou, AGU, FWU, up_tree_mid)
    down_mid()

    dkv_mine = scatter_end(dkv, rkv, RKV)
    both = tn(normed[...], dkv_mine).astype(BF)
    gc[:, 0:64, :] = both[:, 0:128].reshape(16, 64, 128)
    gc[:, 64:128, :] = both[:, 128:256].reshape(16, 64, 128)
    combine_start(gc, pc, 4)
    d_qkv = jnp.concatenate([dq, dkv_mine], axis=1)
    da = nt(d_qkv, wqkv[...])
    reduce_start(da, rs4s, rs4r, RS4)
    combined(gc, pc, 4)
    scatter_start(gc, rc, RC)
    down_end()
    tree_start(od, AGW, FWW, down_tree_mid)
    up_tree_mid(ou, AGU, FWU)
    vec_row(4, rows_sum(da * xhat_all[...]))
    vec_row(5, rows_sum(da))
    for j in range(8):
        vs[j, 6:8, :] = jnp.zeros((2, 128), F32)
    each(1, 8, lambda d: to_wa(vs.at[lax.rem(wa + d, 8)], vr.at[d], RS5, d).start())
    sends.append(lambda: wa_sent(vs, RS5))
    cvs[12:13, :] = rows_sum(dq.astype(F32))
    cvs[13:14, :] = rows_sum(dkv_mine[:, 128:256].astype(F32))
    cvs[14:16, :] = jnp.zeros((2, 128), F32)
    ob[slot] = scatter_end(gb, rb, RB)
    spread_start(ob, AGB, FWB)

    hat_one, rstd_one = normalize(x_mine)
    d_first = reduce_end(rs4s, rs4r, RS4)
    g_all[wa] = (d_hidden + norm_back(d_first, ln1_gain, hat_one, rstd_one)).astype(BF)
    gather_start(g_all, AGG)

    each(1, 8, lambda d: to_wa(vs.at[lax.rem(wa + d, 8)], vr.at[d], RS5, d).wait_recv())
    vec_sum = vs[wa]
    for d in range(1, 8):
        vec_sum = vec_sum + vr[d]
    cvs[0:8, :] = vec_sum
    cvr[ctx] = cvs[...]

    def to_ctx(dst, d):
        return pltpu.make_async_remote_copy(
            src_ref=cvs,
            dst_ref=cvr.at[dst],
            send_sem=cs_s.at[5 + d],
            recv_sem=cs_r.at[5 + d],
            device_id={"ctx": lax.rem(ctx + d, 16)},
            device_id_type=MESH,
        )

    each(1, 16, lambda d: to_ctx(ctx, d).start())
    sends.append(lambda: each(1, 16, lambda d: to_ctx(ctx, d).wait_send()))
    oc[slot] = scatter_end(gc, rc, RC)
    spread_start(oc, AGCC, FWC)
    down_tree_mid(od, AGW, FWW)
    tree_pass(ou, AGU, FWU)
    y_all[wa] = (hidden + reduce_end(rs3s, rs3r, RS3) + b_down).astype(BF)
    gather_start(y_all, AGY)
    each(1, 16, lambda d: to_ctx(lax.rem(ctx + 16 - d, 16), d).wait_recv())
    ctx_sum = cvr[0]
    for i in range(1, 16):
        ctx_sum = ctx_sum + cvr[i]
    ctx_out[...] = ctx_sum[8:16, :]
    vall[wa] = ctx_sum[0:8, :]
    gather_start(vall, AGV)
    spread_pass(ob, AGB, FWB)
    tree_end(ou, AGU, FWU)
    ou_out[...] = ou[...]
    tree_pass(od, AGW, FWW)
    tree_end(od, AGW, FWW)
    od_out[...] = od[...]
    spread_pass(oc, AGCC, FWC)
    gather_end(g_all, AGG)
    gin_out[...] = g_all[...].reshape(128, 1024)
    spread_end(ob, AGB, FWB)
    ob_out[...] = ob[...]
    gather_end(y_all, AGY)
    y_out[...] = y_all[...].reshape(128, 1024)
    gather_end(vall, AGV)
    vec_out[...] = vall[...]
    spread_end(oc, AGCC, FWC)
    oc_out[...] = oc[...]

    for sent in sends:
        sent()


def finish(
    y_ref,
    gin_ref,
    ou_ref,
    od_ref,
    ob_ref,
    oc_ref,
    vec_ref,
    ctx_ref,
    y_out,
    gin_out,
    ln1g_out,
    ln1b_out,
    gqkv_out,
    bqv_out,
    gwo_out,
    bout_out,
    ln2g_out,
    ln2b_out,
    gup_out,
    bup_out,
    gdn_out,
    bdown_out,
    gin,
    gqkv,
    gwo,
    gup,
    gdn,
    sems,
):
    copies = []

    def leave(src, dst):
        copies.append(pltpu.make_async_copy(src, dst, sems.at[len(copies)]))
        copies[-1].start()

    leave(y_ref, y_out)
    for i in range(4):
        rows = pl.ds(256 * i, 256)
        gup[rows, :] = ou_ref[4 * i : 4 * i + 4].astype(F32).reshape(256, 512)
        leave(gup.at[rows], gup_out.at[rows])
    for i in range(4):
        rows = pl.ds(128 * i, 128)
        part = od_ref[4 * i : 4 * i + 4].astype(F32)
        gdn[rows, 0:512] = part[:, 0:32].reshape(128, 512)
        gdn[rows, 512:1024] = part[:, 32:64].reshape(128, 512)
        leave(gdn.at[rows], gdn_out.at[rows])
    gin[...] = gin_ref[...].astype(F32)
    leave(gin, gin_out)
    for s in range(16):
        gwo[64 * (s % 2) : 64 * (s % 2) + 64, 128 * (s // 2) : 128 * (s // 2) + 128] = ob_ref[
            s, 0:64, :
        ].astype(F32)
    leave(gwo, gwo_out)
    gqkv[0] = ob_ref[:, 64:128, :].astype(F32).reshape(1024, 128)
    leave(gqkv.at[0], gqkv_out.at[0])
    gqkv[1] = oc_ref[:, 0:64, :].astype(F32).reshape(1024, 128)
    leave(gqkv.at[1], gqkv_out.at[1])
    gqkv[2] = oc_ref[:, 64:128, :].astype(F32).reshape(1024, 128)
    leave(gqkv.at[2], gqkv_out.at[2])
    for r, out in enumerate((ln2g_out, ln2b_out, bout_out, bdown_out, ln1g_out, ln1b_out)):
        out[...] = vec_ref[:, r, :]
    bup_out[...] = ctx_ref[0:4, :]
    bqv_out[...] = ctx_ref[4:6, :]
    for copy in copies:
        copy.wait()


def body(
    layer_input,
    block_order,
    seg_ids,
    cotangent,
    ln1_gain,
    ln1_bias,
    w_qkv,
    b_qv,
    w_out,
    b_out,
    ln2_gain,
    ln2_bias,
    w_up,
    b_up,
    w_down,
    b_down,
):
    vmem = pl.BlockSpec(memory_space=pltpu.VMEM)
    hbm = pl.BlockSpec(memory_space=pl.ANY)
    far = pl.BlockSpec(memory_space=pltpu.HBM)

    def stay(operand):
        return pltpu.with_memory_space_constraint(operand, pltpu.HBM)

    def bf(*shape):
        return pltpu.VMEM(shape, BF)

    def f32(*shape):
        return pltpu.VMEM(shape, F32)

    outs = pl.pallas_call(
        layer,
        out_shape=(
            jax.ShapeDtypeStruct((128, 1024), BF),
            jax.ShapeDtypeStruct((128, 1024), BF),
            jax.ShapeDtypeStruct((16, 64, 512), BF),
            jax.ShapeDtypeStruct((16, 64, 512), BF),
            jax.ShapeDtypeStruct((16, 128, 128), BF),
            jax.ShapeDtypeStruct((16, 128, 128), BF),
            jax.ShapeDtypeStruct((8, 8, 128), F32),
            jax.ShapeDtypeStruct((8, 128), F32),
        ),
        in_specs=[far] * 16,
        out_specs=(vmem,) * 8,
        scratch_shapes=[
            pltpu.SMEM((32,), jnp.int32),
            pltpu.VMEM((16, 128), jnp.int32),
            bf(128, 1024),
            bf(128, 1024),
            bf(8, 128),
            bf(8, 128),
            bf(8, 128),
            bf(8, 128),
            bf(8, 128),
            bf(8, 128),
            bf(4, 128),
            bf(2, 128),
            bf(1024, 384),
            bf(128, 1024),
            bf(1024, 512),
            bf(512, 1024),
            pltpu.SemaphoreType.DMA((18,)),
            f32(128, 1024),
            bf(128, 1024),
            bf(16, 128, 128),
            bf(16, 128, 128),
            bf(256, 128),
            f32(16, 128, 256),
            f32(128, 256),
            f32(128, 128),
            bf(128, 128),
            bf(8, 16, 1024),
            bf(8, 16, 1024),
            bf(8, 16, 1024),
            f32(128, 512),
            bf(8, 16, 1024),
            bf(8, 16, 1024),
            bf(8, 16, 1024),
            bf(8, 16, 1024),
            bf(8, 16, 1024),
            bf(8, 16, 1024),
            bf(16, 128, 256),
            bf(8, 128, 256),
            bf(8, 128, 256),
            bf(2, 2, 4, 64, 512),
            bf(2, 4, 64, 512),
            bf(4, 2, 64, 512),
            bf(2, 64, 512),
            bf(64, 512),
            bf(16, 64, 512),
            bf(2, 2, 4, 64, 512),
            bf(2, 4, 64, 512),
            bf(4, 64, 512),
            bf(4, 64, 512),
            bf(4, 64, 512),
            bf(16, 64, 512),
            bf(16, 128, 128),
            bf(8, 128, 128),
            bf(8, 128, 128),
            bf(16, 128, 128),
            bf(16, 128, 128),
            bf(8, 128, 128),
            bf(8, 128, 128),
            bf(16, 128, 128),
            bf(8, 16, 1024),
            bf(8, 16, 1024),
            bf(8, 16, 1024),
            f32(8, 8, 128),
            f32(8, 8, 128),
            f32(8, 8, 128),
            f32(16, 128),
            f32(16, 16, 128),
            pltpu.SemaphoreType.DMA((NSEM, 8)),
            pltpu.SemaphoreType.DMA((NSEM, 8)),
            pltpu.SemaphoreType.DMA((21,)),
            pltpu.SemaphoreType.DMA((21,)),
        ],
        compiler_params=pltpu.CompilerParams(
            collective_id=0, has_side_effects=True, vmem_limit_bytes=32 << 20
        ),
        name="decoder",
    )(
        stay(block_order),
        stay(seg_ids.reshape(16, 128)),
        stay(layer_input),
        stay(cotangent),
        *(
            stay(v.reshape(-1, 128))
            for v in (ln1_gain, ln1_bias, b_out, ln2_gain, ln2_bias, b_down, b_up)
        ),
        stay(b_qv),
        stay(w_qkv.transpose(1, 0, 2)),
        stay(w_out),
        stay(w_up),
        stay(w_down),
    )
    shapes = (
        ((128, 1024), BF),
        ((128, 1024), F32),
        ((8, 128), F32),
        ((8, 128), F32),
        ((3, 1024, 128), F32),
        ((2, 128), F32),
        ((128, 1024), F32),
        ((8, 128), F32),
        ((8, 128), F32),
        ((8, 128), F32),
        ((1024, 512), F32),
        ((4, 128), F32),
        ((512, 1024), F32),
        ((8, 128), F32),
    )
    large = (0, 1, 4, 6, 10, 12)
    done = list(
        pl.pallas_call(
            finish,
            out_shape=tuple(jax.ShapeDtypeStruct(*shape) for shape in shapes),
            in_specs=[vmem] * 8,
            out_specs=tuple(hbm if i in large else vmem for i in range(14)),
            scratch_shapes=[
                f32(128, 1024),
                f32(3, 1024, 128),
                f32(128, 1024),
                f32(1024, 512),
                f32(512, 1024),
                pltpu.SemaphoreType.DMA((14,)),
            ],
            compiler_params=pltpu.CompilerParams(vmem_limit_bytes=24 << 20),
            name="finish",
        )(*outs)
    )
    for i in (2, 3, 7, 8, 9, 11, 13):
        done[i] = done[i].reshape(-1)
    done[4] = done[4].transpose(1, 0, 2)
    return tuple(done)


def solution(mesh):
    placed = (
        P("ctx", None),
        P(),
        P(),
        P("ctx", None),
        P(),
        P(),
        P(None, None, "wa"),
        P(None, "wa"),
        P("wa", None),
        P(),
        P(),
        P(),
        P(None, "wa"),
        P("wa"),
        P("wa", None),
        P(),
    )
    return jax.shard_map(
        body,
        mesh=mesh,
        in_specs=placed,
        out_specs=(
            P("ctx", None),
            P("ctx", None),
            P(),
            P(),
            P(None, None, "wa"),
            P(None, "wa"),
            P("wa", None),
            P(),
            P(),
            P(),
            P(None, "wa"),
            P("wa"),
            P("wa", None),
            P(),
        ),
        check_vma=False,
    )
```

```python
import jax
import jax.numpy as jnp
from jax import lax
from jax.experimental import pallas as pl
from jax.experimental.pallas import tpu as pltpu
from jax.sharding import PartitionSpec as P

F32 = jnp.float32
BF = jnp.bfloat16
MESH = pl.DeviceIdType.MESH
GELU_A = 0.7978845608028654
GELU_B = 0.044715

(
    KK,
    KKF,
    VV,
    VVF,
    RS1,
    AGC,
    RS2,
    RS3,
    AGD,
    AGY,
    RKV,
    RUX,
    RUY,
    AGU,
    FWU,
    RDY,
    RDX,
    AGW,
    FWW,
    RB,
    AGB,
    FWB,
    RC,
    AGCC,
    FWC,
    RS4,
    RS5,
    AGG,
    AGV,
    NSEM,
) = range(30)


def nn(a, b):
    return lax.dot_general(a, b, (((1,), (0,)), ((), ())), preferred_element_type=F32)


def nt(a, b):
    return lax.dot_general(a, b, (((1,), (1,)), ((), ())), preferred_element_type=F32)


def tn(a, b):
    return lax.dot_general(a, b, (((0,), (0,)), ((), ())), preferred_element_type=F32)


def normalize(rows):
    centered = rows - jnp.mean(rows, -1, keepdims=True)
    rstd = lax.rsqrt(jnp.mean(centered * centered, -1, keepdims=True) + 1e-05)
    return centered * rstd, rstd


def norm_back(grad, gain, xhat, rstd):
    gx = grad * gain
    return rstd * (
        gx - jnp.mean(gx, -1, keepdims=True) - xhat * jnp.mean(gx * xhat, -1, keepdims=True)
    )


def layer(
    order_hbm,
    seg_hbm,
    x_hbm,
    g_hbm,
    ln1g_hbm,
    ln1b_hbm,
    bout_hbm,
    ln2g_hbm,
    ln2b_hbm,
    bdown_hbm,
    bup_hbm,
    bqv_hbm,
    wqkv_hbm,
    wout_hbm,
    wup_hbm,
    wdn_hbm,
    y_out,
    gin_out,
    ou_out,
    od_out,
    ob_out,
    oc_out,
    vec_out,
    ctx_out,
    order_ref,
    seg_ref,
    x_ref,
    g_ref,
    ln1g_ref,
    ln1b_ref,
    bout_ref,
    ln2g_ref,
    ln2b_ref,
    bdown_ref,
    bup_ref,
    bqv_ref,
    wqkv,
    wout,
    wup,
    wdn,
    load_sem,
    xhat_all,
    normed,
    k_all,
    v_all,
    q2,
    scores,
    acc,
    attn_t,
    attn_low,
    rs1s,
    rs1r,
    c_all,
    dm,
    rs2s,
    rs2r,
    rs3s,
    rs3r,
    dh_all,
    y_all,
    dkv,
    pkv,
    rkv,
    gu,
    pu,
    rux,
    tu,
    ruy,
    ou,
    gd,
    pd,
    rdy,
    td,
    rdx,
    od,
    gb,
    pb,
    rb,
    ob,
    gc,
    pc,
    rc,
    oc,
    rs4s,
    rs4r,
    g_all,
    vs,
    vr,
    vall,
    cvs,
    cvr,
    ss,
    rs,
    cs_s,
    cs_r,
):
    ctx = lax.axis_index("ctx")
    wa = lax.axis_index("wa")
    core = lax.rem(ctx, 2)
    chip = lax.div(ctx, 2)
    other = 1 - core
    row_at = lax.div(chip, 4)
    col_at = lax.rem(chip, 4)
    row_far = 1 - row_at
    slot = core * 8 + chip
    partner = chip * 2 + other

    def to_wa(src, dst, kind, d):
        return pltpu.make_async_remote_copy(
            src_ref=src,
            dst_ref=dst,
            send_sem=ss.at[kind, d],
            recv_sem=rs.at[kind, d],
            device_id={"wa": lax.rem(wa + d, 8)},
            device_id_type=MESH,
        )

    def to_chip(src, dst, kind, d):
        return pltpu.make_async_remote_copy(
            src_ref=src,
            dst_ref=dst,
            send_sem=ss.at[kind, d],
            recv_sem=rs.at[kind, d],
            device_id={"ctx": lax.rem(chip + d, 8) * 2 + core},
            device_id_type=MESH,
        )

    def to_partner(src, dst, kind, d):
        return pltpu.make_async_remote_copy(
            src_ref=src,
            dst_ref=dst,
            send_sem=ss.at[kind, d],
            recv_sem=rs.at[kind, d],
            device_id={"ctx": partner},
            device_id_type=MESH,
        )

    sends = []
    arrivals = {}

    def each(low, high, step):
        @pl.loop(low, high)
        def _(d):
            step(d)

    loads = [
        pltpu.make_async_copy(
            wqkv_hbm.at[i], wqkv.at[:, pl.ds(128 * i, 128)], load_sem.at[i]
        )
        for i in range(3)
    ] + [
        pltpu.make_async_copy(wdn_hbm, wdn, load_sem.at[3]),
        pltpu.make_async_copy(wout_hbm, wout, load_sem.at[4]),
        pltpu.make_async_copy(wup_hbm, wup, load_sem.at[5]),
        pltpu.make_async_copy(x_hbm, x_ref, load_sem.at[6]),
        pltpu.make_async_copy(g_hbm, g_ref, load_sem.at[7]),
    ]
    small = [
        pltpu.make_async_copy(src, dst, load_sem.at[8 + i])
        for i, (src, dst) in enumerate(
            (
                (ln1g_hbm, ln1g_ref),
                (ln1b_hbm, ln1b_ref),
                (bqv_hbm, bqv_ref),
                (order_hbm, order_ref),
                (seg_hbm, seg_ref),
                (bout_hbm, bout_ref),
                (ln2g_hbm, ln2g_ref),
                (ln2b_hbm, ln2b_ref),
                (bdown_hbm, bdown_ref),
                (bup_hbm, bup_ref),
            )
        )
    ]
    loads[6].start()
    for load in small:
        load.start()
    for i in (1, 2, 0, 7, 3, 4, 5):
        loads[i].start()

    def combine(buf, kept, index):
        return pltpu.make_async_remote_copy(
            src_ref=buf.at[pl.ds(pl.multiple_of(other * 8, 8), 8)],
            dst_ref=kept,
            send_sem=cs_s.at[index],
            recv_sem=cs_r.at[index],
            device_id={"ctx": partner},
            device_id_type=MESH,
        )

    def combine_start(buf, kept, index):
        combine(buf, kept, index).start()
        sends.append(lambda: combine(buf, kept, index).wait_send())
        arrivals[100 + index] = lambda: combined(buf, kept, index)

    def combined(buf, kept, index):
        arrivals.pop(100 + index)
        combine(buf, kept, index).wait_recv()

        @pl.loop(0, 8)
        def _(j):
            buf[core * 8 + j] = (buf[core * 8 + j].astype(F32) + kept[j].astype(F32)).astype(BF)

    def scatter_start(buf, recv, kind):
        sends.append(
            lambda: each(
                1, 8, lambda d: to_chip(buf.at[slot], buf.at[slot], kind, d).wait_send()
            )
        )
        arrivals[kind] = lambda: scatter_end(buf, recv, kind)
        each(
            1,
            8,
            lambda d: to_chip(
                buf.at[core * 8 + lax.rem(chip + d, 8)], recv.at[d], kind, d
            ).start(),
        )

    def scatter_end(buf, recv, kind):
        arrivals.pop(kind)
        each(
            1,
            8,
            lambda d: to_chip(
                buf.at[core * 8 + lax.rem(chip + d, 8)], recv.at[d], kind, d
            ).wait_recv(),
        )
        whole = buf[slot].astype(F32)
        for d in range(1, 8):
            whole = whole + recv[d].astype(F32)
        return whole.astype(BF)

    def spread_start(buf, kind, forward):
        sends.append(lambda: spread_sent(buf, kind, forward))
        arrivals[kind] = lambda: (
            spread_pass(buf, kind, forward),
            spread_end(buf, kind, forward),
        )
        to_partner(buf.at[slot], buf.at[slot], kind, 0).start()
        each(1, 8, lambda d: to_chip(buf.at[slot], buf.at[slot], kind, d).start())

    def spread_sent(buf, kind, forward):
        to_partner(buf.at[slot], buf.at[slot], kind, 0).wait_send()

        def sent(d):
            to_chip(buf.at[slot], buf.at[slot], kind, d).wait_send()
            to_partner(buf.at[slot], buf.at[slot], forward, d).wait_send()

        each(1, 8, sent)

    def spread_pass(buf, kind, forward):
        arrivals[kind] = lambda: spread_end(buf, kind, forward)

        def step(d):
            s = core * 8 + lax.rem(chip + 8 - d, 8)
            to_chip(buf.at[slot], buf.at[s], kind, d).wait_recv()
            to_partner(buf.at[s], buf.at[s], forward, d).start()

        each(1, 8, step)

    def spread_end(buf, kind, forward):
        arrivals.pop(kind)
        s = other * 8 + chip
        to_partner(buf.at[s], buf.at[s], kind, 0).wait_recv()

        def step(d):
            t = other * 8 + lax.rem(chip + 8 - d, 8)
            to_partner(buf.at[t], buf.at[t], forward, d).wait_recv()

        each(1, 8, step)

    def reduce_start(part, send, recv, kind):
        send[...] = part.astype(BF).reshape(8, 16, 1024)
        each(1, 8, lambda d: to_wa(send.at[lax.rem(wa + d, 8)], recv.at[d], kind, d).start())
        sends.append(lambda: wa_sent(send, kind))
        arrivals[kind] = lambda: reduce_end(send, recv, kind)

    def reduce_end(send, recv, kind):
        arrivals.pop(kind)
        each(1, 8, lambda d: to_wa(send.at[lax.rem(wa + d, 8)], recv.at[d], kind, d).wait_recv())
        whole = send[wa].astype(F32)
        for d in range(1, 8):
            whole = whole + recv[d].astype(F32)
        return whole

    def gather_start(buf, kind):
        each(1, 8, lambda d: to_wa(buf.at[wa], buf.at[wa], kind, d).start())
        sends.append(lambda: wa_sent(buf, kind))
        arrivals[kind] = lambda: gather_end(buf, kind)

    def wa_sent(buf, kind):
        each(1, 8, lambda d: to_wa(buf.at[wa], buf.at[wa], kind, d).wait_send())

    def gather_end(buf, kind):
        arrivals.pop(kind)
        each(
            1,
            8,
            lambda d: to_wa(buf.at[wa], buf.at[lax.rem(wa + 8 - d, 8)], kind, d).wait_recv(),
        )

    def to_x(src, dst, kind, at, d):
        return pltpu.make_async_remote_copy(
            src_ref=src,
            dst_ref=dst,
            send_sem=ss.at[kind, at],
            recv_sem=rs.at[kind, at],
            device_id={"ctx": (row_at * 4 + lax.rem(col_at + d, 4)) * 2 + core},
            device_id_type=MESH,
        )

    def to_y(src, dst, kind, at):
        return pltpu.make_async_remote_copy(
            src_ref=src,
            dst_ref=dst,
            send_sem=ss.at[kind, at],
            recv_sem=rs.at[kind, at],
            device_id={"ctx": lax.rem(chip + 4, 8) * 2 + core},
            device_id_type=MESH,
        )

    def pair(buf, kept, index):
        return pltpu.make_async_remote_copy(
            src_ref=buf.at[other],
            dst_ref=kept,
            send_sem=cs_s.at[index],
            recv_sem=cs_r.at[index],
            device_id={"ctx": partner},
            device_id_type=MESH,
        )

    def pair_start(buf, kept, index):
        pair(buf, kept, index).start()
        sends.append(lambda: pair(buf, kept, index).wait_send())
        arrivals[100 + index] = lambda: pair_end(buf, kept, index)

    def pair_end(buf, kept, index):
        arrivals.pop(100 + index)
        pair(buf, kept, index).wait_recv()

        @pl.loop(0, 8)
        def _(j):
            at = (lax.div(j, 4), lax.rem(j, 4))
            buf[(core, *at)] = (buf[(core, *at)].astype(F32) + kept[at].astype(F32)).astype(BF)

    def up_x(d):
        return to_x(gu.at[core, :, lax.rem(col_at + d, 4)], rux.at[d], RUX, d, d)

    def up_start():
        each(1, 4, lambda d: up_x(d).start())
        sends.append(lambda: each(1, 4, lambda d: up_x(d).wait_send()))
        arrivals[RUX] = up_mid

    def up_mid():
        arrivals.pop(RUX)
        each(1, 4, lambda d: up_x(d).wait_recv())
        for y in range(2):
            whole = gu[core, y, col_at].astype(F32)
            for d in range(1, 4):
                whole = whole + rux[d, y].astype(F32)
            tu[y] = whole.astype(BF)
        to_y(tu.at[row_far], ruy, RUY, 0).start()
        sends.append(lambda: to_y(tu.at[row_far], ruy, RUY, 0).wait_send())
        arrivals[RUY] = up_end

    def up_end():
        arrivals.pop(RUY)
        to_y(tu.at[row_far], ruy, RUY, 0).wait_recv()
        ou[slot] = (tu[row_at].astype(F32) + ruy[...].astype(F32)).astype(BF)

    def down_y():
        return to_y(gd.at[core, row_far], rdy, RDY, 0)

    def down_x(d):
        return to_x(td.at[lax.rem(col_at + d, 4)], rdx.at[d], RDX, d, d)

    def down_start():
        down_y().start()
        sends.append(lambda: down_y().wait_send())
        arrivals[RDY] = down_mid

    def down_mid():
        arrivals.pop(RDY)
        down_y().wait_recv()
        for x in range(4):
            td[x] = (gd[core, row_at, x].astype(F32) + rdy[x].astype(F32)).astype(BF)
        each(1, 4, lambda d: down_x(d).start())
        sends.append(lambda: each(1, 4, lambda d: down_x(d).wait_send()))
        arrivals[RDX] = down_end

    def down_end():
        arrivals.pop(RDX)
        each(1, 4, lambda d: down_x(d).wait_recv())
        whole = td[col_at].astype(F32)
        for d in range(1, 4):
            whole = whole + rdx[d].astype(F32)
        od[slot] = whole.astype(BF)

    def place(side, y, d):
        return side * 8 + y * 4 + lax.rem(col_at + 4 - d, 4)

    def tree_start(buf, kind, forward, middle):
        own = buf.at[slot]
        to_y(own, own, kind, 4).start()
        each(1, 4, lambda d: to_x(own, own, kind, d, d).start())
        to_partner(own, own, kind, 0).start()

        def sent():
            each(0, 8, lambda d: to_y(own, own, kind, d).wait_send())
            each(1, 8, lambda d: to_y(own, own, forward, d).wait_send())

        sends.append(sent)
        arrivals[kind] = lambda: (
            middle(buf, kind, forward),
            tree_pass(buf, kind, forward),
            tree_end(buf, kind, forward),
        )

    def take(buf, s, kind, forward, d):
        at = buf.at[s]
        to_y(at, at, kind, d).wait_recv()
        to_partner(at, at, forward, d).start()

    def up_tree_mid(buf, kind, forward):
        s = place(core, row_far, 0)
        take(buf, s, kind, forward, 4)
        each(1, 4, lambda d: to_x(buf.at[s], buf.at[s], kind, 4 + d, d).start())
        each(1, 4, lambda d: take(buf, place(core, row_at, d), kind, forward, d))
        arrivals[kind] = lambda: (tree_pass(buf, kind, forward), tree_end(buf, kind, forward))

    def down_tree_mid(buf, kind, forward):
        def step(d):
            s = place(core, row_at, d)
            take(buf, s, kind, forward, d)
            to_y(buf.at[s], buf.at[s], kind, 4 + d).start()

        each(1, 4, step)
        take(buf, place(core, row_far, 0), kind, forward, 4)
        arrivals[kind] = lambda: (tree_pass(buf, kind, forward), tree_end(buf, kind, forward))

    def tree_pass(buf, kind, forward):
        each(1, 4, lambda d: take(buf, place(core, row_far, d), kind, forward, 4 + d))
        arrivals[kind] = lambda: tree_end(buf, kind, forward)

    def tree_end(buf, kind, forward):
        arrivals.pop(kind)

        def landed(s, sem, d):
            to_partner(buf.at[s], buf.at[s], sem, d).wait_recv()

        landed(other * 8 + chip, kind, 0)
        landed(place(other, row_far, 0), forward, 4)

        def step(d):
            landed(place(other, row_at, d), forward, d)
            landed(place(other, row_far, d), forward, 4 + d)

        each(1, 4, step)

    barrier = pltpu.get_barrier_semaphore()
    each(
        1,
        16,
        lambda d: pl.semaphore_signal(
            barrier, inc=1, device_id={"ctx": lax.rem(ctx + d, 16)}, device_id_type=MESH
        ),
    )
    each(
        1,
        8,
        lambda d: pl.semaphore_signal(
            barrier, inc=1, device_id={"wa": lax.rem(wa + d, 8)}, device_id_type=MESH
        ),
    )

    def vector(ref):
        rows = ref[...].astype(F32)
        return jnp.concatenate([rows[j : j + 1, :] for j in range(rows.shape[0])], axis=1)

    loads[6].wait()
    xhat, _ = normalize(x_ref[...].astype(F32))
    xhat_all[...] = xhat
    for load in small:
        load.wait()
    ln1_gain = vector(ln1g_ref)
    ln1_bias = vector(ln1b_ref)
    b_qv = bqv_ref[...].astype(F32)
    normed[...] = (xhat * ln1_gain + ln1_bias).astype(BF)
    for i in range(1, 3):
        loads[i].wait()
    proj = nn(normed[...], wqkv[:, 128:384])
    k_all[slot] = proj[:, 0:128].astype(BF)
    v_all[slot] = (proj[:, 128:256] + b_qv[1:2, :]).astype(BF)
    pl.semaphore_wait(barrier, 22)

    spread_start(k_all, KK, KKF)
    spread_start(v_all, VV, VVF)

    loads[0].wait()
    q_low = (nn(normed[...], wqkv[:, 0:128]) + b_qv[0:1, :]).astype(BF) * jnp.asarray(0.125, BF)
    lane = lax.broadcasted_iota(jnp.int32, (128, 128), 1)
    zero = jnp.zeros((128, 128), BF)
    q2[0:128, :] = jnp.where(lane < 64, q_low, zero)
    q2[128:256, :] = jnp.where(lane >= 64, q_low, zero)

    lanes = lax.broadcasted_iota(jnp.int32, (1, 256), 1)
    lanes = jnp.where(lanes >= 128, lanes - 128, lanes)
    q_pos = jnp.where(
        lanes < 64, lanes + 64 * order_ref[2 * ctx], lanes - 64 + 64 * order_ref[2 * ctx + 1]
    )
    seg = seg_ref[...]
    one = jnp.ones(seg.shape, F32)
    none = jnp.zeros(seg.shape, F32)

    def count(test):
        part = jnp.sum(jnp.where(test, one, none), axis=0, keepdims=True)
        return jnp.sum(part, axis=1, keepdims=True)

    first_end = count(seg < 1)
    second_end = count(seg < 2)
    q_float = q_pos.astype(F32)
    q_first = jnp.where(
        q_float >= second_end,
        second_end,
        jnp.where(q_float >= first_end, first_end, jnp.zeros_like(q_float)),
    ).astype(jnp.int32)
    row = lax.broadcasted_iota(jnp.int32, (128, 256), 0)

    def score(s, top):
        keys = k_all[s]
        owner = 2 * lax.rem(s, 8) + lax.div(s, 8)
        k_pos = jnp.where(
            row < 64, row + 64 * order_ref[2 * owner], row - 64 + 64 * order_ref[2 * owner + 1]
        )
        allowed = (k_pos <= q_pos) & (k_pos >= q_first)
        masked = jnp.where(allowed, nt(keys, q2[...]), -1e30)
        scores[s] = masked
        return jnp.maximum(top, jnp.max(masked.reshape(16, 8, 256), axis=0))

    top = score(slot, jnp.full((8, 256), -1e30, F32))
    loads[7].wait()
    loads[3].wait()
    dm[...] = nt(g_ref[...], wdn[...])
    b_out = vector(bout_ref)
    ln2_gain = vector(ln2g_ref)
    ln2_bias = vector(ln2b_ref)
    b_down = vector(bdown_ref)
    b_up = vector(bup_ref)

    def near(d, top):
        s = core * 8 + lax.rem(chip + 8 - d, 8)
        to_chip(k_all.at[slot], k_all.at[s], KK, d).wait_recv()
        to_partner(k_all.at[s], k_all.at[s], KKF, d).start()
        return score(s, top)

    top = lax.fori_loop(1, 8, near, top)
    to_partner(k_all.at[slot], k_all.at[other * 8 + chip], KK, 0).wait_recv()
    top = score(other * 8 + chip, top)
    spread_pass(v_all, VV, VVF)

    def far(d, top):
        s = other * 8 + lax.rem(chip + 8 - d, 8)
        to_partner(k_all.at[s], k_all.at[s], KKF, d).wait_recv()
        return score(s, top)

    top = lax.fori_loop(1, 8, far, top)
    arrivals.pop(KK)
    spread_end(v_all, VV, VVF)
    top = jnp.max(top, axis=0, keepdims=True)
    acc[...] = jnp.zeros_like(acc)

    def mix(s, total):
        p = jnp.exp(scores[s] - top)
        acc[...] += tn(v_all[s], p.astype(BF))
        return total + jnp.sum(p.reshape(16, 8, 256), axis=0)

    total = lax.fori_loop(0, 16, mix, jnp.zeros((8, 256), F32), unroll=16)
    total = jnp.sum(total, axis=0, keepdims=True)
    lse = top + jnp.log(total)
    half = lax.broadcasted_iota(jnp.int32, (128, 128), 0) < 64

    def diagonal(both):
        return jnp.where(half, both[:, 0:128], both[:, 128:256])

    raw_t = diagonal(acc[...] / total)
    attn_t[...] = raw_t
    attn_low[...] = raw_t.T.astype(BF)

    loads[4].wait()
    reduce_start(nn(attn_low[...], wout[...]), rs1s, rs1r, RS1)
    mine = pl.ds(pl.multiple_of(wa * 16, 16), 16)
    x_mine = x_ref[mine, :].astype(F32)
    g_mine = g_ref[mine, :].astype(F32)
    hidden = x_mine + reduce_end(rs1s, rs1r, RS1) + b_out
    hat_two, rstd_two = normalize(hidden)
    c_all[wa] = (hat_two * ln2_gain + ln2_bias).astype(BF)
    gather_start(c_all, AGC)
    loads[5].wait()
    gather_end(c_all, AGC)

    c_low = c_all[...].reshape(128, 1024)
    up = nn(c_low, wup[...]) + b_up
    tanh = jnp.tanh(GELU_A * (up + GELU_B * up * up * up))
    slope = 0.5 * (1.0 + tanh) + 0.5 * up * (1.0 - tanh * tanh) * GELU_A * (
        1.0 + 3.0 * GELU_B * up * up
    )
    du = (dm[...] * slope).astype(BF)
    act = (0.5 * up * (1.0 + tanh)).astype(BF)
    reduce_start(nt(du, wup[...]), rs2s, rs2r, RS2)
    gu[...] = tn(c_low, du).astype(BF).reshape(2, 2, 4, 64, 512)
    pair_start(gu, pu, 0)
    down = tn(act, g_ref[...]).astype(BF)
    gd[:, :, :, 0:32, :] = down[:, 0:512].reshape(2, 2, 4, 32, 512)
    gd[:, :, :, 32:64, :] = down[:, 512:1024].reshape(2, 2, 4, 32, 512)
    pair_start(gd, pd, 1)
    pair_end(gu, pu, 0)
    up_start()

    def vec_row(r, value):
        for j in range(8):
            vs[j, r : r + 1, :] = value[:, 128 * j : 128 * j + 128]

    def rows_sum(value):
        return jnp.sum(value, axis=0, keepdims=True)

    sum_up = rows_sum(du.astype(F32))
    for j in range(4):
        cvs[8 + j : 9 + j, :] = sum_up[:, 128 * j : 128 * j + 128]

    dc = reduce_end(rs2s, rs2r, RS2)
    d_hidden = g_mine + norm_back(dc, ln2_gain, hat_two, rstd_two)
    dh_all[wa] = d_hidden.astype(BF)
    gather_start(dh_all, AGD)
    pair_end(gd, pd, 1)
    vec_row(0, rows_sum(dc * hat_two))
    vec_row(1, rows_sum(dc))
    vec_row(2, rows_sum(d_hidden))
    vec_row(3, rows_sum(g_mine))
    gather_end(dh_all, AGD)
    down_start()
    up_mid()

    dh_low = dh_all[...].reshape(128, 1024)
    d_attn = nt(dh_low, wout[...]).astype(BF)
    dot_t = d_attn.astype(F32).T * attn_t[...]
    delta = jnp.concatenate(
        [
            jnp.sum(dot_t[0:64], axis=0, keepdims=True),
            jnp.sum(dot_t[64:128], axis=0, keepdims=True),
        ],
        axis=1,
    )
    do2 = jnp.concatenate(
        [jnp.where(lane < 64, d_attn, zero), jnp.where(lane >= 64, d_attn, zero)], axis=0
    )
    acc[...] = jnp.zeros_like(acc)

    def back(s):
        p = jnp.exp(scores[s] - lse)
        ds = (p * (nt(v_all[s], do2) - delta)).astype(BF)
        acc[...] += tn(k_all[s], ds)
        dkv[s, :, 0:128] = nn(ds, q2[...]).astype(BF)
        dkv[s, :, 128:256] = nn(p.astype(BF), do2).astype(BF)

    def send_half(side, y, index):
        return pltpu.make_async_remote_copy(
            src_ref=dkv.at[pl.ds(side * 8 + y * 4, 4)],
            dst_ref=pkv.at[pl.ds(y * 4, 4)],
            send_sem=cs_s.at[index],
            recv_sem=cs_r.at[index],
            device_id={"ctx": partner},
            device_id_type=MESH,
        )

    def add_half(y, index):
        send_half(other, y, index).wait_recv()

        def step(j):
            at = core * 8 + y * 4 + j
            dkv[at] = (dkv[at].astype(F32) + pkv[y * 4 + j].astype(F32)).astype(BF)

        each(0, 4, step)

    def kv_near(d):
        return to_x(dkv.at[core * 8 + row_at * 4 + lax.rem(col_at + d, 4)], rkv.at[d], RKV, d, d)

    def kv_far(d):
        return pltpu.make_async_remote_copy(
            src_ref=dkv.at[core * 8 + row_far * 4 + lax.rem(col_at + d, 4)],
            dst_ref=rkv.at[4 + d],
            send_sem=ss.at[RKV, 4 + d],
            recv_sem=rs.at[RKV, 4 + d],
            device_id={"ctx": (row_far * 4 + lax.rem(col_at + d, 4)) * 2 + core},
            device_id_type=MESH,
        )

    each(0, 4, lambda j: back(other * 8 + row_far * 4 + j))
    send_half(other, row_far, 2).start()
    each(0, 4, lambda j: back(core * 8 + row_far * 4 + j))
    each(0, 4, lambda j: back(other * 8 + row_at * 4 + j))
    send_half(other, row_at, 21).start()
    add_half(row_far, 2)
    each(0, 4, lambda d: kv_far(d).start())
    up_end()
    tree_start(ou, AGU, FWU, up_tree_mid)
    each(0, 4, lambda j: back(core * 8 + row_at * 4 + j))
    add_half(row_at, 21)
    each(1, 4, lambda d: kv_near(d).start())

    def kv_sent():
        send_half(other, row_far, 2).wait_send()
        send_half(other, row_at, 21).wait_send()
        each(0, 4, lambda d: kv_far(d).wait_send())
        each(1, 4, lambda d: kv_near(d).wait_send())

    sends.append(kv_sent)

    def kv_end():
        each(1, 4, lambda d: kv_near(d).wait_recv())
        each(0, 4, lambda d: kv_far(d).wait_recv())
        whole = dkv[slot].astype(F32)
        for d in range(1, 8):
            whole = whole + rkv[d].astype(F32)
        return whole.astype(BF)

    dq = (diagonal(acc[...]) * 0.125).T.astype(BF)
    gb[:, 64:128, :] = tn(normed[...], dq).astype(BF).reshape(16, 64, 128)
    d_out = tn(attn_low[...], dh_low).astype(BF)
    for s in range(16):
        gb[s, 0:64, :] = d_out[64 * (s % 2) : 64 * (s % 2) + 64, 128 * (s // 2) : 128 * (s // 2) + 128]
    combine_start(gb, pb, 3)
    reduce_start(nn(act, wdn[...]), rs3s, rs3r, RS3)
    combined(gb, pb, 3)
    scatter_start(gb, rb, RB)
    down_mid()

    dkv_mine = kv_end()
    both = tn(normed[...], dkv_mine).astype(BF)
    gc[:, 0:64, :] = both[:, 0:128].reshape(16, 64, 128)
    gc[:, 64:128, :] = both[:, 128:256].reshape(16, 64, 128)
    combine_start(gc, pc, 4)
    d_qkv = jnp.concatenate([dq, dkv_mine], axis=1)
    da = nt(d_qkv, wqkv[...])
    reduce_start(da, rs4s, rs4r, RS4)
    combined(gc, pc, 4)
    scatter_start(gc, rc, RC)
    down_end()
    tree_start(od, AGW, FWW, down_tree_mid)
    up_tree_mid(ou, AGU, FWU)
    vec_row(4, rows_sum(da * xhat_all[...]))
    vec_row(5, rows_sum(da))
    for j in range(8):
        vs[j, 6:8, :] = jnp.zeros((2, 128), F32)
    each(1, 8, lambda d: to_wa(vs.at[lax.rem(wa + d, 8)], vr.at[d], RS5, d).start())
    sends.append(lambda: wa_sent(vs, RS5))
    cvs[12:13, :] = rows_sum(dq.astype(F32))
    cvs[13:14, :] = rows_sum(dkv_mine[:, 128:256].astype(F32))
    cvs[14:16, :] = jnp.zeros((2, 128), F32)
    ob[slot] = scatter_end(gb, rb, RB)
    spread_start(ob, AGB, FWB)

    hat_one, rstd_one = normalize(x_mine)
    d_first = reduce_end(rs4s, rs4r, RS4)
    g_all[wa] = (d_hidden + norm_back(d_first, ln1_gain, hat_one, rstd_one)).astype(BF)
    gather_start(g_all, AGG)

    each(1, 8, lambda d: to_wa(vs.at[lax.rem(wa + d, 8)], vr.at[d], RS5, d).wait_recv())
    vec_sum = vs[wa]
    for d in range(1, 8):
        vec_sum = vec_sum + vr[d]
    cvs[0:8, :] = vec_sum
    cvr[ctx] = cvs[...]

    def to_ctx(dst, d):
        return pltpu.make_async_remote_copy(
            src_ref=cvs,
            dst_ref=cvr.at[dst],
            send_sem=cs_s.at[5 + d],
            recv_sem=cs_r.at[5 + d],
            device_id={"ctx": lax.rem(ctx + d, 16)},
            device_id_type=MESH,
        )

    each(1, 16, lambda d: to_ctx(ctx, d).start())
    sends.append(lambda: each(1, 16, lambda d: to_ctx(ctx, d).wait_send()))
    oc[slot] = scatter_end(gc, rc, RC)
    spread_start(oc, AGCC, FWC)
    down_tree_mid(od, AGW, FWW)
    tree_pass(ou, AGU, FWU)
    y_all[wa] = (hidden + reduce_end(rs3s, rs3r, RS3) + b_down).astype(BF)
    gather_start(y_all, AGY)
    each(1, 16, lambda d: to_ctx(lax.rem(ctx + 16 - d, 16), d).wait_recv())
    ctx_sum = cvr[0]
    for i in range(1, 16):
        ctx_sum = ctx_sum + cvr[i]
    ctx_out[...] = ctx_sum[8:16, :]
    vall[wa] = ctx_sum[0:8, :]
    gather_start(vall, AGV)
    spread_pass(ob, AGB, FWB)
    tree_end(ou, AGU, FWU)
    ou_out[...] = ou[...].astype(F32).reshape(1024, 512)
    tree_pass(od, AGW, FWW)
    tree_end(od, AGW, FWW)
    od_out[:, 0:512] = od[:, 0:32, :].astype(F32).reshape(512, 512)
    od_out[:, 512:1024] = od[:, 32:64, :].astype(F32).reshape(512, 512)
    spread_pass(oc, AGCC, FWC)
    gather_end(g_all, AGG)
    gin_out[...] = g_all[...].reshape(128, 1024)
    spread_end(ob, AGB, FWB)
    ob_out[...] = ob[...]
    gather_end(y_all, AGY)
    y_out[...] = y_all[...].reshape(128, 1024)
    gather_end(vall, AGV)
    vec_out[...] = vall[...]
    spread_end(oc, AGCC, FWC)
    oc_out[...] = oc[...]

    for sent in sends:
        sent()


def finish(
    y_ref,
    gin_ref,
    ou_ref,
    od_ref,
    ob_ref,
    oc_ref,
    vec_ref,
    ctx_ref,
    y_out,
    gin_out,
    ln1g_out,
    ln1b_out,
    gqkv_out,
    bqv_out,
    gwo_out,
    bout_out,
    ln2g_out,
    ln2b_out,
    gup_out,
    bup_out,
    gdn_out,
    bdown_out,
    gin,
    gqkv,
    gwo,
    sems,
):
    copies = []

    def leave(src, dst):
        copies.append(pltpu.make_async_copy(src, dst, sems.at[len(copies)]))
        copies[-1].start()

    leave(y_ref, y_out)
    leave(ou_ref, gup_out)
    leave(od_ref, gdn_out)
    gin[...] = gin_ref[...].astype(F32)
    leave(gin, gin_out)
    for s in range(16):
        gwo[64 * (s % 2) : 64 * (s % 2) + 64, 128 * (s // 2) : 128 * (s // 2) + 128] = ob_ref[
            s, 0:64, :
        ].astype(F32)
    leave(gwo, gwo_out)
    gqkv[0] = ob_ref[:, 64:128, :].astype(F32).reshape(1024, 128)
    leave(gqkv.at[0], gqkv_out.at[0])
    gqkv[1] = oc_ref[:, 0:64, :].astype(F32).reshape(1024, 128)
    leave(gqkv.at[1], gqkv_out.at[1])
    gqkv[2] = oc_ref[:, 64:128, :].astype(F32).reshape(1024, 128)
    leave(gqkv.at[2], gqkv_out.at[2])
    for r, out in enumerate((ln2g_out, ln2b_out, bout_out, bdown_out, ln1g_out, ln1b_out)):
        out[...] = vec_ref[:, r, :]
    bup_out[...] = ctx_ref[0:4, :]
    bqv_out[...] = ctx_ref[4:6, :]
    for copy in copies:
        copy.wait()


def body(
    layer_input,
    block_order,
    seg_ids,
    cotangent,
    ln1_gain,
    ln1_bias,
    w_qkv,
    b_qv,
    w_out,
    b_out,
    ln2_gain,
    ln2_bias,
    w_up,
    b_up,
    w_down,
    b_down,
):
    vmem = pl.BlockSpec(memory_space=pltpu.VMEM)
    hbm = pl.BlockSpec(memory_space=pl.ANY)
    far = pl.BlockSpec(memory_space=pltpu.HBM)

    def stay(operand):
        return pltpu.with_memory_space_constraint(operand, pltpu.HBM)

    def bf(*shape):
        return pltpu.VMEM(shape, BF)

    def f32(*shape):
        return pltpu.VMEM(shape, F32)

    outs = pl.pallas_call(
        layer,
        out_shape=(
            jax.ShapeDtypeStruct((128, 1024), BF),
            jax.ShapeDtypeStruct((128, 1024), BF),
            jax.ShapeDtypeStruct((1024, 512), F32),
            jax.ShapeDtypeStruct((512, 1024), F32),
            jax.ShapeDtypeStruct((16, 128, 128), BF),
            jax.ShapeDtypeStruct((16, 128, 128), BF),
            jax.ShapeDtypeStruct((8, 8, 128), F32),
            jax.ShapeDtypeStruct((8, 128), F32),
        ),
        in_specs=[far] * 16,
        out_specs=(vmem,) * 8,
        scratch_shapes=[
            pltpu.SMEM((32,), jnp.int32),
            pltpu.VMEM((16, 128), jnp.int32),
            bf(128, 1024),
            bf(128, 1024),
            bf(8, 128),
            bf(8, 128),
            bf(8, 128),
            bf(8, 128),
            bf(8, 128),
            bf(8, 128),
            bf(4, 128),
            bf(2, 128),
            bf(1024, 384),
            bf(128, 1024),
            bf(1024, 512),
            bf(512, 1024),
            pltpu.SemaphoreType.DMA((18,)),
            f32(128, 1024),
            bf(128, 1024),
            bf(16, 128, 128),
            bf(16, 128, 128),
            bf(256, 128),
            f32(16, 128, 256),
            f32(128, 256),
            f32(128, 128),
            bf(128, 128),
            bf(8, 16, 1024),
            bf(8, 16, 1024),
            bf(8, 16, 1024),
            f32(128, 512),
            bf(8, 16, 1024),
            bf(8, 16, 1024),
            bf(8, 16, 1024),
            bf(8, 16, 1024),
            bf(8, 16, 1024),
            bf(8, 16, 1024),
            bf(16, 128, 256),
            bf(8, 128, 256),
            bf(8, 128, 256),
            bf(2, 2, 4, 64, 512),
            bf(2, 4, 64, 512),
            bf(4, 2, 64, 512),
            bf(2, 64, 512),
            bf(64, 512),
            bf(16, 64, 512),
            bf(2, 2, 4, 64, 512),
            bf(2, 4, 64, 512),
            bf(4, 64, 512),
            bf(4, 64, 512),
            bf(4, 64, 512),
            bf(16, 64, 512),
            bf(16, 128, 128),
            bf(8, 128, 128),
            bf(8, 128, 128),
            bf(16, 128, 128),
            bf(16, 128, 128),
            bf(8, 128, 128),
            bf(8, 128, 128),
            bf(16, 128, 128),
            bf(8, 16, 1024),
            bf(8, 16, 1024),
            bf(8, 16, 1024),
            f32(8, 8, 128),
            f32(8, 8, 128),
            f32(8, 8, 128),
            f32(16, 128),
            f32(16, 16, 128),
            pltpu.SemaphoreType.DMA((NSEM, 8)),
            pltpu.SemaphoreType.DMA((NSEM, 8)),
            pltpu.SemaphoreType.DMA((22,)),
            pltpu.SemaphoreType.DMA((22,)),
        ],
        compiler_params=pltpu.CompilerParams(
            collective_id=0, has_side_effects=True, vmem_limit_bytes=32 << 20
        ),
        name="decoder",
    )(
        stay(block_order),
        stay(seg_ids.reshape(16, 128)),
        stay(layer_input),
        stay(cotangent),
        *(
            stay(v.reshape(-1, 128))
            for v in (ln1_gain, ln1_bias, b_out, ln2_gain, ln2_bias, b_down, b_up)
        ),
        stay(b_qv),
        stay(w_qkv.transpose(1, 0, 2)),
        stay(w_out),
        stay(w_up),
        stay(w_down),
    )
    shapes = (
        ((128, 1024), BF),
        ((128, 1024), F32),
        ((8, 128), F32),
        ((8, 128), F32),
        ((3, 1024, 128), F32),
        ((2, 128), F32),
        ((128, 1024), F32),
        ((8, 128), F32),
        ((8, 128), F32),
        ((8, 128), F32),
        ((1024, 512), F32),
        ((4, 128), F32),
        ((512, 1024), F32),
        ((8, 128), F32),
    )
    large = (0, 1, 4, 6, 10, 12)
    done = list(
        pl.pallas_call(
            finish,
            out_shape=tuple(jax.ShapeDtypeStruct(*shape) for shape in shapes),
            in_specs=[vmem] * 8,
            out_specs=tuple(hbm if i in large else vmem for i in range(14)),
            scratch_shapes=[
                f32(128, 1024),
                f32(3, 1024, 128),
                f32(128, 1024),
                pltpu.SemaphoreType.DMA((14,)),
            ],
            compiler_params=pltpu.CompilerParams(vmem_limit_bytes=24 << 20),
            name="finish",
        )(*outs)
    )
    for i in (2, 3, 7, 8, 9, 11, 13):
        done[i] = done[i].reshape(-1)
    done[4] = done[4].transpose(1, 0, 2)
    return tuple(done)


def solution(mesh):
    placed = (
        P("ctx", None),
        P(),
        P(),
        P("ctx", None),
        P(),
        P(),
        P(None, None, "wa"),
        P(None, "wa"),
        P("wa", None),
        P(),
        P(),
        P(),
        P(None, "wa"),
        P("wa"),
        P("wa", None),
        P(),
    )
    return jax.shard_map(
        body,
        mesh=mesh,
        in_specs=placed,
        out_specs=(
            P("ctx", None),
            P("ctx", None),
            P(),
            P(),
            P(None, None, "wa"),
            P(None, "wa"),
            P("wa", None),
            P(),
            P(),
            P(),
            P(None, "wa"),
            P("wa"),
            P("wa", None),
            P(),
        ),
        check_vma=False,
    )
```

```python
import jax
import jax.numpy as jnp
from jax import lax
from jax.experimental import pallas as pl
from jax.experimental.pallas import tpu as pltpu
from jax.sharding import PartitionSpec as P

F32 = jnp.float32
BF = jnp.bfloat16
MESH = pl.DeviceIdType.MESH
GELU_A = 0.7978845608028654
GELU_B = 0.044715

(
    KK,
    KKF,
    VV,
    VVF,
    RS1,
    AGC,
    RS2,
    RS3,
    AGD,
    AGY,
    RKV,
    RUX,
    RUY,
    AGU,
    FWU,
    RDY,
    RDX,
    AGW,
    AGX,
    FWW,
    RB,
    AGB,
    FWB,
    RC,
    AGCC,
    FWC,
    RS4,
    RS5,
    AGG,
    AGV,
    NSEM,
) = range(31)


def nn(a, b):
    return lax.dot_general(a, b, (((1,), (0,)), ((), ())), preferred_element_type=F32)


def nt(a, b):
    return lax.dot_general(a, b, (((1,), (1,)), ((), ())), preferred_element_type=F32)


def tn(a, b):
    return lax.dot_general(a, b, (((0,), (0,)), ((), ())), preferred_element_type=F32)


def normalize(rows):
    centered = rows - jnp.mean(rows, -1, keepdims=True)
    rstd = lax.rsqrt(jnp.mean(centered * centered, -1, keepdims=True) + 1e-05)
    return centered * rstd, rstd


def norm_back(grad, gain, xhat, rstd):
    gx = grad * gain
    return rstd * (
        gx - jnp.mean(gx, -1, keepdims=True) - xhat * jnp.mean(gx * xhat, -1, keepdims=True)
    )


def layer(
    order_hbm,
    seg_hbm,
    x_hbm,
    g_hbm,
    ln1g_hbm,
    ln1b_hbm,
    bout_hbm,
    ln2g_hbm,
    ln2b_hbm,
    bdown_hbm,
    bup_hbm,
    bqv_hbm,
    wqkv_hbm,
    wout_hbm,
    wup_hbm,
    wdn_hbm,
    y_out,
    gin_out,
    ou_out,
    od_out,
    ob_out,
    oc_out,
    vec_out,
    ctx_out,
    order_ref,
    seg_ref,
    x_ref,
    g_ref,
    ln1g_ref,
    ln1b_ref,
    bout_ref,
    ln2g_ref,
    ln2b_ref,
    bdown_ref,
    bup_ref,
    bqv_ref,
    wqkv,
    wout,
    wup,
    wdn,
    load_sem,
    xhat_all,
    normed,
    k_all,
    v_all,
    q2,
    scores,
    acc,
    attn_t,
    attn_low,
    rs1s,
    rs1r,
    c_all,
    dm,
    rs2s,
    rs2r,
    rs3s,
    rs3r,
    dh_all,
    y_all,
    dkv,
    pkv,
    rkv,
    gu,
    pu,
    rux,
    tu,
    ruy,
    ou,
    gd,
    pd,
    rdy,
    td,
    rdx,
    od,
    gb,
    pb,
    rb,
    ob,
    gc,
    pc,
    rc,
    oc,
    rs4s,
    rs4r,
    g_all,
    vs,
    vr,
    vall,
    cvs,
    cvr,
    ss,
    rs,
    cs_s,
    cs_r,
):
    ctx = lax.axis_index("ctx")
    wa = lax.axis_index("wa")
    core = lax.rem(ctx, 2)
    chip = lax.div(ctx, 2)
    other = 1 - core
    row_at = lax.div(chip, 4)
    col_at = lax.rem(chip, 4)
    row_far = 1 - row_at
    slot = core * 8 + chip
    partner = chip * 2 + other

    def to_wa(src, dst, kind, d):
        return pltpu.make_async_remote_copy(
            src_ref=src,
            dst_ref=dst,
            send_sem=ss.at[kind, d],
            recv_sem=rs.at[kind, d],
            device_id={"wa": lax.rem(wa + d, 8)},
            device_id_type=MESH,
        )

    def to_chip(src, dst, kind, d):
        return pltpu.make_async_remote_copy(
            src_ref=src,
            dst_ref=dst,
            send_sem=ss.at[kind, d],
            recv_sem=rs.at[kind, d],
            device_id={"ctx": lax.rem(chip + d, 8) * 2 + core},
            device_id_type=MESH,
        )

    def to_partner(src, dst, kind, d):
        return pltpu.make_async_remote_copy(
            src_ref=src,
            dst_ref=dst,
            send_sem=ss.at[kind, d],
            recv_sem=rs.at[kind, d],
            device_id={"ctx": partner},
            device_id_type=MESH,
        )

    sends = []
    arrivals = {}

    def each(low, high, step):
        @pl.loop(low, high)
        def _(d):
            step(d)

    loads = [
        pltpu.make_async_copy(
            wqkv_hbm.at[i], wqkv.at[:, pl.ds(128 * i, 128)], load_sem.at[i]
        )
        for i in range(3)
    ] + [
        pltpu.make_async_copy(wdn_hbm, wdn, load_sem.at[3]),
        pltpu.make_async_copy(wout_hbm, wout, load_sem.at[4]),
        pltpu.make_async_copy(wup_hbm, wup, load_sem.at[5]),
        pltpu.make_async_copy(x_hbm, x_ref, load_sem.at[6]),
        pltpu.make_async_copy(g_hbm, g_ref, load_sem.at[7]),
    ]
    small = [
        pltpu.make_async_copy(src, dst, load_sem.at[8 + i])
        for i, (src, dst) in enumerate(
            (
                (ln1g_hbm, ln1g_ref),
                (ln1b_hbm, ln1b_ref),
                (bqv_hbm, bqv_ref),
                (order_hbm, order_ref),
                (seg_hbm, seg_ref),
                (bout_hbm, bout_ref),
                (ln2g_hbm, ln2g_ref),
                (ln2b_hbm, ln2b_ref),
                (bdown_hbm, bdown_ref),
                (bup_hbm, bup_ref),
            )
        )
    ]
    loads[6].start()
    for load in small:
        load.start()
    for i in (1, 2, 0, 7, 3, 4, 5):
        loads[i].start()

    def combine(buf, kept, index):
        return pltpu.make_async_remote_copy(
            src_ref=buf.at[pl.ds(pl.multiple_of(other * 8, 8), 8)],
            dst_ref=kept,
            send_sem=cs_s.at[index],
            recv_sem=cs_r.at[index],
            device_id={"ctx": partner},
            device_id_type=MESH,
        )

    def combine_start(buf, kept, index):
        combine(buf, kept, index).start()
        sends.append(lambda: combine(buf, kept, index).wait_send())
        arrivals[100 + index] = lambda: combined(buf, kept, index)

    def combined(buf, kept, index):
        arrivals.pop(100 + index)
        combine(buf, kept, index).wait_recv()

        @pl.loop(0, 8)
        def _(j):
            buf[core * 8 + j] = (buf[core * 8 + j].astype(F32) + kept[j].astype(F32)).astype(BF)

    def scatter_start(buf, recv, kind):
        sends.append(
            lambda: each(
                1, 8, lambda d: to_chip(buf.at[slot], buf.at[slot], kind, d).wait_send()
            )
        )
        arrivals[kind] = lambda: scatter_end(buf, recv, kind)
        each(
            1,
            8,
            lambda d: to_chip(
                buf.at[core * 8 + lax.rem(chip + d, 8)], recv.at[d], kind, d
            ).start(),
        )

    def scatter_end(buf, recv, kind):
        arrivals.pop(kind)
        each(
            1,
            8,
            lambda d: to_chip(
                buf.at[core * 8 + lax.rem(chip + d, 8)], recv.at[d], kind, d
            ).wait_recv(),
        )
        whole = buf[slot].astype(F32)
        for d in range(1, 8):
            whole = whole + recv[d].astype(F32)
        return whole.astype(BF)

    def spread_start(buf, kind, forward):
        sends.append(lambda: spread_sent(buf, kind, forward))
        arrivals[kind] = lambda: (
            spread_pass(buf, kind, forward),
            spread_end(buf, kind, forward),
        )
        to_partner(buf.at[slot], buf.at[slot], kind, 0).start()
        each(1, 8, lambda d: to_chip(buf.at[slot], buf.at[slot], kind, d).start())

    def spread_sent(buf, kind, forward):
        to_partner(buf.at[slot], buf.at[slot], kind, 0).wait_send()

        def sent(d):
            to_chip(buf.at[slot], buf.at[slot], kind, d).wait_send()
            to_partner(buf.at[slot], buf.at[slot], forward, d).wait_send()

        each(1, 8, sent)

    def spread_pass(buf, kind, forward):
        arrivals[kind] = lambda: spread_end(buf, kind, forward)

        def step(d):
            s = core * 8 + lax.rem(chip + 8 - d, 8)
            to_chip(buf.at[slot], buf.at[s], kind, d).wait_recv()
            to_partner(buf.at[s], buf.at[s], forward, d).start()

        each(1, 8, step)

    def spread_end(buf, kind, forward):
        arrivals.pop(kind)
        s = other * 8 + chip
        to_partner(buf.at[s], buf.at[s], kind, 0).wait_recv()

        def step(d):
            t = other * 8 + lax.rem(chip + 8 - d, 8)
            to_partner(buf.at[t], buf.at[t], forward, d).wait_recv()

        each(1, 8, step)

    def reduce_start(part, send, recv, kind):
        send[...] = part.astype(BF).reshape(8, 16, 1024)
        each(1, 8, lambda d: to_wa(send.at[lax.rem(wa + d, 8)], recv.at[d], kind, d).start())
        sends.append(lambda: wa_sent(send, kind))
        arrivals[kind] = lambda: reduce_end(send, recv, kind)

    def reduce_end(send, recv, kind):
        arrivals.pop(kind)
        each(1, 8, lambda d: to_wa(send.at[lax.rem(wa + d, 8)], recv.at[d], kind, d).wait_recv())
        whole = send[wa].astype(F32)
        for d in range(1, 8):
            whole = whole + recv[d].astype(F32)
        return whole

    def gather_start(buf, kind):
        each(1, 8, lambda d: to_wa(buf.at[wa], buf.at[wa], kind, d).start())
        sends.append(lambda: wa_sent(buf, kind))
        arrivals[kind] = lambda: gather_end(buf, kind)

    def wa_sent(buf, kind):
        each(1, 8, lambda d: to_wa(buf.at[wa], buf.at[wa], kind, d).wait_send())

    def gather_end(buf, kind):
        arrivals.pop(kind)
        each(
            1,
            8,
            lambda d: to_wa(buf.at[wa], buf.at[lax.rem(wa + 8 - d, 8)], kind, d).wait_recv(),
        )

    def to_x(src, dst, kind, at, d):
        return pltpu.make_async_remote_copy(
            src_ref=src,
            dst_ref=dst,
            send_sem=ss.at[kind, at],
            recv_sem=rs.at[kind, at],
            device_id={"ctx": (row_at * 4 + lax.rem(col_at + d, 4)) * 2 + core},
            device_id_type=MESH,
        )

    def to_y(src, dst, kind, at):
        return pltpu.make_async_remote_copy(
            src_ref=src,
            dst_ref=dst,
            send_sem=ss.at[kind, at],
            recv_sem=rs.at[kind, at],
            device_id={"ctx": lax.rem(chip + 4, 8) * 2 + core},
            device_id_type=MESH,
        )

    def pair(buf, kept, index):
        return pltpu.make_async_remote_copy(
            src_ref=buf.at[other],
            dst_ref=kept,
            send_sem=cs_s.at[index],
            recv_sem=cs_r.at[index],
            device_id={"ctx": partner},
            device_id_type=MESH,
        )

    def pair_start(buf, kept, index):
        pair(buf, kept, index).start()
        sends.append(lambda: pair(buf, kept, index).wait_send())
        arrivals[100 + index] = lambda: pair_end(buf, kept, index)

    def pair_end(buf, kept, index):
        arrivals.pop(100 + index)
        pair(buf, kept, index).wait_recv()

        @pl.loop(0, 8)
        def _(j):
            at = (lax.div(j, 4), lax.rem(j, 4))
            buf[(core, *at)] = (buf[(core, *at)].astype(F32) + kept[at].astype(F32)).astype(BF)

    def up_x(d):
        return to_x(gu.at[core, :, lax.rem(col_at + d, 4)], rux.at[d], RUX, d, d)

    def up_start():
        each(1, 4, lambda d: up_x(d).start())
        sends.append(lambda: each(1, 4, lambda d: up_x(d).wait_send()))
        arrivals[RUX] = up_mid

    def up_mid():
        arrivals.pop(RUX)
        each(1, 4, lambda d: up_x(d).wait_recv())
        for y in range(2):
            whole = gu[core, y, col_at].astype(F32)
            for d in range(1, 4):
                whole = whole + rux[d, y].astype(F32)
            tu[y] = whole.astype(BF)
        to_y(tu.at[row_far], ruy, RUY, 0).start()
        sends.append(lambda: to_y(tu.at[row_far], ruy, RUY, 0).wait_send())
        arrivals[RUY] = up_end

    def up_end():
        arrivals.pop(RUY)
        to_y(tu.at[row_far], ruy, RUY, 0).wait_recv()
        ou[slot] = (tu[row_at].astype(F32) + ruy[...].astype(F32)).astype(BF)

    def down_y():
        return to_y(gd.at[core, row_far], rdy, RDY, 0)

    def down_x(d):
        return to_x(td.at[lax.rem(col_at + d, 4)], rdx.at[d], RDX, d, d)

    def down_start():
        down_y().start()
        sends.append(lambda: down_y().wait_send())
        arrivals[RDY] = down_mid

    def down_mid():
        arrivals.pop(RDY)
        down_y().wait_recv()
        for x in range(4):
            td[x] = (gd[core, row_at, x].astype(F32) + rdy[x].astype(F32)).astype(BF)
        each(1, 4, lambda d: down_x(d).start())
        sends.append(lambda: each(1, 4, lambda d: down_x(d).wait_send()))
        arrivals[RDX] = down_end

    def down_end():
        arrivals.pop(RDX)
        each(1, 4, lambda d: down_x(d).wait_recv())
        whole = td[col_at].astype(F32)
        for d in range(1, 4):
            whole = whole + rdx[d].astype(F32)
        od[slot] = whole.astype(BF)

    def place(side, y, d):
        return side * 8 + y * 4 + lax.rem(col_at + 4 - d, 4)

    def tree_start(buf, kind, forward, middle, sent_all=None):
        own = buf.at[slot]
        to_y(own, own, kind, 4).start()
        each(1, 4, lambda d: to_x(own, own, kind, d, d).start())
        to_partner(own, own, kind, 0).start()

        def sent():
            each(0, 8, lambda d: to_y(own, own, kind, d).wait_send())
            each(1, 8, lambda d: to_y(own, own, forward, d).wait_send())

        sends.append(sent if sent_all is None else lambda: sent_all(buf, kind, forward))
        arrivals[kind] = lambda: (
            middle(buf, kind, forward),
            tree_pass(buf, kind, forward),
            tree_end(buf, kind, forward),
        )

    def take(buf, s, kind, forward, d):
        at = buf.at[s]
        to_y(at, at, kind, d).wait_recv()
        to_partner(at, at, forward, d).start()

    def up_tree_mid(buf, kind, forward):
        s = place(core, row_far, 0)
        take(buf, s, kind, forward, 4)
        each(1, 4, lambda d: to_x(buf.at[s], buf.at[s], kind, 4 + d, d).start())
        each(1, 4, lambda d: take(buf, place(core, row_at, d), kind, forward, d))
        arrivals[kind] = lambda: (tree_pass(buf, kind, forward), tree_end(buf, kind, forward))

    def down_tree_mid(buf, kind, forward):
        def step(d):
            s = place(core, row_at, d)
            take(buf, s, kind, forward, d)
            top = buf.at[s, pl.ds(0, 32)]
            to_y(top, top, kind, 4 + d).start()

        each(1, 4, step)
        s = place(core, row_far, 0)
        take(buf, s, kind, forward, 4)
        low = buf.at[s, pl.ds(32, 32)]
        each(1, 4, lambda d: to_x(low, low, AGX, d, d).start())
        arrivals[kind] = lambda: (down_tree_pass(buf, kind, forward), tree_end(buf, kind, forward))

    def down_tree_pass(buf, kind, forward):
        def step(d):
            s = place(core, row_far, d)
            top = buf.at[s, pl.ds(0, 32)]
            low = buf.at[s, pl.ds(32, 32)]
            to_y(top, top, kind, 4 + d).wait_recv()
            to_y(low, low, AGX, d).wait_recv()
            to_partner(buf.at[s], buf.at[s], forward, 4 + d).start()

        each(1, 4, step)
        arrivals[kind] = lambda: tree_end(buf, kind, forward)

    def down_tree_sent(buf, kind, forward):
        own = buf.at[slot]
        part = buf.at[slot, pl.ds(0, 32)]
        each(0, 5, lambda d: to_y(own, own, kind, d).wait_send())
        each(1, 8, lambda d: to_y(own, own, forward, d).wait_send())
        each(5, 8, lambda d: to_y(part, part, kind, d).wait_send())
        each(1, 4, lambda d: to_y(part, part, AGX, d).wait_send())

    def tree_pass(buf, kind, forward):
        each(1, 4, lambda d: take(buf, place(core, row_far, d), kind, forward, 4 + d))
        arrivals[kind] = lambda: tree_end(buf, kind, forward)

    def tree_end(buf, kind, forward):
        arrivals.pop(kind)

        def landed(s, sem, d):
            to_partner(buf.at[s], buf.at[s], sem, d).wait_recv()

        landed(other * 8 + chip, kind, 0)
        landed(place(other, row_far, 0), forward, 4)

        def step(d):
            landed(place(other, row_at, d), forward, d)
            landed(place(other, row_far, d), forward, 4 + d)

        each(1, 4, step)

    barrier = pltpu.get_barrier_semaphore()
    each(
        1,
        16,
        lambda d: pl.semaphore_signal(
            barrier, inc=1, device_id={"ctx": lax.rem(ctx + d, 16)}, device_id_type=MESH
        ),
    )
    each(
        1,
        8,
        lambda d: pl.semaphore_signal(
            barrier, inc=1, device_id={"wa": lax.rem(wa + d, 8)}, device_id_type=MESH
        ),
    )

    def vector(ref):
        rows = ref[...].astype(F32)
        return jnp.concatenate([rows[j : j + 1, :] for j in range(rows.shape[0])], axis=1)

    loads[6].wait()
    xhat, _ = normalize(x_ref[...].astype(F32))
    xhat_all[...] = xhat
    for load in small:
        load.wait()
    ln1_gain = vector(ln1g_ref)
    ln1_bias = vector(ln1b_ref)
    b_qv = bqv_ref[...].astype(F32)
    normed[...] = (xhat * ln1_gain + ln1_bias).astype(BF)
    for i in range(1, 3):
        loads[i].wait()
    proj = nn(normed[...], wqkv[:, 128:384])
    k_all[slot] = proj[:, 0:128].astype(BF)
    v_all[slot] = (proj[:, 128:256] + b_qv[1:2, :]).astype(BF)
    pl.semaphore_wait(barrier, 22)

    spread_start(k_all, KK, KKF)
    spread_start(v_all, VV, VVF)

    loads[0].wait()
    q_low = (nn(normed[...], wqkv[:, 0:128]) + b_qv[0:1, :]).astype(BF) * jnp.asarray(0.125, BF)
    lane = lax.broadcasted_iota(jnp.int32, (128, 128), 1)
    zero = jnp.zeros((128, 128), BF)
    q2[0:128, :] = jnp.where(lane < 64, q_low, zero)
    q2[128:256, :] = jnp.where(lane >= 64, q_low, zero)

    lanes = lax.broadcasted_iota(jnp.int32, (1, 256), 1)
    lanes = jnp.where(lanes >= 128, lanes - 128, lanes)
    q_pos = jnp.where(
        lanes < 64, lanes + 64 * order_ref[2 * ctx], lanes - 64 + 64 * order_ref[2 * ctx + 1]
    )
    seg = seg_ref[...]
    one = jnp.ones(seg.shape, F32)
    none = jnp.zeros(seg.shape, F32)

    def count(test):
        part = jnp.sum(jnp.where(test, one, none), axis=0, keepdims=True)
        return jnp.sum(part, axis=1, keepdims=True)

    first_end = count(seg < 1)
    second_end = count(seg < 2)
    q_float = q_pos.astype(F32)
    q_first = jnp.where(
        q_float >= second_end,
        second_end,
        jnp.where(q_float >= first_end, first_end, jnp.zeros_like(q_float)),
    ).astype(jnp.int32)
    row = lax.broadcasted_iota(jnp.int32, (128, 256), 0)

    def score(s, top):
        keys = k_all[s]
        owner = 2 * lax.rem(s, 8) + lax.div(s, 8)
        k_pos = jnp.where(
            row < 64, row + 64 * order_ref[2 * owner], row - 64 + 64 * order_ref[2 * owner + 1]
        )
        allowed = (k_pos <= q_pos) & (k_pos >= q_first)
        masked = jnp.where(allowed, nt(keys, q2[...]), -1e30)
        scores[s] = masked
        return jnp.maximum(top, jnp.max(masked.reshape(16, 8, 256), axis=0))

    top = score(slot, jnp.full((8, 256), -1e30, F32))
    loads[7].wait()
    loads[3].wait()
    dm[...] = nt(g_ref[...], wdn[...])
    b_out = vector(bout_ref)
    ln2_gain = vector(ln2g_ref)
    ln2_bias = vector(ln2b_ref)
    b_down = vector(bdown_ref)
    b_up = vector(bup_ref)

    def near(d, top):
        s = core * 8 + lax.rem(chip + 8 - d, 8)
        to_chip(k_all.at[slot], k_all.at[s], KK, d).wait_recv()
        to_partner(k_all.at[s], k_all.at[s], KKF, d).start()
        return score(s, top)

    top = lax.fori_loop(1, 8, near, top)
    to_partner(k_all.at[slot], k_all.at[other * 8 + chip], KK, 0).wait_recv()
    top = score(other * 8 + chip, top)
    spread_pass(v_all, VV, VVF)

    def far(d, top):
        s = other * 8 + lax.rem(chip + 8 - d, 8)
        to_partner(k_all.at[s], k_all.at[s], KKF, d).wait_recv()
        return score(s, top)

    top = lax.fori_loop(1, 8, far, top)
    arrivals.pop(KK)
    spread_end(v_all, VV, VVF)
    top = jnp.max(top, axis=0, keepdims=True)
    acc[...] = jnp.zeros_like(acc)

    def mix(s, total):
        p = jnp.exp(scores[s] - top)
        acc[...] += tn(v_all[s], p.astype(BF))
        return total + jnp.sum(p.reshape(16, 8, 256), axis=0)

    total = lax.fori_loop(0, 16, mix, jnp.zeros((8, 256), F32), unroll=16)
    total = jnp.sum(total, axis=0, keepdims=True)
    lse = top + jnp.log(total)
    half = lax.broadcasted_iota(jnp.int32, (128, 128), 0) < 64

    def diagonal(both):
        return jnp.where(half, both[:, 0:128], both[:, 128:256])

    raw_t = diagonal(acc[...] / total)
    attn_t[...] = raw_t
    attn_low[...] = raw_t.T.astype(BF)

    loads[4].wait()
    reduce_start(nn(attn_low[...], wout[...]), rs1s, rs1r, RS1)
    mine = pl.ds(pl.multiple_of(wa * 16, 16), 16)
    x_mine = x_ref[mine, :].astype(F32)
    g_mine = g_ref[mine, :].astype(F32)
    hidden = x_mine + reduce_end(rs1s, rs1r, RS1) + b_out
    hat_two, rstd_two = normalize(hidden)
    c_all[wa] = (hat_two * ln2_gain + ln2_bias).astype(BF)
    gather_start(c_all, AGC)
    loads[5].wait()
    gather_end(c_all, AGC)

    c_low = c_all[...].reshape(128, 1024)
    up = nn(c_low, wup[...]) + b_up
    tanh = jnp.tanh(GELU_A * (up + GELU_B * up * up * up))
    slope = 0.5 * (1.0 + tanh) + 0.5 * up * (1.0 - tanh * tanh) * GELU_A * (
        1.0 + 3.0 * GELU_B * up * up
    )
    du = (dm[...] * slope).astype(BF)
    act = (0.5 * up * (1.0 + tanh)).astype(BF)
    reduce_start(nt(du, wup[...]), rs2s, rs2r, RS2)
    gu[...] = tn(c_low, du).astype(BF).reshape(2, 2, 4, 64, 512)
    pair_start(gu, pu, 0)
    down = tn(act, g_ref[...]).astype(BF)
    gd[:, :, :, 0:32, :] = down[:, 0:512].reshape(2, 2, 4, 32, 512)
    gd[:, :, :, 32:64, :] = down[:, 512:1024].reshape(2, 2, 4, 32, 512)
    pair_start(gd, pd, 1)
    pair_end(gu, pu, 0)
    up_start()

    def vec_row(r, value):
        for j in range(8):
            vs[j, r : r + 1, :] = value[:, 128 * j : 128 * j + 128]

    def rows_sum(value):
        return jnp.sum(value, axis=0, keepdims=True)

    sum_up = rows_sum(du.astype(F32))
    for j in range(4):
        cvs[8 + j : 9 + j, :] = sum_up[:, 128 * j : 128 * j + 128]

    dc = reduce_end(rs2s, rs2r, RS2)
    d_hidden = g_mine + norm_back(dc, ln2_gain, hat_two, rstd_two)
    dh_all[wa] = d_hidden.astype(BF)
    gather_start(dh_all, AGD)
    pair_end(gd, pd, 1)
    vec_row(0, rows_sum(dc * hat_two))
    vec_row(1, rows_sum(dc))
    vec_row(2, rows_sum(d_hidden))
    vec_row(3, rows_sum(g_mine))
    gather_end(dh_all, AGD)
    down_start()
    up_mid()

    dh_low = dh_all[...].reshape(128, 1024)
    d_attn = nt(dh_low, wout[...]).astype(BF)
    dot_t = d_attn.astype(F32).T * attn_t[...]
    delta = jnp.concatenate(
        [
            jnp.sum(dot_t[0:64], axis=0, keepdims=True),
            jnp.sum(dot_t[64:128], axis=0, keepdims=True),
        ],
        axis=1,
    )
    do2 = jnp.concatenate(
        [jnp.where(lane < 64, d_attn, zero), jnp.where(lane >= 64, d_attn, zero)], axis=0
    )
    acc[...] = jnp.zeros_like(acc)

    def back(s):
        p = jnp.exp(scores[s] - lse)
        ds = (p * (nt(v_all[s], do2) - delta)).astype(BF)
        acc[...] += tn(k_all[s], ds)
        dkv[s, :, 0:128] = nn(ds, q2[...]).astype(BF)
        dkv[s, :, 128:256] = nn(p.astype(BF), do2).astype(BF)

    def send_half(side, y, index):
        return pltpu.make_async_remote_copy(
            src_ref=dkv.at[pl.ds(side * 8 + y * 4, 4)],
            dst_ref=pkv.at[pl.ds(y * 4, 4)],
            send_sem=cs_s.at[index],
            recv_sem=cs_r.at[index],
            device_id={"ctx": partner},
            device_id_type=MESH,
        )

    def add_half(y, index):
        send_half(other, y, index).wait_recv()

        def step(j):
            at = core * 8 + y * 4 + j
            dkv[at] = (dkv[at].astype(F32) + pkv[y * 4 + j].astype(F32)).astype(BF)

        each(0, 4, step)

    def kv_near(d):
        return to_x(dkv.at[core * 8 + row_at * 4 + lax.rem(col_at + d, 4)], rkv.at[d], RKV, d, d)

    def kv_far(d):
        return pltpu.make_async_remote_copy(
            src_ref=dkv.at[core * 8 + row_far * 4 + lax.rem(col_at + d, 4)],
            dst_ref=rkv.at[4 + d],
            send_sem=ss.at[RKV, 4 + d],
            recv_sem=rs.at[RKV, 4 + d],
            device_id={"ctx": (row_far * 4 + lax.rem(col_at + d, 4)) * 2 + core},
            device_id_type=MESH,
        )

    each(0, 4, lambda j: back(other * 8 + row_far * 4 + j))
    send_half(other, row_far, 2).start()
    each(0, 4, lambda j: back(core * 8 + row_far * 4 + j))
    each(0, 4, lambda j: back(other * 8 + row_at * 4 + j))
    send_half(other, row_at, 21).start()
    add_half(row_far, 2)
    each(0, 4, lambda d: kv_far(d).start())
    up_end()
    tree_start(ou, AGU, FWU, up_tree_mid)
    each(0, 4, lambda j: back(core * 8 + row_at * 4 + j))
    add_half(row_at, 21)
    each(1, 4, lambda d: kv_near(d).start())

    def kv_sent():
        send_half(other, row_far, 2).wait_send()
        send_half(other, row_at, 21).wait_send()
        each(0, 4, lambda d: kv_far(d).wait_send())
        each(1, 4, lambda d: kv_near(d).wait_send())

    sends.append(kv_sent)

    def kv_end():
        each(1, 4, lambda d: kv_near(d).wait_recv())
        each(0, 4, lambda d: kv_far(d).wait_recv())
        whole = dkv[slot].astype(F32)
        for d in range(1, 8):
            whole = whole + rkv[d].astype(F32)
        return whole.astype(BF)

    dq = (diagonal(acc[...]) * 0.125).T.astype(BF)
    gb[:, 64:128, :] = tn(normed[...], dq).astype(BF).reshape(16, 64, 128)
    d_out = tn(attn_low[...], dh_low).astype(BF)
    for s in range(16):
        gb[s, 0:64, :] = d_out[64 * (s % 2) : 64 * (s % 2) + 64, 128 * (s // 2) : 128 * (s // 2) + 128]
    combine_start(gb, pb, 3)
    reduce_start(nn(act, wdn[...]), rs3s, rs3r, RS3)
    combined(gb, pb, 3)
    scatter_start(gb, rb, RB)
    down_mid()

    dkv_mine = kv_end()
    d_qkv = jnp.concatenate([dq, dkv_mine], axis=1)
    da = nt(d_qkv, wqkv[...])
    reduce_start(da, rs4s, rs4r, RS4)
    both = tn(normed[...], dkv_mine).astype(BF)
    gc[:, 0:64, :] = both[:, 0:128].reshape(16, 64, 128)
    gc[:, 64:128, :] = both[:, 128:256].reshape(16, 64, 128)
    combine_start(gc, pc, 4)
    combined(gc, pc, 4)
    scatter_start(gc, rc, RC)
    down_end()
    tree_start(od, AGW, FWW, down_tree_mid, down_tree_sent)
    up_tree_mid(ou, AGU, FWU)
    vec_row(4, rows_sum(da * xhat_all[...]))
    vec_row(5, rows_sum(da))
    for j in range(8):
        vs[j, 6:8, :] = jnp.zeros((2, 128), F32)
    each(1, 8, lambda d: to_wa(vs.at[lax.rem(wa + d, 8)], vr.at[d], RS5, d).start())
    sends.append(lambda: wa_sent(vs, RS5))
    cvs[12:13, :] = rows_sum(dq.astype(F32))
    cvs[13:14, :] = rows_sum(dkv_mine[:, 128:256].astype(F32))
    cvs[14:16, :] = jnp.zeros((2, 128), F32)
    ob[slot] = scatter_end(gb, rb, RB)
    spread_start(ob, AGB, FWB)

    hat_one, rstd_one = normalize(x_mine)
    d_first = reduce_end(rs4s, rs4r, RS4)
    g_all[wa] = (d_hidden + norm_back(d_first, ln1_gain, hat_one, rstd_one)).astype(BF)
    gather_start(g_all, AGG)

    each(1, 8, lambda d: to_wa(vs.at[lax.rem(wa + d, 8)], vr.at[d], RS5, d).wait_recv())
    vec_sum = vs[wa]
    for d in range(1, 8):
        vec_sum = vec_sum + vr[d]
    cvs[0:8, :] = vec_sum
    cvr[ctx] = cvs[...]

    def to_ctx(dst, d):
        return pltpu.make_async_remote_copy(
            src_ref=cvs,
            dst_ref=cvr.at[dst],
            send_sem=cs_s.at[5 + d],
            recv_sem=cs_r.at[5 + d],
            device_id={"ctx": lax.rem(ctx + d, 16)},
            device_id_type=MESH,
        )

    each(1, 16, lambda d: to_ctx(ctx, d).start())
    sends.append(lambda: each(1, 16, lambda d: to_ctx(ctx, d).wait_send()))
    oc[slot] = scatter_end(gc, rc, RC)
    spread_start(oc, AGCC, FWC)
    down_tree_mid(od, AGW, FWW)
    tree_pass(ou, AGU, FWU)
    y_all[wa] = (hidden + reduce_end(rs3s, rs3r, RS3) + b_down).astype(BF)
    gather_start(y_all, AGY)
    each(1, 16, lambda d: to_ctx(lax.rem(ctx + 16 - d, 16), d).wait_recv())
    ctx_sum = cvr[0]
    for i in range(1, 16):
        ctx_sum = ctx_sum + cvr[i]
    ctx_out[...] = ctx_sum[8:16, :]
    vall[wa] = ctx_sum[0:8, :]
    gather_start(vall, AGV)
    spread_pass(ob, AGB, FWB)
    tree_end(ou, AGU, FWU)
    ou_out[...] = ou[...].astype(F32).reshape(1024, 512)
    spread_pass(oc, AGCC, FWC)
    down_tree_pass(od, AGW, FWW)
    tree_end(od, AGW, FWW)
    od_out[:, 0:512] = od[:, 0:32, :].astype(F32).reshape(512, 512)
    od_out[:, 512:1024] = od[:, 32:64, :].astype(F32).reshape(512, 512)
    gather_end(g_all, AGG)
    gin_out[...] = g_all[...].reshape(128, 1024)
    spread_end(ob, AGB, FWB)
    ob_out[...] = ob[...]
    gather_end(y_all, AGY)
    y_out[...] = y_all[...].reshape(128, 1024)
    gather_end(vall, AGV)
    vec_out[...] = vall[...]
    spread_end(oc, AGCC, FWC)
    oc_out[...] = oc[...]

    for sent in sends:
        sent()


def finish(
    y_ref,
    gin_ref,
    ou_ref,
    od_ref,
    ob_ref,
    oc_ref,
    vec_ref,
    ctx_ref,
    y_out,
    gin_out,
    ln1g_out,
    ln1b_out,
    gqkv_out,
    bqv_out,
    gwo_out,
    bout_out,
    ln2g_out,
    ln2b_out,
    gup_out,
    bup_out,
    gdn_out,
    bdown_out,
    gin,
    gqkv,
    gwo,
    sems,
):
    copies = []

    def leave(src, dst):
        copies.append(pltpu.make_async_copy(src, dst, sems.at[len(copies)]))
        copies[-1].start()

    leave(y_ref, y_out)
    leave(ou_ref, gup_out)
    leave(od_ref, gdn_out)
    gin[...] = gin_ref[...].astype(F32)
    leave(gin, gin_out)
    for s in range(16):
        gwo[64 * (s % 2) : 64 * (s % 2) + 64, 128 * (s // 2) : 128 * (s // 2) + 128] = ob_ref[
            s, 0:64, :
        ].astype(F32)
    leave(gwo, gwo_out)
    gqkv[0] = ob_ref[:, 64:128, :].astype(F32).reshape(1024, 128)
    leave(gqkv.at[0], gqkv_out.at[0])
    gqkv[1] = oc_ref[:, 0:64, :].astype(F32).reshape(1024, 128)
    leave(gqkv.at[1], gqkv_out.at[1])
    gqkv[2] = oc_ref[:, 64:128, :].astype(F32).reshape(1024, 128)
    leave(gqkv.at[2], gqkv_out.at[2])
    for r, out in enumerate((ln2g_out, ln2b_out, bout_out, bdown_out, ln1g_out, ln1b_out)):
        out[...] = vec_ref[:, r, :]
    bup_out[...] = ctx_ref[0:4, :]
    bqv_out[...] = ctx_ref[4:6, :]
    for copy in copies:
        copy.wait()


def body(
    layer_input,
    block_order,
    seg_ids,
    cotangent,
    ln1_gain,
    ln1_bias,
    w_qkv,
    b_qv,
    w_out,
    b_out,
    ln2_gain,
    ln2_bias,
    w_up,
    b_up,
    w_down,
    b_down,
):
    vmem = pl.BlockSpec(memory_space=pltpu.VMEM)
    hbm = pl.BlockSpec(memory_space=pl.ANY)
    far = pl.BlockSpec(memory_space=pltpu.HBM)

    def stay(operand):
        return pltpu.with_memory_space_constraint(operand, pltpu.HBM)

    def bf(*shape):
        return pltpu.VMEM(shape, BF)

    def f32(*shape):
        return pltpu.VMEM(shape, F32)

    outs = pl.pallas_call(
        layer,
        out_shape=(
            jax.ShapeDtypeStruct((128, 1024), BF),
            jax.ShapeDtypeStruct((128, 1024), BF),
            jax.ShapeDtypeStruct((1024, 512), F32),
            jax.ShapeDtypeStruct((512, 1024), F32),
            jax.ShapeDtypeStruct((16, 128, 128), BF),
            jax.ShapeDtypeStruct((16, 128, 128), BF),
            jax.ShapeDtypeStruct((8, 8, 128), F32),
            jax.ShapeDtypeStruct((8, 128), F32),
        ),
        in_specs=[far] * 16,
        out_specs=(vmem,) * 8,
        scratch_shapes=[
            pltpu.SMEM((32,), jnp.int32),
            pltpu.VMEM((16, 128), jnp.int32),
            bf(128, 1024),
            bf(128, 1024),
            bf(8, 128),
            bf(8, 128),
            bf(8, 128),
            bf(8, 128),
            bf(8, 128),
            bf(8, 128),
            bf(4, 128),
            bf(2, 128),
            bf(1024, 384),
            bf(128, 1024),
            bf(1024, 512),
            bf(512, 1024),
            pltpu.SemaphoreType.DMA((18,)),
            f32(128, 1024),
            bf(128, 1024),
            bf(16, 128, 128),
            bf(16, 128, 128),
            bf(256, 128),
            f32(16, 128, 256),
            f32(128, 256),
            f32(128, 128),
            bf(128, 128),
            bf(8, 16, 1024),
            bf(8, 16, 1024),
            bf(8, 16, 1024),
            f32(128, 512),
            bf(8, 16, 1024),
            bf(8, 16, 1024),
            bf(8, 16, 1024),
            bf(8, 16, 1024),
            bf(8, 16, 1024),
            bf(8, 16, 1024),
            bf(16, 128, 256),
            bf(8, 128, 256),
            bf(8, 128, 256),
            bf(2, 2, 4, 64, 512),
            bf(2, 4, 64, 512),
            bf(4, 2, 64, 512),
            bf(2, 64, 512),
            bf(64, 512),
            bf(16, 64, 512),
            bf(2, 2, 4, 64, 512),
            bf(2, 4, 64, 512),
            bf(4, 64, 512),
            bf(4, 64, 512),
            bf(4, 64, 512),
            bf(16, 64, 512),
            bf(16, 128, 128),
            bf(8, 128, 128),
            bf(8, 128, 128),
            bf(16, 128, 128),
            bf(16, 128, 128),
            bf(8, 128, 128),
            bf(8, 128, 128),
            bf(16, 128, 128),
            bf(8, 16, 1024),
            bf(8, 16, 1024),
            bf(8, 16, 1024),
            f32(8, 8, 128),
            f32(8, 8, 128),
            f32(8, 8, 128),
            f32(16, 128),
            f32(16, 16, 128),
            pltpu.SemaphoreType.DMA((NSEM, 8)),
            pltpu.SemaphoreType.DMA((NSEM, 8)),
            pltpu.SemaphoreType.DMA((22,)),
            pltpu.SemaphoreType.DMA((22,)),
        ],
        compiler_params=pltpu.CompilerParams(
            collective_id=0, has_side_effects=True, vmem_limit_bytes=32 << 20
        ),
        name="decoder",
    )(
        stay(block_order),
        stay(seg_ids.reshape(16, 128)),
        stay(layer_input),
        stay(cotangent),
        *(
            stay(v.reshape(-1, 128))
            for v in (ln1_gain, ln1_bias, b_out, ln2_gain, ln2_bias, b_down, b_up)
        ),
        stay(b_qv),
        stay(w_qkv.transpose(1, 0, 2)),
        stay(w_out),
        stay(w_up),
        stay(w_down),
    )
    shapes = (
        ((128, 1024), BF),
        ((128, 1024), F32),
        ((8, 128), F32),
        ((8, 128), F32),
        ((3, 1024, 128), F32),
        ((2, 128), F32),
        ((128, 1024), F32),
        ((8, 128), F32),
        ((8, 128), F32),
        ((8, 128), F32),
        ((1024, 512), F32),
        ((4, 128), F32),
        ((512, 1024), F32),
        ((8, 128), F32),
    )
    large = (0, 1, 4, 6, 10, 12)
    done = list(
        pl.pallas_call(
            finish,
            out_shape=tuple(jax.ShapeDtypeStruct(*shape) for shape in shapes),
            in_specs=[vmem] * 8,
            out_specs=tuple(hbm if i in large else vmem for i in range(14)),
            scratch_shapes=[
                f32(128, 1024),
                f32(3, 1024, 128),
                f32(128, 1024),
                pltpu.SemaphoreType.DMA((14,)),
            ],
            compiler_params=pltpu.CompilerParams(vmem_limit_bytes=24 << 20),
            name="finish",
        )(*outs)
    )
    for i in (2, 3, 7, 8, 9, 11, 13):
        done[i] = done[i].reshape(-1)
    done[4] = done[4].transpose(1, 0, 2)
    return tuple(done)


def solution(mesh):
    placed = (
        P("ctx", None),
        P(),
        P(),
        P("ctx", None),
        P(),
        P(),
        P(None, None, "wa"),
        P(None, "wa"),
        P("wa", None),
        P(),
        P(),
        P(),
        P(None, "wa"),
        P("wa"),
        P("wa", None),
        P(),
    )
    return jax.shard_map(
        body,
        mesh=mesh,
        in_specs=placed,
        out_specs=(
            P("ctx", None),
            P("ctx", None),
            P(),
            P(),
            P(None, None, "wa"),
            P(None, "wa"),
            P("wa", None),
            P(),
            P(),
            P(),
            P(None, "wa"),
            P("wa"),
            P("wa", None),
            P(),
        ),
        check_vma=False,
    )
```
